256 devices in a mesh: region: 32 (over z, x), cell: 8 (over y, core).
Axes of the slice: x: 4, y: 4, z: 8, core: 2. Of those that a mesh axis runs over, the one named last changes fastest.
Arguments:
- points: float32 [3, 2097152], P(None, ('region', 'cell')), may hold values from -1951 to 1951
- cell_counts: int32 [8192], P(('region', 'cell')), may hold values from 192 to 256
- pair_cells: int32 [2, 106496], P(None, ('region', 'cell')), may hold values from 0 to 31, as said below
- pair_counts: int32 [256], P(('region', 'cell')), may hold values from 32 to 416, as said below
- nugget: float32 [2097152], P(('region', 'cell')), may hold values from 0.1 to 1
- solution: float32 [16, 2097152], P(None, ('region', 'cell')), may hold values from -6 to 6
- residual: float32 [16, 2097152], P(None, ('region', 'cell')), may hold values from -12 to 12
- direction: float32 [16, 2097152], P(None, ('region', 'cell')), may hold values from -12 to 12
- ritz_basis: float32 [32, 2097152], P(None, ('region', 'cell')), may hold values from -1.5 to 1.5
- ritz_image: float32 [32, 2097152], P(None, ('region', 'cell')), may hold values from -0.00390625 to 0.00390625
- inverse_gram: float32 [32, 32], replicated, may hold values from -1 to 1
Outputs:
- solution_out: float32 [16, 2097152], P(None, ('region', 'cell'))
- residual_out: float32 [16, 2097152], P(None, ('region', 'cell'))
- direction_out: float32 [16, 2097152], P(None, ('region', 'cell'))
The draws below stay inside these ranges and needn't reach their ends.
Inputs may be any that keep to these rules, and one draw needn't show every extreme that they name: `pair_cells`: for each device, column s of its 416 columns is used if s < pair_counts of that device; used columns come first and unused ones hold (0, 0). Row 0 is a cell of that device (0 to 31), row 1 the distance in the cell order to the pair's second cell, 0 to 12; the second cell exists. Each cell is paired with itself exactly once and with the cells that directly follow it up to its last partner, at most 12 of them; used pairs are distinct. Points of two cells that are not paired are more than distance 1 apart. `pair_counts`: some device uses all 416 slots.
All inputs are finite; a program needn't handle non-finite values.
Results may differ from the reference program's by a relative error of at most 0.0025.
Values sent between devices are 32-bit elements; how exact they have to be, the bound alone decides.
No kernel may reach another device: no remote copies, remote signals or barrier semaphores. Data moves between devices by JAX's collectives and lax.ppermute only.
A program may use at most 64 MiB of HBM per device.

```python
import math
import jax
import jax.numpy as jnp
from jax import lax

CELLS_DEV = 32
PTS = 256
RHS = 16
RITZ = 32
KMAX = 12
REACH = 12
PAIRS_DEV = 416
CELLS = 8192
POINTS = 2097152
N_REGION = 32
N_CELL = 8


def layout(key):
    key = jax.random.fold_in(key, 7)
    devices = N_REGION * N_CELL
    blocks = devices // 2
    level_table = jnp.array([2, 6, 8, 12], dtype=jnp.int32)
    shuffled = jax.random.permutation(key, blocks).astype(jnp.int32) % 4
    block_gap = jnp.take(level_table, shuffled)
    cell_gap = jnp.repeat(block_gap, 2 * CELLS_DEV)
    cell_total = devices * CELLS_DEV
    at_start = jnp.arange(cell_total, dtype=jnp.int32) % CELLS_DEV == 0
    cell_gap = jnp.where(at_start, 2, cell_gap)
    return jnp.cumsum(cell_gap).astype(jnp.int32)


def pair_tables(key):
    position = layout(key)
    devices = N_REGION * N_CELL
    cell_total = devices * CELLS_DEV
    offsets = jnp.arange(1, KMAX + 1, dtype=jnp.int32)
    later = jnp.arange(cell_total, dtype=jnp.int32)[:, None] + offsets[None, :]
    later_safe = jnp.minimum(later, cell_total - 1)
    distance_units = jnp.take(position, later_safe) - position[:, None]
    linked = (later < cell_total) & (distance_units <= 2 * KMAX)
    flat_used = jnp.concatenate([jnp.ones((cell_total, 1), jnp.int32), linked.astype(jnp.int32)], axis=1)
    flat_used = flat_used.reshape(devices, PAIRS_DEV)
    offset_row = jnp.concatenate([jnp.zeros((1,), jnp.int32), offsets])
    flat_offset = jnp.broadcast_to(offset_row[None, :], (cell_total, KMAX + 1)).reshape(devices, PAIRS_DEV)
    flat_first = jnp.broadcast_to(jnp.arange(CELLS_DEV, dtype=jnp.int32)[:, None], (CELLS_DEV, KMAX + 1)).reshape(PAIRS_DEV)
    flat_first = jnp.broadcast_to(flat_first[None, :], (devices, PAIRS_DEV))
    sort_keys = (1 - flat_used) * PAIRS_DEV + jnp.arange(PAIRS_DEV, dtype=jnp.int32)[None, :]
    arrange = jnp.argsort(sort_keys, axis=1)
    sorted_used = jnp.take_along_axis(flat_used, arrange, axis=1)
    first_out = jnp.take_along_axis(flat_first, arrange, axis=1) * sorted_used
    offset_out = jnp.take_along_axis(flat_offset, arrange, axis=1) * sorted_used
    pair_table = jnp.stack([first_out.reshape(-1), offset_out.reshape(-1)]).astype(jnp.int32)
    return (pair_table, jnp.sum(flat_used, axis=1).astype(jnp.int32))


def draw_pair_cells(key, part):
    return pair_tables(key)[0]


def draw_pair_counts(key, part):
    return pair_tables(key)[1]


def draw_points(key, part):
    position = layout(key)
    key = jax.random.fold_in(key, 3)
    key_side, key_jitter = jax.random.split(key, 2)
    cell_total = N_REGION * N_CELL * CELLS_DEV
    unit_length = 1.7 / (2 * KMAX + 1)
    middle = 7 * cell_total // 2
    along = (position - middle).astype(jnp.float32) * unit_length
    side = jax.random.uniform(key_side, (2, cell_total), jnp.float32, -0.25, 0.25)
    jitter = jax.random.uniform(key_jitter, (3, cell_total, PTS), jnp.float32, -0.3, 0.3)
    centres = jnp.concatenate([along[None, :], side], axis=0)
    return (centres[:, :, None] + jitter).reshape(3, cell_total * PTS)


def field_draw(key, salt_value):
    key = jax.random.fold_in(key, salt_value)
    key_base, key_common, key_spread = jax.random.split(key, 3)
    cell_total = N_REGION * N_CELL * CELLS_DEV
    random_part = jax.random.normal(key_base, (RHS, cell_total, PTS), jnp.float32)
    common = 0.1 * jax.random.normal(key_common, (RHS, cell_total, 1), jnp.float32)
    spread = jnp.exp(jax.random.uniform(key_spread, (cell_total,), jnp.float32, math.log(0.5), math.log(2.0)))
    rising = jnp.sqrt(1.0 + 2.0 * jnp.arange(cell_total, dtype=jnp.float32) / cell_total)
    value = rising[None, :, None] * spread[None, :, None] * (random_part + common)
    return jnp.clip(value, -12.0, 12.0).reshape(RHS, cell_total * PTS)


def draw_residual(key, part):
    return field_draw(key, 21)


def draw_direction(key, part):
    return field_draw(key, 22)


def with_ends(values, rng, low, top_value):
    longest = values.shape.index(max(values.shape))
    spots = []
    for shift in (0, 1):
        where = [jax.random.randint(jax.random.fold_in(rng, axis), (), 0, length) for axis, length in enumerate(values.shape)]
        where[longest] = (where[longest] + shift) % values.shape[longest]
        spots.append(tuple(where))
    return values.at[spots[0]].set(low).at[spots[1]].set(top_value)


def level_of(own_key, extent, cuts, smallest, high):
    factor_of, own = 1.0, jax.random.fold_in(own_key, 6)
    for dim, parts in cuts:
        draws = jnp.exp(jax.random.uniform(jax.random.fold_in(own, dim), (parts,), jnp.float32, smallest / len(cuts), high / len(cuts)))
        factor_of = factor_of * jnp.repeat(draws, extent[dim] // parts).reshape([-1 if axis == dim else 1 for axis in range(len(extent))])
    return factor_of


def bell_draw(key, extent, scale, reach, cuts=(), kind=jnp.bfloat16):
    values = scale * jax.random.normal(key, extent, jnp.float32)
    if cuts:
        values = values * level_of(key, extent, cuts, -0.22, 0.18)
    return jnp.clip(values, -reach, reach).astype(kind)


def setup_inputs(seed: int = 0) -> dict:
    key_list = jax.random.split(jax.random.key(seed), 12)
    points = draw_points(jax.random.fold_in(key_list[11], 71), 0)
    cell_counts = with_ends(jax.random.randint(key_list[1], (CELLS,), PTS * 3 // 4, PTS + 1), jax.random.fold_in(key_list[1], 1), PTS * 3 // 4, PTS).astype(jnp.int32)
    pair_cells = draw_pair_cells(jax.random.fold_in(key_list[11], 71), 0)
    pair_counts = draw_pair_counts(jax.random.fold_in(key_list[11], 71), 0)
    nugget = jnp.clip(jnp.exp(math.log(1.0) - 2.3025851 * jax.random.uniform(key_list[4], (POINTS,), jnp.float32) ** level_of(key_list[4], (POINTS,), ((0, 256),), -0.2, 0.2)), 0.1, 1.0)
    solution = bell_draw(key_list[5], (RHS, POINTS), 1.0, 6.0, ((1, 256),), jnp.float32)
    residual = draw_residual(jax.random.fold_in(key_list[11], 71), 0)
    direction = draw_direction(jax.random.fold_in(key_list[11], 71), 0)
    ritz_basis = bell_draw(key_list[8], (RITZ, POINTS), 0.25, 1.5, ((1, 256),), jnp.float32)
    ritz_image = bell_draw(key_list[9], (RITZ, POINTS), POINTS ** -0.5, 0.00390625, ((1, 256),), jnp.float32)
    inverse_gram = bell_draw(key_list[10], (RITZ, RITZ), RITZ ** -0.5, 1.0, (), jnp.float32)
    return dict(points=points, cell_counts=cell_counts, pair_cells=pair_cells, pair_counts=pair_counts, nugget=nugget, solution=solution, residual=residual, direction=direction, ritz_basis=ritz_basis, ritz_image=ritz_image, inverse_gram=inverse_gram)


def wendland(distance):
    inner = jnp.maximum(1.0 - distance, 0.0)
    square = inner * inner
    return square * square * (4.0 * distance + 1.0)

def pair_terms(coords_ext, dirs_ext, first_cell, second_cell, in_use):
    coords_first = jnp.take(coords_ext, first_cell, axis=1)
    coords_second = jnp.take(coords_ext, second_cell, axis=1)
    gap_vec = coords_first[:, :, :, None] - coords_second[:, :, None, :]
    distance = jnp.sqrt(lax.optimization_barrier(jnp.sum(gap_vec * gap_vec, axis=0)))
    kernel_tile = (wendland(distance) * in_use[:, None, None]).astype(jnp.bfloat16)
    tile_wide = kernel_tile.astype(jnp.float32)
    dir_first = jnp.take(dirs_ext, first_cell, axis=1).astype(jnp.float32)
    dir_second = jnp.take(dirs_ext, second_cell, axis=1).astype(jnp.float32)
    to_first = jnp.einsum('bij,kbj->kbi', tile_wide, dir_second)
    to_second = jnp.einsum('bij,kbi->kbj', tile_wide, dir_first)
    apart = (first_cell != second_cell).astype(jnp.float32)
    return (to_first, to_second * apart[None, :, None])

def pair_products(coords_ext, dirs_ext, first_cell, second_cell, used_count):
    per_turn = 16
    total_slots = first_cell.shape[0]
    padded = -(-total_slots // per_turn) * per_turn
    extra = jnp.zeros((padded - total_slots,), jnp.int32)
    first_all = jnp.concatenate([first_cell.astype(jnp.int32), extra])
    second_all = jnp.concatenate([second_cell.astype(jnp.int32), extra])
    totals_zero = jnp.zeros(dirs_ext.shape, jnp.float32)
    turn_count = ((used_count + per_turn - 1) // per_turn).astype(jnp.int32)

    def one_turn(turn, totals):
        begin_at = (turn * per_turn).astype(jnp.int32)
        first_now = lax.dynamic_slice_in_dim(first_all, begin_at, per_turn)
        second_now = lax.dynamic_slice_in_dim(second_all, begin_at, per_turn)
        in_use = (begin_at + jnp.arange(per_turn, dtype=jnp.int32) < used_count).astype(jnp.float32)
        to_first, to_second = pair_terms(coords_ext, dirs_ext, first_now, second_now, in_use)
        totals = totals.at[:, first_now].add(to_first)
        return totals.at[:, second_now].add(to_second)
    return lax.fori_loop(jnp.int32(0), turn_count, one_turn, totals_zero)

def reference(points, cell_counts, pair_cells, pair_counts, nugget, solution, residual, direction, ritz_basis, ritz_image, inverse_gram):
    devices = N_REGION * N_CELL
    cells = CELLS_DEV * devices
    hop_count = -(-REACH // CELLS_DEV)
    window_cells = CELLS_DEV * (1 + hop_count)
    in_cell = (jnp.arange(PTS, dtype=jnp.int32)[None, :] < cell_counts[:, None]).astype(jnp.float32)
    dir_live = direction.reshape(RHS, cells, PTS) * in_cell
    res_live = residual.reshape(RHS, cells, PTS) * in_cell
    sol_live = solution.reshape(RHS, cells, PTS) * in_cell
    dir_half = dir_live.astype(jnp.bfloat16)
    coords = points.reshape(3, cells, PTS)
    coords_pad = jnp.concatenate([coords, jnp.zeros((3, hop_count * CELLS_DEV, PTS), jnp.float32)], axis=1)
    dirs_pad = jnp.concatenate([dir_half, jnp.zeros((RHS, hop_count * CELLS_DEV, PTS), jnp.bfloat16)], axis=1)
    totals_zero = jnp.zeros((RHS, cells + hop_count * CELLS_DEV, PTS), jnp.float32)

    def per_device(device, totals):
        device = device.astype(jnp.int32)
        begin_at = device * CELLS_DEV
        coords_win = lax.dynamic_slice_in_dim(coords_pad, begin_at, window_cells, 1)
        dirs_win = lax.dynamic_slice_in_dim(dirs_pad, begin_at, window_cells, 1)
        pair_lists = lax.dynamic_slice_in_dim(pair_cells, device * PAIRS_DEV, PAIRS_DEV, 1)
        first_cell = pair_lists[0]
        second_cell = first_cell + pair_lists[1]
        local_terms = pair_products(coords_win, dirs_win, first_cell, second_cell, pair_counts[device])
        current = lax.dynamic_slice_in_dim(totals, begin_at, window_cells, 1)
        return lax.dynamic_update_slice_in_dim(totals, current + local_terms, begin_at, 1)
    totals = lax.fori_loop(0, devices, per_device, totals_zero)
    kernel_part = totals[:, :cells]
    image = in_cell * (nugget.reshape(cells, PTS)[None] * dir_live + kernel_part)
    curvature = lax.optimization_barrier(jnp.sum(dir_live * image, axis=(1, 2)))
    res_norm = lax.optimization_barrier(jnp.sum(res_live * res_live, axis=(1, 2)))
    step_len = res_norm / curvature
    solution_out = sol_live + step_len[:, None, None] * dir_live
    residual_out = res_live - step_len[:, None, None] * image
    new_norm = lax.optimization_barrier(jnp.sum(residual_out * residual_out, axis=(1, 2)))
    flat_res = residual_out.reshape(RHS, POINTS)
    projected = lax.dot_general(ritz_image, flat_res, (((1,), (1,)), ((), ())), precision=lax.Precision.HIGHEST)
    coefficients = jnp.dot(inverse_gram, projected, precision=lax.Precision.HIGHEST)
    correction = lax.dot_general(coefficients, ritz_basis, (((0,), (0,)), ((), ())), precision=lax.Precision.HIGHEST)
    growth = new_norm / res_norm
    direction_out = in_cell * (growth[:, None, None] * dir_live + residual_out - correction.reshape(RHS, cells, PTS))
    return (solution_out.reshape(RHS, POINTS), flat_res, direction_out.reshape(RHS, POINTS))
```

```python
import jax
import jax.numpy as jnp
from jax import lax
from jax.experimental import pallas as pl
from jax.experimental.pallas import tpu as pltpu
from jax.sharding import PartitionSpec as P

PTS = 256
REACH = 12
KF = 48
FAR = 1e18
ROOM = 16.0
AXES = ("region", "cell")
F32 = jnp.float32
BF16 = jnp.bfloat16


def mm(x, y):
    return lax.dot_general(x, y, (((1,), (0,)), ((), ())), preferred_element_type=F32)


def mm_t(x, y):
    return lax.dot_general(x, y, (((1,), (1,)), ((), ())), preferred_element_type=F32)


def high(x):
    return x.astype(BF16).astype(F32)


def split3(x):
    h = high(x)
    m = high(x - h)
    return h, m, high(x - h - m)


def tile_of(scaled_square):
    s = jnp.maximum(scaled_square, 1e-30)
    t = s * lax.rsqrt(s)
    u = jnp.maximum(4.0 - t, 0.0)
    u2 = u * u
    return ((u2 * u2) * (t + 1.0)).astype(BF16)


def cols(block, size=PTS):
    return pl.ds(pl.multiple_of(block * size, size), size)


def with_norm(vec):
    row = lax.broadcasted_iota(jnp.int32, vec.shape, 0)
    return row, jnp.sum(vec * vec, axis=0, keepdims=True)


def weights_side(p):
    row, norm = with_norm(p)
    a = jnp.where(row == 3, norm, -2.0 * p)
    h, m, l = split3(a)
    one_h = jnp.where(row == 3, 1.0, h)
    one_m = jnp.where(row == 3, 1.0, m)
    return jnp.concatenate([h, m, one_h, one_m, l, one_h], axis=0).astype(BF16)


def rows_side(q):
    row, norm = with_norm(q)
    a = jnp.where(row == 3, norm, q)
    h, m, l = split3(a)
    one = jnp.where(row == 3, 1.0, h)
    mid_h = jnp.where(row == 3, h, m)
    return jnp.concatenate([one, one, mid_h, m, one, l], axis=0), norm


def pair_kernel(
    cells,
    halo_cells,
    cnt,
    hcnt,
    pts,
    dirs,
    hdirs,
    hpts,
    own,
    halo,
    off,
    dc,
    pc,
    db,
    fs,
    cen,
    acc_i,
    acc_j,
    f0,
    f1,
    s0,
    s1,
    w0,
    w1,
    tab_v,
    tab_s,
    sem,
):
    blocks = cells + halo_cells
    spare = blocks
    lane1 = lax.broadcasted_iota(jnp.int32, (1, PTS), 1)
    lane128 = lax.broadcasted_iota(jnp.int32, (1, 128), 1)
    dc[...] = jnp.zeros_like(dc)
    pc[...] = jnp.zeros_like(pc)
    acc_i[...] = jnp.zeros_like(acc_i)
    acc_j[...] = jnp.zeros_like(acc_j)

    def place(c, at, count, dref, pref):
        shift = at % 128
        base = pl.multiple_of((at // 128) * 128, 128)
        live = lane1 < count
        dv = jnp.where(live, dref[:, cols(c)], 0.0)
        pv = jnp.where(live, pref[:, cols(c)], 0.0)
        for ref, val in ((dc, dv), (pc, pv)):
            rows = val.shape[0]
            wide = jnp.concatenate([val, jnp.zeros((rows, 128), F32)], axis=1)
            wide = pltpu.roll(wide, shift, 1)
            old = ref[:rows, pl.ds(base, 128)]
            ref[:rows, pl.ds(base, 128)] = jnp.where(lane128 < shift, old, wide[:, :128])
            ref[:rows, pl.ds(base + 128, 256)] = wide[:, 128:]
        return at + count

    def place_own(c, at):
        off[c] = at
        return place(c, at, cnt[c], dirs, pts)

    own_end = lax.fori_loop(0, cells, place_own, jnp.int32(0))
    strips = (own_end + (PTS - 1)) // PTS
    halo_at = strips * PTS

    def place_halo(c, at):
        off[cells + c] = at
        return place(c, at, hcnt[c], hdirs, hpts)

    halo_end = lax.fori_loop(0, halo_cells, place_halo, halo_at)
    db[...] = dc[...].astype(BF16)

    def prepare(j, carry):
        low, top, far = carry
        here = pc[:, cols(j)]
        at = j * PTS + lane1
        valid = (at < own_end) | ((at >= halo_at) & (at < halo_end))
        lo = jnp.min(jnp.where(valid, here, FAR), axis=1, keepdims=True)
        hi = jnp.max(jnp.where(valid, here, -FAR), axis=1, keepdims=True)
        centre = jnp.where(lo <= hi, 0.5 * (lo + hi), 0.0)
        cen[pl.ds(pl.multiple_of(j * 8, 8), 8), :] = jnp.broadcast_to(centre, (8, 128))
        feats, norm = rows_side(4.0 * (here - centre))
        fs[cols(j), :] = feats.T.astype(BF16)
        low = jnp.where(lane128 == j, lo, low)
        top = jnp.where(lane128 == j, hi, top)
        return low, top, jnp.maximum(far, jnp.where(valid, norm, 0.0))

    start = (
        jnp.full((8, 128), FAR, F32),
        jnp.full((8, 128), -FAR, F32),
        jnp.zeros((1, PTS), F32),
    )
    low, top, far = lax.fori_loop(0, blocks, prepare, start)
    cen[pl.ds(blocks * 8, 8), :] = jnp.zeros((8, 128), F32)
    fs[pl.ds(blocks * PTS, PTS), :] = jnp.zeros((PTS, KF), BF16)
    square = lambda v: jnp.concatenate([v, jnp.zeros((120, 128), F32)], axis=0).T
    low_t, top_t = square(low), square(top)
    gap2 = jnp.zeros((128, 128), F32)
    for k in range(3):
        gap = jnp.maximum(low[k : k + 1] - top_t[:, k : k + 1], low_t[:, k : k + 1] - top[k : k + 1])
        gap = jnp.maximum(gap, 0.0)
        gap2 = gap2 + gap * gap
    ri = lax.broadcasted_iota(jnp.int32, (128, 128), 0)
    rj = lax.broadcasted_iota(jnp.int32, (128, 128), 1)
    need = (gap2 <= 1.001) & (rj > ri)
    stop = jnp.max(jnp.where(need, rj + 1, ri + 1).astype(F32), axis=1, keepdims=True)
    stop = jnp.broadcast_to(stop, (128, 128)).T[:8].astype(jnp.int32)
    radius = jnp.max(far, axis=1, keepdims=True)
    spread = jnp.where(radius > 16.0 * ROOM, 1, 0)
    tab_v[...] = jnp.where(lane128 == 127, spread, stop)
    copy = pltpu.make_async_copy(tab_v, tab_s, sem)
    copy.start()
    copy.wait()

    def following(i, j):
        n = j + 1
        over = n >= tab_s[0, i]
        up = jnp.where(i + 1 >= strips, spare, i + 1)
        return jnp.where(over, up, i), jnp.where(over, up, n)

    def stage0(i, j, f):
        c = cen[pl.ds(pl.multiple_of(j * 8, 8), 8), :]
        f[...] = weights_side(4.0 * (pc[:, cols(i)] - jnp.concatenate([c, c], axis=1)))

    def stage1(j, f, s):
        s[...] = mm(fs[cols(j), :], f[...])

    def stage2(s, w):
        w[...] = tile_of(s[...])

    def stage3(i, j, w):
        tile = w[...]
        acc_i[:, cols(i)] += mm(db[:, cols(j)], tile)
        keep = jnp.where(j > i, 1.0, 0.0)
        acc_j[:, cols(j)] += mm_t(db[:, cols(i)], tile) * keep

    zero = jnp.int32(0)
    last = jnp.int32(spare)
    total = lax.fori_loop(0, strips, lambda i, n: n + tab_s[0, i] - i, zero)

    @pl.when(tab_s[0, 127] == 0)
    def _():
        w1[...] = jnp.zeros_like(w1)
        ib, jb = following(zero, zero)
        stage0(zero, zero, f0)
        stage1(zero, f0, s0)
        stage0(ib, jb, f1)

        def two(_, carry):
            ia, ja, i0, j0, i1, j1 = carry
            i2, j2 = following(i1, j1)
            stage0(i2, j2, f0)
            stage1(j1, f1, s1)
            stage2(s0, w0)
            stage3(ia, ja, w1)
            i3, j3 = following(i2, j2)
            stage0(i3, j3, f1)
            stage1(j2, f0, s0)
            stage2(s1, w1)
            stage3(i0, j0, w0)
            return i1, j1, i2, j2, i3, j3

        lax.fori_loop(0, total // 2 + 1, two, (last, last, zero, zero, ib, jb))

    @pl.when(tab_s[0, 127] != 0)
    def _():
        def one(_, carry):
            i, j = carry
            pj = pc[:, cols(j)].T
            pi = pc[:, cols(i)]
            for h in range(0, PTS, 64):
                s = jnp.zeros((64, PTS), F32)
                for k in range(3):
                    d = 4.0 * (pj[h : h + 64, k : k + 1] - pi[k : k + 1, :])
                    s = s + d * d
                w0[pl.ds(h, 64), :] = tile_of(s)
            stage3(i, j, w0)
            return following(i, j)

        lax.fori_loop(0, total, one, (zero, zero))

    def take(c, count, ref, k):
        at = off[k]
        base = pl.multiple_of((at // 128) * 128, 128)
        both = acc_i[:, pl.ds(base, 384)] + acc_j[:, pl.ds(base, 384)]
        back = pltpu.roll(both, 384 - at % 128, 1)[:, :PTS] * (1.0 / 256.0)
        ref[:, cols(c)] = jnp.where(lane1 < count, back, 0.0)

    def take_own(c, _):
        take(c, cnt[c], own, c)
        return 0

    def take_halo(c, _):
        take(c, hcnt[c], halo, cells + c)
        return 0

    lax.fori_loop(0, cells, take_own, 0)
    lax.fori_loop(0, halo_cells, take_halo, 0)


VM = pl.BlockSpec(memory_space=pltpu.VMEM)
SM = pl.BlockSpec(memory_space=pltpu.SMEM)
BIG = pltpu.CompilerParams(vmem_limit_bytes=56 << 20)


def pair_products(counts, halo_counts, points, direction, halo_dirs, halo_points):
    cells, halo_cells = counts.shape[0], halo_counts.shape[0]
    rhs = direction.shape[0]
    blocks = cells + halo_cells + 1
    wide = blocks * PTS + 256

    def kernel(*refs):
        pair_kernel(cells, halo_cells, *refs)

    return pl.pallas_call(
        kernel,
        name="pairs",
        out_shape=[
            jax.ShapeDtypeStruct((rhs, cells * PTS), F32),
            jax.ShapeDtypeStruct((rhs, halo_cells * PTS), F32),
        ],
        in_specs=[SM, SM, VM, VM, VM, VM],
        out_specs=[VM, VM],
        scratch_shapes=[
            pltpu.SMEM((cells + halo_cells,), jnp.int32),
            pltpu.VMEM((rhs, wide), F32),
            pltpu.VMEM((8, wide), F32),
            pltpu.VMEM((rhs, wide), BF16),
            pltpu.VMEM((blocks * PTS, KF), BF16),
            pltpu.VMEM((blocks * 8, 128), F32),
            pltpu.VMEM((rhs, wide), F32),
            pltpu.VMEM((rhs, wide), F32),
            pltpu.VMEM((KF, PTS), BF16),
            pltpu.VMEM((KF, PTS), BF16),
            pltpu.VMEM((PTS, PTS), F32),
            pltpu.VMEM((PTS, PTS), F32),
            pltpu.VMEM((PTS, PTS), BF16),
            pltpu.VMEM((PTS, PTS), BF16),
            pltpu.VMEM((8, 128), jnp.int32),
            pltpu.SMEM((8, 128), jnp.int32),
            pltpu.SemaphoreType.DMA,
        ],
        compiler_params=BIG,
    )(counts, halo_counts, points, direction, halo_dirs, halo_points)


def sums_kernel(cnt, own, back, nug, dirs, res, ritz, image, sums):
    cells = own.shape[1] // PTS
    halo_cells = back.shape[1] // PTS
    lane1 = lax.broadcasted_iota(jnp.int32, (1, PTS), 1)

    def of_cell(c, part, extra):
        live = lane1 < cnt[c]
        d = jnp.where(live, dirs[:, cols(c)], 0.0)
        r = jnp.where(live, res[:, cols(c)], 0.0)
        k = own[:, cols(c)]
        if extra:
            k = k + back[:, cols(c)]
        im = jnp.where(live, nug[:, cols(c)] * d + k, 0.0)
        image[:, cols(c)] = im
        dk, rr, ri, ii, prod = part
        both = jnp.concatenate([r, im], axis=0)
        bh = high(both)
        z = ritz[:, cols(c)]
        zh = high(z)
        left = jnp.concatenate([bh, both - bh], axis=0).astype(BF16)
        right = jnp.concatenate([zh, z - zh], axis=0).astype(BF16)
        return dk + d * im, rr + r * r, ri + r * im, ii + im * im, prod + mm_t(left, right)

    rhs = own.shape[0]
    zero = jnp.zeros((rhs, PTS), F32)
    part = (zero, zero, zero, zero, jnp.zeros((4 * rhs, 2 * ritz.shape[0]), F32))
    part = lax.fori_loop(0, halo_cells, lambda c, p: of_cell(c, p, True), part)
    part = lax.fori_loop(halo_cells, cells, lambda c, p: of_cell(c, p, False), part)
    dots = [jnp.sum(p, axis=1, keepdims=True) for p in part[:4]]
    prod = part[4]
    n = ritz.shape[0]
    h = 2 * rhs
    prod = prod[:h, :n] + prod[:h, n:] + prod[h:, :n]
    sums[...] = jnp.zeros_like(sums)
    sums[:, :n] = prod[:rhs]
    sums[:, n : 2 * n] = prod[rhs:]
    for k in range(4):
        sums[:, 2 * n + k : 2 * n + k + 1] = dots[k]


def local_sums(counts, own, back, nugget, direction, residual, ritz_image):
    return pl.pallas_call(
        sums_kernel,
        name="sums",
        out_shape=[
            jax.ShapeDtypeStruct(own.shape, F32),
            jax.ShapeDtypeStruct((own.shape[0], 128), F32),
        ],
        in_specs=[SM] + [VM] * 6,
        out_specs=[VM, VM],
        compiler_params=BIG,
    )(counts, own, back, nugget, direction, residual, ritz_image)


def finish_kernel(cnt, sums, gram, image, dirs, res, sol, basis, sol_out, res_out, dir_out):
    cells = image.shape[1] // PTS
    n = gram.shape[0]
    lane1 = lax.broadcasted_iota(jnp.int32, (1, PTS), 1)
    curvature, rr, ri, ii = (sums[:, 2 * n + k : 2 * n + k + 1] for k in range(4))
    step = rr / curvature
    growth = (rr + step * (step * ii - 2.0 * ri)) / rr
    projected = sums[:, :n] - step * sums[:, n : 2 * n]
    coef = lax.dot_general(
        projected,
        gram[...],
        (((1,), (1,)), ((), ())),
        precision=lax.Precision.HIGHEST,
        preferred_element_type=F32,
    )
    ch = high(coef)
    left = jnp.concatenate([ch, ch, coef - ch], axis=1).astype(BF16)

    def of_cell(c, _):
        live = lane1 < cnt[c]
        d = jnp.where(live, dirs[:, cols(c)], 0.0)
        r = jnp.where(live, res[:, cols(c)], 0.0)
        s = jnp.where(live, sol[:, cols(c)], 0.0)
        b = basis[:, cols(c)]
        bh = high(b)
        right = jnp.concatenate([bh, b - bh, bh], axis=0).astype(BF16)
        new = r - step * image[:, cols(c)]
        sol_out[:, cols(c)] = s + step * d
        res_out[:, cols(c)] = new
        dir_out[:, cols(c)] = jnp.where(live, growth * d + new - mm(left, right), 0.0)
        return 0

    lax.fori_loop(0, cells, of_cell, 0)


def finish(counts, sums, gram, image, direction, residual, solution, basis):
    return pl.pallas_call(
        finish_kernel,
        name="finish",
        out_shape=[jax.ShapeDtypeStruct(image.shape, F32)] * 3,
        in_specs=[SM] + [VM] * 7,
        out_specs=[VM] * 3,
        compiler_params=BIG,
    )(counts, sums, gram, image, direction, residual, solution, basis)


def passed_along(array, by):
    length = lax.axis_size(AXES)
    pairs = [(i, i + by) for i in range(length) if 0 <= i + by < length]
    return lax.ppermute(array, AXES, pairs)


def summed(array):
    for axis in ("cell", "region"):
        copies = jnp.broadcast_to(array[None], (lax.axis_size(axis),) + array.shape)
        array = jnp.sum(lax.all_to_all(copies, axis, 0, 0), axis=0)
    return array


def local(
    points,
    cell_counts,
    pair_cells,
    pair_counts,
    nugget,
    solution,
    residual,
    direction,
    ritz_basis,
    ritz_image,
    inverse_gram,
):
    width = min(cell_counts.shape[0], REACH)
    halo_counts = passed_along(cell_counts[:width], -1)
    halo_dirs = passed_along(direction[:, : width * PTS], -1)
    halo_points = passed_along(points[:, : width * PTS], -1)
    own, beyond = pair_products(
        cell_counts, halo_counts, points, direction, halo_dirs, halo_points
    )
    back = passed_along(beyond, 1)
    image, sums = local_sums(
        cell_counts, own, back, nugget.reshape(1, -1), direction, residual, ritz_image
    )
    return tuple(
        finish(
            cell_counts,
            summed(sums),
            inverse_gram,
            image,
            direction,
            residual,
            solution,
            ritz_basis,
        )
    )


def solution(mesh):
    split = P(None, AXES)
    line = P(AXES)
    in_specs = (split, line, split, line, line, split, split, split, split, split, P())
    return jax.shard_map(
        local, mesh=mesh, in_specs=in_specs, out_specs=(split,) * 3, check_vma=False
    )
```

```python
import jax
import jax.numpy as jnp
from jax import lax
from jax.experimental import pallas as pl
from jax.experimental.pallas import tpu as pltpu
from jax.sharding import PartitionSpec as P

PTS = 256
REACH = 12
KF = 48
FAR = 1e18
ROOM = 16.0
AXES = ("region", "cell")
F32 = jnp.float32
BF16 = jnp.bfloat16


def mm(x, y):
    return lax.dot_general(x, y, (((1,), (0,)), ((), ())), preferred_element_type=F32)


def mm_t(x, y):
    return lax.dot_general(x, y, (((1,), (1,)), ((), ())), preferred_element_type=F32)


def high(x):
    return x.astype(BF16).astype(F32)


def split3(x):
    h = high(x)
    m = high(x - h)
    return h, m, high(x - h - m)


def tile_of(scaled_square):
    s = jnp.maximum(scaled_square, 1e-30)
    t = s * lax.rsqrt(s)
    u = jnp.maximum(4.0 - t, 0.0)
    u2 = u * u
    return ((u2 * u2) * (t + 1.0)).astype(BF16)


def cols(block, size=PTS):
    return pl.ds(pl.multiple_of(block * size, size), size)


def with_norm(vec):
    row = lax.broadcasted_iota(jnp.int32, vec.shape, 0)
    return row, jnp.sum(vec * vec, axis=0, keepdims=True)


def weights_side(p):
    row, norm = with_norm(p)
    a = jnp.where(row == 3, norm, -2.0 * p)
    h, m, l = split3(a)
    one_h = jnp.where(row == 3, 1.0, h)
    one_m = jnp.where(row == 3, 1.0, m)
    return jnp.concatenate([h, m, one_h, one_m, l, one_h], axis=0).astype(BF16)


def rows_side(q):
    row, norm = with_norm(q)
    a = jnp.where(row == 3, norm, q)
    h, m, l = split3(a)
    one = jnp.where(row == 3, 1.0, h)
    mid_h = jnp.where(row == 3, h, m)
    return jnp.concatenate([one, one, mid_h, m, one, l], axis=0), norm


def pack(cells, cnt, off, dirs, pts, dc, pc):
    lane1 = lax.broadcasted_iota(jnp.int32, (1, PTS), 1)
    lane128 = lax.broadcasted_iota(jnp.int32, (1, 128), 1)
    dc[...] = jnp.zeros_like(dc)
    pc[...] = jnp.zeros_like(pc)

    def place(c, at):
        off[c] = at
        shift = at % 128
        base = pl.multiple_of((at // 128) * 128, 128)
        live = lane1 < cnt[c]
        dv = jnp.where(live, dirs[:, cols(c)], 0.0)
        pv = jnp.where(live, pts[:, cols(c)], 0.0)
        for ref, val in ((dc, dv), (pc, pv)):
            rows = val.shape[0]
            wide = jnp.concatenate([val, jnp.zeros((rows, 128), F32)], axis=1)
            wide = pltpu.roll(wide, shift, 1)
            old = ref[:rows, pl.ds(base, 128)]
            ref[:rows, pl.ds(base, 128)] = jnp.where(lane128 < shift, old, wide[:, :128])
            ref[:rows, pl.ds(base + 128, 256)] = wide[:, 128:]
        return at + cnt[c]

    return lax.fori_loop(0, cells, place, jnp.int32(0), unroll=4)


def prepare(blocks, pc, end, cen, fs):
    lane1 = lax.broadcasted_iota(jnp.int32, (1, PTS), 1)
    lane128 = lax.broadcasted_iota(jnp.int32, (1, 128), 1)

    def one(j, carry):
        low, top, far = carry
        here = pc[:, cols(j)]
        valid = j * PTS + lane1 < end
        lo = jnp.min(jnp.where(valid, here, FAR), axis=1, keepdims=True)
        hi = jnp.max(jnp.where(valid, here, -FAR), axis=1, keepdims=True)
        centre = jnp.where(lo <= hi, 0.5 * (lo + hi), 0.0)
        cen[pl.ds(pl.multiple_of(j * 8, 8), 8), :] = jnp.broadcast_to(centre, (8, 128))
        feats, norm = rows_side(4.0 * (here - centre))
        fs[cols(j), :] = feats.T.astype(BF16)
        low = jnp.where(lane128 == j, lo, low)
        top = jnp.where(lane128 == j, hi, top)
        return low, top, jnp.maximum(far, jnp.where(valid, norm, 0.0))

    start = (
        jnp.full((8, 128), FAR, F32),
        jnp.full((8, 128), -FAR, F32),
        jnp.zeros((1, PTS), F32),
    )
    low, top, far = lax.fori_loop(0, blocks, one, start, unroll=4)
    cen[pl.ds(blocks * 8, 8), :] = jnp.zeros((8, 128), F32)
    fs[pl.ds(blocks * PTS, PTS), :] = jnp.zeros((PTS, KF), BF16)
    wide = jnp.max(far, axis=1, keepdims=True) > 16.0 * ROOM
    return low, top, jnp.where(wide, 1, 0)


def square(v):
    return jnp.concatenate([v, jnp.zeros((120, 128), F32)], axis=0).T


def near(low_i, top_i, low_j, top_j):
    low_t, top_t = square(low_i), square(top_i)
    gap2 = jnp.zeros((128, 128), F32)
    for k in range(3):
        gap = jnp.maximum(
            low_j[k : k + 1] - top_t[:, k : k + 1], low_t[:, k : k + 1] - top_j[k : k + 1]
        )
        gap = jnp.maximum(gap, 0.0)
        gap2 = gap2 + gap * gap
    return gap2 <= 1.001


def as_rows(last):
    last = jnp.max(last.astype(F32), axis=1, keepdims=True)
    return jnp.broadcast_to(last, (128, 128)).T[:8].astype(jnp.int32)


def to_scalars(values, tab_v, tab_s, sem):
    tab_v[...] = values
    copy = pltpu.make_async_copy(tab_v, tab_s, sem)
    copy.start()
    copy.wait()


def sweep(first, end, begin, stop, spare, spread, side_i, side_j, acc_i, acc_j, bufs):
    pc_i, db_i = side_i
    pc_j, db_j, fs_j, cen_j = side_j
    f0, f1, s0, s1, w0, w1 = bufs
    zero = jnp.int32(0)

    def enter(i):
        i = jnp.where(i >= end, spare[0], i)
        return i, jnp.where(i == spare[0], spare[1], begin(i))

    def following(i, j):
        n = j + 1
        over = (n >= stop(i)) | (i == spare[0])
        i2, j2 = enter(i + 1)
        return jnp.where(over, i2, i), jnp.where(over, j2, n)

    def stage0(i, j, f):
        c = cen_j[pl.ds(pl.multiple_of(j * 8, 8), 8), :]
        f[...] = weights_side(4.0 * (pc_i[:, cols(i)] - jnp.concatenate([c, c], axis=1)))

    def stage1(j, f, s):
        s[...] = mm(fs_j[cols(j), :], f[...])

    def stage2(s, w):
        w[...] = tile_of(s[...])

    same = acc_j is not None and db_i is db_j

    def stage3(i, j, w):
        tile = w[...]
        acc_i[:, cols(i)] += mm(db_j[:, cols(j)], tile)
        other = mm_t(db_i[:, cols(i)], tile)
        if same:
            other = other * jnp.where(j > i, 1.0, 0.0)
        acc_j[:, cols(j)] += other

    total = lax.fori_loop(first, end, lambda i, n: n + stop(i) - begin(i), zero)
    ia, ja = enter(jnp.int32(first))

    @pl.when(spread == 0)
    def _():
        w1[...] = jnp.zeros_like(w1)
        ib, jb = following(ia, ja)
        stage0(ia, ja, f0)
        stage1(ja, f0, s0)
        stage0(ib, jb, f1)

        def two(_, carry):
            iz, jz, i0, j0, i1, j1 = carry
            i2, j2 = following(i1, j1)
            stage0(i2, j2, f0)
            stage1(j1, f1, s1)
            stage2(s0, w0)
            stage3(iz, jz, w1)
            i3, j3 = following(i2, j2)
            stage0(i3, j3, f1)
            stage1(j2, f0, s0)
            stage2(s1, w1)
            stage3(i0, j0, w0)
            return i1, j1, i2, j2, i3, j3

        last = (jnp.int32(spare[0]), jnp.int32(spare[1]))
        lax.fori_loop(0, total // 2 + 1, two, last + (ia, ja, ib, jb))

    @pl.when(spread != 0)
    def _():
        def one(_, carry):
            i, j = carry
            pj = pc_j[:, cols(j)].T
            pi = pc_i[:, cols(i)]
            for h in range(0, PTS, 64):
                s = jnp.zeros((64, PTS), F32)
                for k in range(3):
                    d = 4.0 * (pj[h : h + 64, k : k + 1] - pi[k : k + 1, :])
                    s = s + d * d
                w0[pl.ds(h, 64), :] = tile_of(s)
            stage3(i, j, w0)
            return following(i, j)

        lax.fori_loop(0, total, one, (ia, ja))


def strips_of(cells, cnt):
    return (lax.fori_loop(0, cells, lambda c, n: n + cnt[c], jnp.int32(0)) + (PTS - 1)) // PTS


def early(strips):
    return (strips * EARLY) // 16


def head_kernel(cells, cnt, pts, dirs, db, pc, fs, cen, box, tab, acc_i, acc_j, off, dc, *rest):
    *bufs, tab_s, sem = rest
    acc_i[...] = jnp.zeros_like(acc_i)
    acc_j[...] = jnp.zeros_like(acc_j)
    own_end = pack(cells, cnt, off, dirs, pts, dc, pc)
    strips = (own_end + (PTS - 1)) // PTS
    db[...] = dc[...].astype(BF16)
    low, top, spread = prepare(cells, pc, own_end, cen, fs)
    box[0:8, :] = low
    box[8:16, :] = top
    ri = lax.broadcasted_iota(jnp.int32, (128, 128), 0)
    rj = lax.broadcasted_iota(jnp.int32, (128, 128), 1)
    need = near(low, top, low, top) & (rj > ri)
    stop = as_rows(jnp.where(need, rj + 1, ri + 1))
    lane128 = lax.broadcasted_iota(jnp.int32, (1, 128), 1)
    to_scalars(jnp.where(lane128 == 127, spread, stop), tab, tab_s, sem)
    side = (pc, db, fs, cen)
    sweep(
        0, early(strips), lambda i: i, lambda i: tab_s[0, i], (cells, cells), tab_s[0, 127],
        side[:2], side, acc_i, acc_j, bufs,
    )


def edge_kernel(cells, halo_cells, cnt, db, pc, box, tab, piece, halo, acc_i, hdb, hfs, hcen, tab_v, *rest):
    *bufs, tab_s, sem = rest
    strips = strips_of(cells, cnt)
    acc_i[...] = jnp.zeros_like(acc_i)
    halo[...] = jnp.zeros_like(halo)
    rhs = hdb.shape[0]
    hdb[:, : halo_cells * PTS] = piece[:rhs, :].astype(BF16)
    hdb[:, halo_cells * PTS :] = jnp.zeros((rhs, PTS), BF16)
    hpc = piece.at[rhs : rhs + 8]
    low, top, spread = prepare(halo_cells, hpc, halo_cells * PTS, hcen, hfs)
    ri = lax.broadcasted_iota(jnp.int32, (128, 128), 0)
    rj = lax.broadcasted_iota(jnp.int32, (128, 128), 1)
    need = near(box[0:8, :], box[8:16, :], low, top) & (rj < halo_cells) & (ri < cells)
    stop = as_rows(jnp.where(need, rj + 1, 0))
    lane128 = lax.broadcasted_iota(jnp.int32, (1, 128), 1)
    first = jnp.min(jnp.where(need, ri, 127).astype(F32), axis=(0, 1), keepdims=True)
    stop = jnp.where(lane128 == 126, first.astype(jnp.int32), stop)
    wide = jnp.where((tab[...] != 0) & (lane128 == 127), 1, 0)
    to_scalars(jnp.where(lane128 == 127, spread + wide, stop), tab_v, tab_s, sem)
    sweep(
        jnp.minimum(tab_s[0, 126], strips), strips, lambda i: jnp.int32(0),
        lambda i: jnp.maximum(tab_s[0, i], 1), (cells, halo_cells), tab_s[0, 127],
        (pc, db), (hpc, hdb, hfs, hcen), acc_i, halo, bufs,
    )
    halo[:, : halo_cells * PTS] = halo[:, : halo_cells * PTS] * (1.0 / 256.0)


def tail_kernel(cells, cnt, db, pc, fs, cen, tab, a1, a2, b1, own, off, acc_i, acc_j, *rest):
    bufs = rest
    lane1 = lax.broadcasted_iota(jnp.int32, (1, PTS), 1)
    acc_i[...] = a1[...] + a2[...]
    acc_j[...] = b1[...]

    def place(c, at):
        off[c] = at
        return at + cnt[c]

    end = lax.fori_loop(0, cells, place, jnp.int32(0))
    strips = (end + (PTS - 1)) // PTS
    side = (pc, db, fs, cen)
    sweep(
        early(strips), strips, lambda i: i, lambda i: tab[0, i], (cells, cells), tab[0, 127],
        side[:2], side, acc_i, acc_j, bufs,
    )

    def take(c, _):
        at = off[c]
        base = pl.multiple_of((at // 128) * 128, 128)
        both = acc_i[:, pl.ds(base, 384)] + acc_j[:, pl.ds(base, 384)]
        back = pltpu.roll(both, 384 - at % 128, 1)[:, :PTS] * (1.0 / 256.0)
        own[:, cols(c)] = jnp.where(lane1 < cnt[c], back, 0.0)
        return 0

    lax.fori_loop(0, cells, take, 0, unroll=4)


def piece_kernel(cells, cnt, pts, dirs, piece):
    rhs = dirs.shape[0]
    lane1 = lax.broadcasted_iota(jnp.int32, (1, PTS), 1)
    piece[rhs:, :] = jnp.zeros_like(piece[rhs:, :])
    for c in range(cells):
        at = slice(c * PTS, (c + 1) * PTS)
        live = lane1 < cnt[c]
        piece[:rhs, at] = jnp.where(live, dirs[:, at], 0.0)
        piece[rhs : rhs + 3, at] = jnp.where(live, pts[:, at], pts[:, c * PTS : c * PTS + 1])


VM = pl.BlockSpec(memory_space=pltpu.VMEM)
SM = pl.BlockSpec(memory_space=pltpu.SMEM)
EARLY = 4


def params(mib):
    return pltpu.CompilerParams(vmem_limit_bytes=mib << 20)


def buffers():
    return [
        pltpu.VMEM((KF, PTS), BF16),
        pltpu.VMEM((KF, PTS), BF16),
        pltpu.VMEM((PTS, PTS), F32),
        pltpu.VMEM((PTS, PTS), F32),
        pltpu.VMEM((PTS, PTS), BF16),
        pltpu.VMEM((PTS, PTS), BF16),
    ]


def cost(units):
    return pl.CostEstimate(flops=units * 60_000_000, bytes_accessed=4_000_000, transcendentals=units * 65536)


def pair_products(counts, points, direction):
    cells = counts.shape[0]
    rhs = direction.shape[0]
    width = min(cells, REACH)
    blocks = cells + 1
    wide = blocks * PTS + 256
    shape = jax.ShapeDtypeStruct

    piece = pl.pallas_call(
        lambda *refs: piece_kernel(width, *refs),
        name="piece",
        grid=(1,),
        out_shape=shape((rhs + 8, width * PTS), F32),
        in_specs=[
            SM,
            pl.BlockSpec((3, width * PTS), lambda i: (0, 0)),
            pl.BlockSpec((rhs, width * PTS), lambda i: (0, 0)),
        ],
        out_specs=pl.BlockSpec((rhs + 8, width * PTS), lambda i: (0, 0)),
        compiler_params=params(8),
    )(counts, points, direction)
    piece = passed_along(piece, -1)
    db, pc, fs, cen, box, tab, acc_i, acc_j = pl.pallas_call(
        lambda *refs: head_kernel(cells, *refs),
        name="head",
        out_shape=[
            shape((rhs, wide), BF16),
            shape((8, wide), F32),
            shape((blocks * PTS, KF), BF16),
            shape((blocks * 8, 128), F32),
            shape((16, 128), F32),
            shape((8, 128), jnp.int32),
            shape((rhs, wide), F32),
            shape((rhs, wide), F32),
        ],
        in_specs=[SM, VM, VM],
        out_specs=[VM] * 8,
        scratch_shapes=[pltpu.SMEM((cells,), jnp.int32), pltpu.VMEM((rhs, wide), F32)]
        + buffers()
        + [pltpu.SMEM((8, 128), jnp.int32), pltpu.SemaphoreType.DMA],
        compiler_params=params(12),
        cost_estimate=cost(100),
    )(counts, points, direction)
    halo, acc_e = pl.pallas_call(
        lambda *refs: edge_kernel(cells, width, *refs),
        name="edge",
        out_shape=[shape((rhs, (width + 1) * PTS), F32), shape((rhs, wide), F32)],
        in_specs=[SM] + [VM] * 5,
        out_specs=[VM] * 2,
        scratch_shapes=[
            pltpu.VMEM((rhs, (width + 1) * PTS), BF16),
            pltpu.VMEM(((width + 1) * PTS, KF), BF16),
            pltpu.VMEM(((width + 1) * 8, 128), F32),
            pltpu.VMEM((8, 128), jnp.int32),
        ]
        + buffers()
        + [pltpu.SMEM((8, 128), jnp.int32), pltpu.SemaphoreType.DMA],
        compiler_params=params(12),
        cost_estimate=cost(70),
    )(counts, db, pc, box, tab, piece)
    back = passed_along(halo, 1)
    own = pl.pallas_call(
        lambda *refs: tail_kernel(cells, *refs),
        name="tail",
        out_shape=shape((rhs, cells * PTS), F32),
        in_specs=[SM] + [VM] * 4 + [SM] + [VM] * 3,
        out_specs=VM,
        scratch_shapes=[
            pltpu.SMEM((cells,), jnp.int32),
            pltpu.VMEM((rhs, wide), F32),
            pltpu.VMEM((rhs, wide), F32),
        ]
        + buffers(),
        compiler_params=params(12),
        cost_estimate=cost(180),
    )(counts, db, pc, fs, cen, tab, acc_i, acc_e, acc_j)
    return own, back


def sums_kernel(cnt, own, back, nug, dirs, res, ritz, image, sums):
    cells = own.shape[1] // PTS
    halo_cells = back.shape[1] // PTS - 1
    lane1 = lax.broadcasted_iota(jnp.int32, (1, PTS), 1)

    def of_cell(c, part, extra):
        live = lane1 < cnt[c]
        d = jnp.where(live, dirs[:, cols(c)], 0.0)
        r = jnp.where(live, res[:, cols(c)], 0.0)
        k = own[:, cols(c)]
        if extra:
            k = k + back[:, cols(c)]
        im = jnp.where(live, nug[:, cols(c)] * d + k, 0.0)
        image[:, cols(c)] = im
        dk, rr, ri, ii, prod = part
        both = jnp.concatenate([r, im], axis=0)
        bh = high(both)
        z = ritz[:, cols(c)]
        zh = high(z)
        left = jnp.concatenate([bh, both - bh], axis=0).astype(BF16)
        right = jnp.concatenate([zh, z - zh], axis=0).astype(BF16)
        return dk + d * im, rr + r * r, ri + r * im, ii + im * im, prod + mm_t(left, right)

    rhs = own.shape[0]
    zero = jnp.zeros((rhs, PTS), F32)
    part = (zero, zero, zero, zero, jnp.zeros((4 * rhs, 2 * ritz.shape[0]), F32))
    part = lax.fori_loop(0, halo_cells, lambda c, p: of_cell(c, p, True), part, unroll=4)
    part = lax.fori_loop(halo_cells, cells, lambda c, p: of_cell(c, p, False), part, unroll=4)
    dots = [jnp.sum(p, axis=1, keepdims=True) for p in part[:4]]
    prod = part[4]
    n = ritz.shape[0]
    h = 2 * rhs
    prod = prod[:h, :n] + prod[:h, n:] + prod[h:, :n]
    sums[...] = jnp.zeros_like(sums)
    sums[:, :n] = prod[:rhs]
    sums[:, n : 2 * n] = prod[rhs:]
    for k in range(4):
        sums[:, 2 * n + k : 2 * n + k + 1] = dots[k]


def local_sums(counts, own, back, nugget, direction, residual, ritz_image):
    return pl.pallas_call(
        sums_kernel,
        name="sums",
        out_shape=[
            jax.ShapeDtypeStruct(own.shape, F32),
            jax.ShapeDtypeStruct((own.shape[0], 128), F32),
        ],
        in_specs=[SM] + [VM] * 6,
        out_specs=[VM, VM],
        compiler_params=params(12),
    )(counts, own, back, nugget, direction, residual, ritz_image)


def finish_kernel(cnt, sums, gram, image, dirs, res, sol, basis, sol_out, res_out, dir_out):
    cells = image.shape[1] // PTS
    n = gram.shape[0]
    lane1 = lax.broadcasted_iota(jnp.int32, (1, PTS), 1)
    curvature, rr, ri, ii = (sums[:, 2 * n + k : 2 * n + k + 1] for k in range(4))
    step = rr / curvature
    growth = (rr + step * (step * ii - 2.0 * ri)) / rr
    projected = sums[:, :n] - step * sums[:, n : 2 * n]
    coef = lax.dot_general(
        projected,
        gram[...],
        (((1,), (1,)), ((), ())),
        precision=lax.Precision.HIGHEST,
        preferred_element_type=F32,
    )
    ch = high(coef)
    left = jnp.concatenate([ch, ch, coef - ch], axis=1).astype(BF16)

    def of_cell(c, _):
        live = lane1 < cnt[c]
        d = jnp.where(live, dirs[:, cols(c)], 0.0)
        r = jnp.where(live, res[:, cols(c)], 0.0)
        s = jnp.where(live, sol[:, cols(c)], 0.0)
        b = basis[:, cols(c)]
        bh = high(b)
        right = jnp.concatenate([bh, b - bh, bh], axis=0).astype(BF16)
        new = r - step * image[:, cols(c)]
        sol_out[:, cols(c)] = s + step * d
        res_out[:, cols(c)] = new
        dir_out[:, cols(c)] = jnp.where(live, growth * d + new - mm(left, right), 0.0)
        return 0

    lax.fori_loop(0, cells, of_cell, 0, unroll=4)


def finish(counts, sums, gram, image, direction, residual, solution, basis):
    return pl.pallas_call(
        finish_kernel,
        name="finish",
        out_shape=[jax.ShapeDtypeStruct(image.shape, F32)] * 3,
        in_specs=[SM] + [VM] * 7,
        out_specs=[VM] * 3,
        compiler_params=params(12),
    )(counts, sums, gram, image, direction, residual, solution, basis)


def passed_along(array, by):
    length = lax.axis_size(AXES)
    pairs = [(i, i + by) for i in range(length) if 0 <= i + by < length]
    return lax.ppermute(array, AXES, pairs)


def summed(array):
    for axis in ("cell", "region"):
        copies = jnp.broadcast_to(array[None], (lax.axis_size(axis),) + array.shape)
        array = jnp.sum(lax.all_to_all(copies, axis, 0, 0), axis=0)
    return array


def local(
    points,
    cell_counts,
    pair_cells,
    pair_counts,
    nugget,
    solution,
    residual,
    direction,
    ritz_basis,
    ritz_image,
    inverse_gram,
):
    own, back = pair_products(cell_counts, points, direction)
    image, sums = local_sums(
        cell_counts, own, back, nugget.reshape(1, -1), direction, residual, ritz_image
    )
    return tuple(
        finish(
            cell_counts,
            summed(sums),
            inverse_gram,
            image,
            direction,
            residual,
            solution,
            ritz_basis,
        )
    )


def solution(mesh):
    split = P(None, AXES)
    line = P(AXES)
    in_specs = (split, line, split, line, line, split, split, split, split, split, P())
    return jax.shard_map(
        local, mesh=mesh, in_specs=in_specs, out_specs=(split,) * 3, check_vma=False
    )
```

```python
import jax
import jax.numpy as jnp
from jax import lax
from jax.experimental import pallas as pl
from jax.experimental.pallas import tpu as pltpu
from jax.sharding import PartitionSpec as P

PTS = 256
REACH = 12
KF = 48
FAR = 1e18
ROOM = 16.0
AXES = ("region", "cell")
F32 = jnp.float32
BF16 = jnp.bfloat16


def mm(x, y):
    return lax.dot_general(x, y, (((1,), (0,)), ((), ())), preferred_element_type=F32)


def mm_t(x, y):
    return lax.dot_general(x, y, (((1,), (1,)), ((), ())), preferred_element_type=F32)


def high(x):
    return x.astype(BF16).astype(F32)


def split3(x):
    h = high(x)
    m = high(x - h)
    return h, m, high(x - h - m)


def tile_of(scaled_square):
    s = jnp.maximum(scaled_square, 1e-30)
    t = s * lax.rsqrt(s)
    u = jnp.maximum(4.0 - t, 0.0)
    u2 = u * u
    return ((u2 * u2) * (t + 1.0)).astype(BF16)


def cols(block, size=PTS):
    return pl.ds(pl.multiple_of(block * size, size), size)


def with_norm(vec):
    row = lax.broadcasted_iota(jnp.int32, vec.shape, 0)
    return row, jnp.sum(vec * vec, axis=0, keepdims=True)


def weights_side(p):
    row, norm = with_norm(p)
    a = jnp.where(row == 3, norm, -2.0 * p)
    h, m, l = split3(a)
    one_h = jnp.where(row == 3, 1.0, h)
    one_m = jnp.where(row == 3, 1.0, m)
    return jnp.concatenate([h, m, one_h, one_m, l, one_h], axis=0).astype(BF16)


def rows_side(q):
    row, norm = with_norm(q)
    a = jnp.where(row == 3, norm, q)
    h, m, l = split3(a)
    one = jnp.where(row == 3, 1.0, h)
    mid_h = jnp.where(row == 3, h, m)
    return jnp.concatenate([one, one, mid_h, m, one, l], axis=0), norm


def pack(cells, cnt, off, dirs, pts, dc, pc):
    lane1 = lax.broadcasted_iota(jnp.int32, (1, PTS), 1)
    lane128 = lax.broadcasted_iota(jnp.int32, (1, 128), 1)
    dc[...] = jnp.zeros_like(dc)
    pc[...] = jnp.zeros_like(pc)

    def place(c, at):
        off[c] = at
        shift = at % 128
        base = pl.multiple_of((at // 128) * 128, 128)
        live = lane1 < cnt[c]
        dv = jnp.where(live, dirs[:, cols(c)], 0.0)
        pv = jnp.where(live, pts[:, cols(c)], 0.0)
        for ref, val in ((dc, dv), (pc, pv)):
            rows = val.shape[0]
            wide = jnp.concatenate([val, jnp.zeros((rows, 128), F32)], axis=1)
            wide = pltpu.roll(wide, shift, 1)
            old = ref[:rows, pl.ds(base, 128)]
            ref[:rows, pl.ds(base, 128)] = jnp.where(lane128 < shift, old, wide[:, :128])
            ref[:rows, pl.ds(base + 128, 256)] = wide[:, 128:]
        return at + cnt[c]

    return lax.fori_loop(0, cells, place, jnp.int32(0), unroll=4)


def prepare(blocks, pc, end, cen, fs):
    lane1 = lax.broadcasted_iota(jnp.int32, (1, PTS), 1)
    lane128 = lax.broadcasted_iota(jnp.int32, (1, 128), 1)

    def one(j, carry):
        low, top, far = carry
        here = pc[:, cols(j)]
        valid = j * PTS + lane1 < end
        lo = jnp.min(jnp.where(valid, here, FAR), axis=1, keepdims=True)
        hi = jnp.max(jnp.where(valid, here, -FAR), axis=1, keepdims=True)
        centre = jnp.where(lo <= hi, 0.5 * (lo + hi), 0.0)
        cen[pl.ds(pl.multiple_of(j * 8, 8), 8), :] = jnp.broadcast_to(centre, (8, 128))
        feats, norm = rows_side(4.0 * (here - centre))
        fs[cols(j), :] = feats.T.astype(BF16)
        low = jnp.where(lane128 == j, lo, low)
        top = jnp.where(lane128 == j, hi, top)
        return low, top, jnp.maximum(far, jnp.where(valid, norm, 0.0))

    start = (
        jnp.full((8, 128), FAR, F32),
        jnp.full((8, 128), -FAR, F32),
        jnp.zeros((1, PTS), F32),
    )
    low, top, far = lax.fori_loop(0, blocks, one, start, unroll=4)
    cen[pl.ds(blocks * 8, 8), :] = jnp.zeros((8, 128), F32)
    fs[pl.ds(blocks * PTS, PTS), :] = jnp.zeros((PTS, KF), BF16)
    wide = jnp.max(far, axis=1, keepdims=True) > 16.0 * ROOM
    return low, top, jnp.where(wide, 1, 0)


def square(v):
    return jnp.concatenate([v, jnp.zeros((120, 128), F32)], axis=0).T


def near(low_i, top_i, low_j, top_j):
    low_t, top_t = square(low_i), square(top_i)
    gap2 = jnp.zeros((128, 128), F32)
    for k in range(3):
        gap = jnp.maximum(
            low_j[k : k + 1] - top_t[:, k : k + 1], low_t[:, k : k + 1] - top_j[k : k + 1]
        )
        gap = jnp.maximum(gap, 0.0)
        gap2 = gap2 + gap * gap
    return gap2 <= 1.001


def as_rows(last):
    last = jnp.max(last.astype(F32), axis=1, keepdims=True)
    return jnp.broadcast_to(last, (128, 128)).T[:8].astype(jnp.int32)


def to_scalars(values, tab_v, tab_s, sem):
    tab_v[...] = values
    copy = pltpu.make_async_copy(tab_v, tab_s, sem)
    copy.start()
    copy.wait()


def sweep(first, end, begin, stop, spare, spread, side_i, side_j, acc_i, acc_j, bufs):
    pc_i, db_i = side_i
    pc_j, db_j, fs_j, cen_j = side_j
    depth = len(bufs)
    zero = jnp.int32(0)

    def enter(i):
        i = jnp.where(i >= end, spare[0], i)
        return i, jnp.where(i == spare[0], spare[1], begin(i))

    def following(i, j):
        n = j + 1
        over = (n >= stop(i)) | (i == spare[0])
        i2, j2 = enter(i + 1)
        return jnp.where(over, i2, i), jnp.where(over, j2, n)

    def squares(i, j, out):
        c = cen_j[pl.ds(pl.multiple_of(j * 8, 8), 8), :]
        f = weights_side(4.0 * (pc_i[:, cols(i)] - jnp.concatenate([c, c], axis=1)))
        out[...] = mm(fs_j[cols(j), :], f)

    same = db_i is db_j

    def products(i, j, tile):
        other = mm_t(db_i[:, cols(i)], tile)
        if same:
            other = other * jnp.where(j > i, 1.0, 0.0)
        return i, j, mm(db_j[:, cols(j)], tile), other

    def add(i, j, mine, other):
        acc_i[:, cols(i)] += mine
        acc_j[:, cols(j)] += other

    total = lax.fori_loop(first, end, lambda i, n: n + stop(i) - begin(i), zero)
    queue = [enter(jnp.int32(first))]
    for _ in range(depth - 1):
        queue.append(following(*queue[-1]))

    @pl.when(spread == 0)
    def _():
        for k in range(depth - 1):
            squares(*queue[k], bufs[k])

        def turn(units):
            def one(_, carry):
                q = list(carry)
                waiting = None
                for g in range(units):
                    squares(*q[-1], bufs[(g + depth - 1) % depth])
                    done = products(*q[0], tile_of(bufs[g % depth][...]))
                    if waiting is not None:
                        add(*waiting)
                    waiting = done
                    q = q[1:] + [following(*q[-1])]
                add(*waiting)
                return tuple(q)

            return one

        state = lax.fori_loop(0, total // LONG, turn(LONG), tuple(queue))
        left = total - (total // LONG) * LONG
        lax.fori_loop(0, (left + depth - 1) // depth, turn(depth), state)

    @pl.when(spread != 0)
    def _():
        def one(_, carry):
            i, j = carry
            pj = pc_j[:, cols(j)].T
            pi = pc_i[:, cols(i)]
            for h in range(0, PTS, 64):
                s = jnp.zeros((64, PTS), F32)
                for k in range(3):
                    d = 4.0 * (pj[h : h + 64, k : k + 1] - pi[k : k + 1, :])
                    s = s + d * d
                bufs[0][pl.ds(h, 64), :] = s
            add(*products(i, j, tile_of(bufs[0][...])))
            return following(i, j)

        lax.fori_loop(0, total, one, queue[0])


def strips_of(cells, cnt):
    return (lax.fori_loop(0, cells, lambda c, n: n + cnt[c], jnp.int32(0)) + (PTS - 1)) // PTS


def early(strips):
    return (strips * EARLY) // 16


def head_kernel(cells, cnt, pts, dirs, db, pc, fs, cen, box, tab, acc_i, acc_j, off, dc, *rest):
    *bufs, tab_s, sem = rest
    acc_i[...] = jnp.zeros_like(acc_i)
    acc_j[...] = jnp.zeros_like(acc_j)
    own_end = pack(cells, cnt, off, dirs, pts, dc, pc)
    strips = (own_end + (PTS - 1)) // PTS
    db[...] = dc[...].astype(BF16)
    low, top, spread = prepare(cells, pc, own_end, cen, fs)
    box[0:8, :] = low
    box[8:16, :] = top
    ri = lax.broadcasted_iota(jnp.int32, (128, 128), 0)
    rj = lax.broadcasted_iota(jnp.int32, (128, 128), 1)
    need = near(low, top, low, top) & (rj > ri)
    stop = as_rows(jnp.where(need, rj + 1, ri + 1))
    lane128 = lax.broadcasted_iota(jnp.int32, (1, 128), 1)
    to_scalars(jnp.where(lane128 == 127, spread, stop), tab, tab_s, sem)
    side = (pc, db, fs, cen)
    sweep(
        0, early(strips), lambda i: i, lambda i: tab_s[0, i], (cells, cells), tab_s[0, 127],
        side[:2], side, acc_i, acc_j, bufs,
    )


def edge_kernel(cells, halo_cells, cnt, db, pc, box, tab, piece, halo, acc_i, hdb, hfs, hcen, tab_v, *rest):
    *bufs, tab_s, sem = rest
    strips = strips_of(cells, cnt)
    acc_i[...] = jnp.zeros_like(acc_i)
    halo[...] = jnp.zeros_like(halo)
    rhs = hdb.shape[0]
    hdb[:, : halo_cells * PTS] = piece[:rhs, :].astype(BF16)
    hdb[:, halo_cells * PTS :] = jnp.zeros((rhs, PTS), BF16)
    hpc = piece.at[rhs : rhs + 8]
    low, top, spread = prepare(halo_cells, hpc, halo_cells * PTS, hcen, hfs)
    ri = lax.broadcasted_iota(jnp.int32, (128, 128), 0)
    rj = lax.broadcasted_iota(jnp.int32, (128, 128), 1)
    need = near(box[0:8, :], box[8:16, :], low, top) & (rj < halo_cells) & (ri < cells)
    stop = as_rows(jnp.where(need, rj + 1, 0))
    lane128 = lax.broadcasted_iota(jnp.int32, (1, 128), 1)
    first = jnp.min(jnp.where(need, ri, 127).astype(F32), axis=(0, 1), keepdims=True)
    stop = jnp.where(lane128 == 126, first.astype(jnp.int32), stop)
    wide = jnp.where((tab[...] != 0) & (lane128 == 127), 1, 0)
    to_scalars(jnp.where(lane128 == 127, spread + wide, stop), tab_v, tab_s, sem)
    sweep(
        jnp.minimum(tab_s[0, 126], strips), strips, lambda i: jnp.int32(0),
        lambda i: jnp.maximum(tab_s[0, i], 1), (cells, halo_cells), tab_s[0, 127],
        (pc, db), (hpc, hdb, hfs, hcen), acc_i, halo, bufs,
    )
    halo[:, : halo_cells * PTS] = halo[:, : halo_cells * PTS] * (1.0 / 256.0)


def tail_kernel(cells, cnt, db, pc, fs, cen, tab, a1, a2, b1, own, off, acc_i, acc_j, *rest):
    bufs = rest
    lane1 = lax.broadcasted_iota(jnp.int32, (1, PTS), 1)
    acc_i[...] = a1[...] + a2[...]
    acc_j[...] = b1[...]

    def place(c, at):
        off[c] = at
        return at + cnt[c]

    end = lax.fori_loop(0, cells, place, jnp.int32(0))
    strips = (end + (PTS - 1)) // PTS
    side = (pc, db, fs, cen)
    sweep(
        early(strips), strips, lambda i: i, lambda i: tab[0, i], (cells, cells), tab[0, 127],
        side[:2], side, acc_i, acc_j, bufs,
    )

    def take(c, _):
        at = off[c]
        base = pl.multiple_of((at // 128) * 128, 128)
        both = acc_i[:, pl.ds(base, 384)] + acc_j[:, pl.ds(base, 384)]
        back = pltpu.roll(both, 384 - at % 128, 1)[:, :PTS] * (1.0 / 256.0)
        own[:, cols(c)] = jnp.where(lane1 < cnt[c], back, 0.0)
        return 0

    lax.fori_loop(0, cells, take, 0, unroll=4)


def piece_kernel(cells, cnt, pts, dirs, piece):
    rhs = dirs.shape[0]
    lane1 = lax.broadcasted_iota(jnp.int32, (1, PTS), 1)
    piece[rhs:, :] = jnp.zeros_like(piece[rhs:, :])
    for c in range(cells):
        at = slice(c * PTS, (c + 1) * PTS)
        live = lane1 < cnt[c]
        piece[:rhs, at] = jnp.where(live, dirs[:, at], 0.0)
        piece[rhs : rhs + 3, at] = jnp.where(live, pts[:, at], pts[:, c * PTS : c * PTS + 1])


VM = pl.BlockSpec(memory_space=pltpu.VMEM)
SM = pl.BlockSpec(memory_space=pltpu.SMEM)
EARLY = 4
LONG = 16
DEPTH = 4


def params(mib):
    return pltpu.CompilerParams(vmem_limit_bytes=mib << 20)


def buffers():
    return [pltpu.VMEM((PTS, PTS), F32)] * DEPTH


def cost(units):
    return pl.CostEstimate(flops=units * 60_000_000, bytes_accessed=4_000_000, transcendentals=units * 65536)


def pair_products(counts, points, direction):
    cells = counts.shape[0]
    rhs = direction.shape[0]
    width = min(cells, REACH)
    blocks = cells + 1
    wide = blocks * PTS + 256
    shape = jax.ShapeDtypeStruct

    piece = pl.pallas_call(
        lambda *refs: piece_kernel(width, *refs),
        name="piece",
        grid=(1,),
        out_shape=shape((rhs + 8, width * PTS), F32),
        in_specs=[
            SM,
            pl.BlockSpec((3, width * PTS), lambda i: (0, 0)),
            pl.BlockSpec((rhs, width * PTS), lambda i: (0, 0)),
        ],
        out_specs=pl.BlockSpec((rhs + 8, width * PTS), lambda i: (0, 0)),
        compiler_params=params(8),
    )(counts, points, direction)
    piece = passed_along(piece, -1)
    db, pc, fs, cen, box, tab, acc_i, acc_j = pl.pallas_call(
        lambda *refs: head_kernel(cells, *refs),
        name="head",
        out_shape=[
            shape((rhs, wide), BF16),
            shape((8, wide), F32),
            shape((blocks * PTS, KF), BF16),
            shape((blocks * 8, 128), F32),
            shape((16, 128), F32),
            shape((8, 128), jnp.int32),
            shape((rhs, wide), F32),
            shape((rhs, wide), F32),
        ],
        in_specs=[SM, VM, VM],
        out_specs=[VM] * 8,
        scratch_shapes=[pltpu.SMEM((cells,), jnp.int32), pltpu.VMEM((rhs, wide), F32)]
        + buffers()
        + [pltpu.SMEM((8, 128), jnp.int32), pltpu.SemaphoreType.DMA],
        compiler_params=params(12),
        cost_estimate=cost(100),
    )(counts, points, direction)
    halo, acc_e = pl.pallas_call(
        lambda *refs: edge_kernel(cells, width, *refs),
        name="edge",
        out_shape=[shape((rhs, (width + 1) * PTS), F32), shape((rhs, wide), F32)],
        in_specs=[SM] + [VM] * 5,
        out_specs=[VM] * 2,
        scratch_shapes=[
            pltpu.VMEM((rhs, (width + 1) * PTS), BF16),
            pltpu.VMEM(((width + 1) * PTS, KF), BF16),
            pltpu.VMEM(((width + 1) * 8, 128), F32),
            pltpu.VMEM((8, 128), jnp.int32),
        ]
        + buffers()
        + [pltpu.SMEM((8, 128), jnp.int32), pltpu.SemaphoreType.DMA],
        compiler_params=params(12),
        cost_estimate=cost(70),
    )(counts, db, pc, box, tab, piece)
    back = passed_along(halo, 1)
    own = pl.pallas_call(
        lambda *refs: tail_kernel(cells, *refs),
        name="tail",
        out_shape=shape((rhs, cells * PTS), F32),
        in_specs=[SM] + [VM] * 4 + [SM] + [VM] * 3,
        out_specs=VM,
        scratch_shapes=[
            pltpu.SMEM((cells,), jnp.int32),
            pltpu.VMEM((rhs, wide), F32),
            pltpu.VMEM((rhs, wide), F32),
        ]
        + buffers(),
        compiler_params=params(12),
        cost_estimate=cost(180),
    )(counts, db, pc, fs, cen, tab, acc_i, acc_e, acc_j)
    return own, back


def sums_kernel(cnt, own, back, nug, dirs, res, ritz, image, sums):
    cells = own.shape[1] // PTS
    halo_cells = back.shape[1] // PTS - 1
    lane1 = lax.broadcasted_iota(jnp.int32, (1, PTS), 1)

    def of_cell(c, part, extra):
        live = lane1 < cnt[c]
        d = jnp.where(live, dirs[:, cols(c)], 0.0)
        r = jnp.where(live, res[:, cols(c)], 0.0)
        k = own[:, cols(c)]
        if extra:
            k = k + back[:, cols(c)]
        im = jnp.where(live, nug[:, cols(c)] * d + k, 0.0)
        image[:, cols(c)] = im
        dk, rr, ri, ii, prod = part
        both = jnp.concatenate([r, im], axis=0)
        bh = high(both)
        z = ritz[:, cols(c)]
        zh = high(z)
        left = jnp.concatenate([bh, both - bh], axis=0).astype(BF16)
        right = jnp.concatenate([zh, z - zh], axis=0).astype(BF16)
        return dk + d * im, rr + r * r, ri + r * im, ii + im * im, prod + mm_t(left, right)

    rhs = own.shape[0]
    zero = jnp.zeros((rhs, PTS), F32)
    part = (zero, zero, zero, zero, jnp.zeros((4 * rhs, 2 * ritz.shape[0]), F32))
    part = lax.fori_loop(0, halo_cells, lambda c, p: of_cell(c, p, True), part, unroll=4)
    part = lax.fori_loop(halo_cells, cells, lambda c, p: of_cell(c, p, False), part, unroll=4)
    dots = [jnp.sum(p, axis=1, keepdims=True) for p in part[:4]]
    prod = part[4]
    n = ritz.shape[0]
    h = 2 * rhs
    prod = prod[:h, :n] + prod[:h, n:] + prod[h:, :n]
    sums[...] = jnp.zeros_like(sums)
    sums[:, :n] = prod[:rhs]
    sums[:, n : 2 * n] = prod[rhs:]
    for k in range(4):
        sums[:, 2 * n + k : 2 * n + k + 1] = dots[k]


def local_sums(counts, own, back, nugget, direction, residual, ritz_image):
    return pl.pallas_call(
        sums_kernel,
        name="sums",
        out_shape=[
            jax.ShapeDtypeStruct(own.shape, F32),
            jax.ShapeDtypeStruct((own.shape[0], 128), F32),
        ],
        in_specs=[SM] + [VM] * 6,
        out_specs=[VM, VM],
        compiler_params=params(12),
    )(counts, own, back, nugget, direction, residual, ritz_image)


def finish_kernel(cnt, sums, gram, image, dirs, res, sol, basis, sol_out, res_out, dir_out):
    cells = image.shape[1] // PTS
    n = gram.shape[0]
    lane1 = lax.broadcasted_iota(jnp.int32, (1, PTS), 1)
    curvature, rr, ri, ii = (sums[:, 2 * n + k : 2 * n + k + 1] for k in range(4))
    step = rr / curvature
    growth = (rr + step * (step * ii - 2.0 * ri)) / rr
    projected = sums[:, :n] - step * sums[:, n : 2 * n]
    coef = lax.dot_general(
        projected,
        gram[...],
        (((1,), (1,)), ((), ())),
        precision=lax.Precision.HIGHEST,
        preferred_element_type=F32,
    )
    ch = high(coef)
    left = jnp.concatenate([ch, ch, coef - ch], axis=1).astype(BF16)

    def of_cell(c, _):
        live = lane1 < cnt[c]
        d = jnp.where(live, dirs[:, cols(c)], 0.0)
        r = jnp.where(live, res[:, cols(c)], 0.0)
        s = jnp.where(live, sol[:, cols(c)], 0.0)
        b = basis[:, cols(c)]
        bh = high(b)
        right = jnp.concatenate([bh, b - bh, bh], axis=0).astype(BF16)
        new = r - step * image[:, cols(c)]
        sol_out[:, cols(c)] = s + step * d
        res_out[:, cols(c)] = new
        dir_out[:, cols(c)] = jnp.where(live, growth * d + new - mm(left, right), 0.0)
        return 0

    lax.fori_loop(0, cells, of_cell, 0, unroll=4)


def finish(counts, sums, gram, image, direction, residual, solution, basis):
    return pl.pallas_call(
        finish_kernel,
        name="finish",
        out_shape=[jax.ShapeDtypeStruct(image.shape, F32)] * 3,
        in_specs=[SM] + [VM] * 7,
        out_specs=[VM] * 3,
        compiler_params=params(12),
    )(counts, sums, gram, image, direction, residual, solution, basis)


def passed_along(array, by):
    length = lax.axis_size(AXES)
    pairs = [(i, i + by) for i in range(length) if 0 <= i + by < length]
    return lax.ppermute(array, AXES, pairs)


def summed(array):
    for axis in ("cell", "region"):
        copies = jnp.broadcast_to(array[None], (lax.axis_size(axis),) + array.shape)
        array = jnp.sum(lax.all_to_all(copies, axis, 0, 0), axis=0)
    return array


def local(
    points,
    cell_counts,
    pair_cells,
    pair_counts,
    nugget,
    solution,
    residual,
    direction,
    ritz_basis,
    ritz_image,
    inverse_gram,
):
    own, back = pair_products(cell_counts, points, direction)
    image, sums = local_sums(
        cell_counts, own, back, nugget.reshape(1, -1), direction, residual, ritz_image
    )
    return tuple(
        finish(
            cell_counts,
            summed(sums),
            inverse_gram,
            image,
            direction,
            residual,
            solution,
            ritz_basis,
        )
    )


def solution(mesh):
    split = P(None, AXES)
    line = P(AXES)
    in_specs = (split, line, split, line, line, split, split, split, split, split, P())
    return jax.shard_map(
        local, mesh=mesh, in_specs=in_specs, out_specs=(split,) * 3, check_vma=False
    )
```

```python
import jax
import jax.numpy as jnp
from jax import lax
from jax.experimental import pallas as pl
from jax.experimental.pallas import tpu as pltpu
from jax.sharding import PartitionSpec as P

PTS = 256
REACH = 12
KF = 48
FAR = 1e18
ROOM = 16.0
AXES = ("region", "cell")
F32 = jnp.float32
BF16 = jnp.bfloat16


def mm(x, y):
    return lax.dot_general(x, y, (((1,), (0,)), ((), ())), preferred_element_type=F32)


def mm_t(x, y):
    return lax.dot_general(x, y, (((1,), (1,)), ((), ())), preferred_element_type=F32)


def high(x):
    return x.astype(BF16).astype(F32)


def split3(x):
    h = high(x)
    m = high(x - h)
    return h, m, high(x - h - m)


def tile_of(scaled_square):
    s = jnp.maximum(scaled_square, 1e-30)
    t = s * lax.rsqrt(s)
    u = jnp.maximum(4.0 - t, 0.0)
    u2 = u * u
    return ((u2 * u2) * (t + 1.0)).astype(BF16)


def cols(block, size=PTS):
    return pl.ds(pl.multiple_of(block * size, size), size)


def with_norm(vec):
    row = lax.broadcasted_iota(jnp.int32, vec.shape, 0)
    return row, jnp.sum(vec * vec, axis=0, keepdims=True)


def weights_side(p):
    row, norm = with_norm(p)
    a = jnp.where(row == 3, norm, -2.0 * p)
    h, m, l = split3(a)
    one_h = jnp.where(row == 3, 1.0, h)
    one_m = jnp.where(row == 3, 1.0, m)
    return jnp.concatenate([h, m, one_h, one_m, l, one_h], axis=0).astype(BF16)


def rows_side(q):
    row, norm = with_norm(q)
    a = jnp.where(row == 3, norm, q)
    h, m, l = split3(a)
    one = jnp.where(row == 3, 1.0, h)
    mid_h = jnp.where(row == 3, h, m)
    return jnp.concatenate([one, one, mid_h, m, one, l], axis=0), norm


def pack(cells, cnt, off, dirs, pts, dc, pc):
    lane1 = lax.broadcasted_iota(jnp.int32, (1, PTS), 1)
    lane128 = lax.broadcasted_iota(jnp.int32, (1, 128), 1)

    def place(c, at):
        off[c] = at
        shift = at % 128
        base = pl.multiple_of((at // 128) * 128, 128)
        live = lane1 < cnt[c]
        dv = jnp.where(live, dirs[:, cols(c)], 0.0)
        pv = jnp.where(live, pts[:, cols(c)], 0.0)
        for ref, val in ((dc, dv), (pc, pv)):
            rows = val.shape[0]
            wide = jnp.concatenate([val, jnp.zeros((rows, 128), F32)], axis=1)
            wide = pltpu.roll(wide, shift, 1)
            old = ref[:rows, pl.ds(base, 128)]
            ref[:rows, pl.ds(base, 128)] = jnp.where(lane128 < shift, old, wide[:, :128])
            ref[:rows, pl.ds(base + 128, 256)] = wide[:, 128:]
        return at + cnt[c]

    return lax.fori_loop(0, cells, place, jnp.int32(0), unroll=8)


def prepare(blocks, pc, end, cen, fs):
    lane1 = lax.broadcasted_iota(jnp.int32, (1, PTS), 1)
    lane128 = lax.broadcasted_iota(jnp.int32, (1, 128), 1)

    def one(j, carry):
        low, top, far = carry
        here = pc[:, cols(j)]
        valid = j * PTS + lane1 < end
        lo = jnp.min(jnp.where(valid, here, FAR), axis=1, keepdims=True)
        hi = jnp.max(jnp.where(valid, here, -FAR), axis=1, keepdims=True)
        centre = jnp.where(lo <= hi, 0.5 * (lo + hi), 0.0)
        cen[pl.ds(pl.multiple_of(j * 8, 8), 8), :] = jnp.broadcast_to(centre, (8, 128))
        feats, norm = rows_side(4.0 * (here - centre))
        fs[cols(j), :] = feats.T.astype(BF16)
        low = jnp.where(lane128 == j, lo, low)
        top = jnp.where(lane128 == j, hi, top)
        return low, top, jnp.maximum(far, jnp.where(valid, norm, 0.0))

    start = (
        jnp.full((8, 128), FAR, F32),
        jnp.full((8, 128), -FAR, F32),
        jnp.zeros((1, PTS), F32),
    )
    low, top, far = lax.fori_loop(0, blocks, one, start, unroll=4 if blocks % 8 else 8)
    cen[pl.ds(blocks * 8, 8), :] = jnp.zeros((8, 128), F32)
    fs[pl.ds(blocks * PTS, PTS), :] = jnp.zeros((PTS, KF), BF16)
    wide = jnp.max(far, axis=1, keepdims=True) > 16.0 * ROOM
    return low, top, jnp.where(wide, 1, 0)


def square(v):
    return jnp.concatenate([v, jnp.zeros((120, 128), F32)], axis=0).T


def near(low_i, top_i, low_j, top_j):
    low_t, top_t = square(low_i), square(top_i)
    gap2 = jnp.zeros((128, 128), F32)
    for k in range(3):
        gap = jnp.maximum(
            low_j[k : k + 1] - top_t[:, k : k + 1], low_t[:, k : k + 1] - top_j[k : k + 1]
        )
        gap = jnp.maximum(gap, 0.0)
        gap2 = gap2 + gap * gap
    return gap2 <= 1.001


def as_rows(last):
    last = jnp.max(last.astype(F32), axis=1, keepdims=True)
    return jnp.broadcast_to(last, (128, 128)).T[:8].astype(jnp.int32)


def to_scalars(values, tab_v, tab_s, sem):
    tab_v[...] = values
    copy = pltpu.make_async_copy(tab_v, tab_s, sem)
    copy.start()
    copy.wait()


def sweep(first, end, begin, stop, spare, spread, side_i, side_j, acc_i, acc_j, bufs):
    pc_i, db_i = side_i
    pc_j, db_j, fs_j, cen_j = side_j
    depth = len(bufs)
    zero = jnp.int32(0)

    def enter(i):
        i = jnp.where(i >= end, spare[0], i)
        return i, jnp.where(i == spare[0], spare[1], begin(i))

    def following(i, j):
        n = j + 1
        over = (n >= stop(i)) | (i == spare[0])
        i2, j2 = enter(i + 1)
        return jnp.where(over, i2, i), jnp.where(over, j2, n)

    def squares(i, j, out):
        c = cen_j[pl.ds(pl.multiple_of(j * 8, 8), 8), :]
        f = weights_side(4.0 * (pc_i[:, cols(i)] - jnp.concatenate([c, c], axis=1)))
        out[...] = mm(fs_j[cols(j), :], f)

    same = db_i is db_j

    def products(i, j, tile):
        other = mm_t(db_i[:, cols(i)], tile)
        if same:
            other = other * jnp.where(j > i, 1.0, 0.0)
        return i, j, mm(db_j[:, cols(j)], tile), other

    def add(i, j, mine, other):
        acc_i[:, cols(i)] += mine
        acc_j[:, cols(j)] += other

    total = lax.fori_loop(first, end, lambda i, n: n + stop(i) - begin(i), zero)
    queue = [enter(jnp.int32(first))]
    for _ in range(depth - 1):
        queue.append(following(*queue[-1]))

    @pl.when(spread == 0)
    def _():
        for k in range(depth - 1):
            squares(*queue[k], bufs[k])

        def turn(units):
            def one(_, carry):
                q = list(carry)
                waiting = None
                for g in range(units):
                    squares(*q[-1], bufs[(g + depth - 1) % depth])
                    done = products(*q[0], tile_of(bufs[g % depth][...]))
                    if waiting is not None:
                        add(*waiting)
                    waiting = done
                    q = q[1:] + [following(*q[-1])]
                add(*waiting)
                return tuple(q)

            return one

        state = lax.fori_loop(0, total // LONG, turn(LONG), tuple(queue))
        left = total - (total // LONG) * LONG
        lax.fori_loop(0, (left + depth - 1) // depth, turn(depth), state)

    @pl.when(spread != 0)
    def _():
        def one(_, carry):
            i, j = carry
            pj = pc_j[:, cols(j)].T
            pi = pc_i[:, cols(i)]
            for h in range(0, PTS, 64):
                s = jnp.zeros((64, PTS), F32)
                for k in range(3):
                    d = 4.0 * (pj[h : h + 64, k : k + 1] - pi[k : k + 1, :])
                    s = s + d * d
                bufs[0][pl.ds(h, 64), :] = s
            add(*products(i, j, tile_of(bufs[0][...])))
            return following(i, j)

        lax.fori_loop(0, total, one, queue[0])


def strips_of(cells, cnt):
    return (lax.fori_loop(0, cells, lambda c, n: n + cnt[c], jnp.int32(0)) + (PTS - 1)) // PTS


def fetch(pairs, sems):
    copies = [pltpu.make_async_copy(src, dst, sems.at[k]) for k, (src, dst) in enumerate(pairs)]
    for copy in copies:
        copy.start()
    return copies


def head_kernel(cells, cnt_h, pts_h, dirs_h, db, pc, fs, cen, box, tab, cnt, pts, dirs, off, dc, sem):
    copies = fetch(((cnt_h, cnt), (pts_h, pts), (dirs_h, dirs)), sem)
    dc[...] = jnp.zeros_like(dc)
    pc[...] = jnp.zeros_like(pc)
    for copy in copies:
        copy.wait()
    own_end = pack(cells, cnt, off, dirs, pts, dc, pc)
    db[...] = dc[...].astype(BF16)
    low, top, spread = prepare(cells, pc, own_end, cen, fs)
    box[0:8, :] = low
    box[8:16, :] = top
    ri = lax.broadcasted_iota(jnp.int32, (128, 128), 0)
    rj = lax.broadcasted_iota(jnp.int32, (128, 128), 1)
    need = near(low, top, low, top) & (rj > ri)
    stop = as_rows(jnp.where(need, rj + 1, ri + 1))
    lane128 = lax.broadcasted_iota(jnp.int32, (1, 128), 1)
    tab[...] = jnp.where(lane128 == 127, spread, stop)


def edge_kernel(cells, halo_cells, cnt, db, pc, box, tab, piece, halo, acc_i, hdb, hfs, hcen, tab_v, *rest):
    *bufs, tab_s, sem = rest
    strips = strips_of(cells, cnt)
    acc_i[...] = jnp.zeros_like(acc_i)
    halo[...] = jnp.zeros_like(halo)
    rhs = hdb.shape[0]
    hdb[:, : halo_cells * PTS] = piece[:rhs, :].astype(BF16)
    hdb[:, halo_cells * PTS :] = jnp.zeros((rhs, PTS), BF16)
    hpc = piece.at[rhs : rhs + 8]
    low, top, spread = prepare(halo_cells, hpc, halo_cells * PTS, hcen, hfs)
    ri = lax.broadcasted_iota(jnp.int32, (128, 128), 0)
    rj = lax.broadcasted_iota(jnp.int32, (128, 128), 1)
    need = near(box[0:8, :], box[8:16, :], low, top) & (rj < halo_cells) & (ri < cells)
    stop = as_rows(jnp.where(need, rj + 1, 0))
    lane128 = lax.broadcasted_iota(jnp.int32, (1, 128), 1)
    first = jnp.min(jnp.where(need, ri, 127).astype(F32), axis=(0, 1), keepdims=True)
    stop = jnp.where(lane128 == 126, first.astype(jnp.int32), stop)
    wide = jnp.where((tab[...] != 0) & (lane128 == 127), 1, 0)
    to_scalars(jnp.where(lane128 == 127, spread + wide, stop), tab_v, tab_s, sem)
    sweep(
        jnp.minimum(tab_s[0, 126], strips), strips, lambda i: jnp.int32(0),
        lambda i: jnp.maximum(tab_s[0, i], 1), (cells, halo_cells), tab_s[0, 127],
        (pc, db), (hpc, hdb, hfs, hcen), acc_i, halo, bufs,
    )
    halo[:, : halo_cells * PTS] = halo[:, : halo_cells * PTS] * (1.0 / 256.0)


def tail_kernel(cells, cnt, db, pc, fs, cen, tab, acc_e, own, off, acc_i, acc_j, *rest):
    bufs = rest
    lane1 = lax.broadcasted_iota(jnp.int32, (1, PTS), 1)
    acc_i[...] = acc_e[...]
    acc_j[...] = jnp.zeros_like(acc_j)

    def place(c, at):
        off[c] = at
        return at + cnt[c]

    end = lax.fori_loop(0, cells, place, jnp.int32(0))
    strips = (end + (PTS - 1)) // PTS
    side = (pc, db, fs, cen)
    sweep(
        0, strips, lambda i: i, lambda i: tab[0, i], (cells, cells), tab[0, 127],
        side[:2], side, acc_i, acc_j, bufs,
    )

    def take(c, _):
        at = off[c]
        base = pl.multiple_of((at // 128) * 128, 128)
        both = acc_i[:, pl.ds(base, 384)] + acc_j[:, pl.ds(base, 384)]
        back = pltpu.roll(both, 384 - at % 128, 1)[:, :PTS] * (1.0 / 256.0)
        own[:, cols(c)] = jnp.where(lane1 < cnt[c], back, 0.0)
        return 0

    lax.fori_loop(0, cells, take, 0, unroll=4)


def piece_kernel(cells, cnt_h, pts_h, dirs_h, piece, cnt, pts, dirs, sem):
    rhs = dirs.shape[0]
    span = pl.ds(0, cells * PTS)
    copies = fetch(((cnt_h, cnt), (pts_h.at[:, span], pts), (dirs_h.at[:, span], dirs)), sem)
    lane1 = lax.broadcasted_iota(jnp.int32, (1, PTS), 1)
    piece[rhs:, :] = jnp.zeros_like(piece[rhs:, :])
    for copy in copies:
        copy.wait()
    for c in range(cells):
        at = slice(c * PTS, (c + 1) * PTS)
        live = lane1 < cnt[c]
        piece[:rhs, at] = jnp.where(live, dirs[:, at], 0.0)
        piece[rhs : rhs + 3, at] = jnp.where(live, pts[:, at], pts[:, c * PTS : c * PTS + 1])


VM = pl.BlockSpec(memory_space=pltpu.VMEM)
SM = pl.BlockSpec(memory_space=pltpu.SMEM)
HB = pl.BlockSpec(memory_space=pltpu.MemorySpace.HBM)
LONG = 16
DEPTH = 4


def params(mib):
    return pltpu.CompilerParams(vmem_limit_bytes=mib << 20)


def buffers():
    return [pltpu.VMEM((PTS, PTS), F32)] * DEPTH


def cost(units):
    return pl.CostEstimate(flops=units * 60_000_000, bytes_accessed=4_000_000, transcendentals=units * 65536)


def pair_products(counts, points, direction):
    cells = counts.shape[0]
    rhs = direction.shape[0]
    width = min(cells, REACH)
    blocks = cells + 1
    wide = blocks * PTS + 256
    shape = jax.ShapeDtypeStruct

    piece = pl.pallas_call(
        lambda *refs: piece_kernel(width, *refs),
        name="piece",
        out_shape=shape((rhs + 8, width * PTS), F32),
        in_specs=[HB] * 3,
        out_specs=VM,
        scratch_shapes=[
            pltpu.SMEM((cells,), jnp.int32),
            pltpu.VMEM((3, width * PTS), F32),
            pltpu.VMEM((rhs, width * PTS), F32),
            pltpu.SemaphoreType.DMA((3,)),
        ],
        compiler_params=params(8),
    )(counts, points, direction)
    piece = passed_along(piece, -1)
    db, pc, fs, cen, box, tab = pl.pallas_call(
        lambda *refs: head_kernel(cells, *refs),
        name="head",
        out_shape=[
            shape((rhs, wide), BF16),
            shape((8, wide), F32),
            shape((blocks * PTS, KF), BF16),
            shape((blocks * 8, 128), F32),
            shape((16, 128), F32),
            shape((8, 128), jnp.int32),
        ],
        in_specs=[HB] * 3,
        out_specs=[VM] * 6,
        scratch_shapes=[
            pltpu.SMEM((cells,), jnp.int32),
            pltpu.VMEM(points.shape, F32),
            pltpu.VMEM(direction.shape, F32),
            pltpu.SMEM((cells,), jnp.int32),
            pltpu.VMEM((rhs, wide), F32),
            pltpu.SemaphoreType.DMA((3,)),
        ],
        compiler_params=params(12),
        cost_estimate=cost(100),
    )(counts, points, direction)
    halo, acc_e = pl.pallas_call(
        lambda *refs: edge_kernel(cells, width, *refs),
        name="edge",
        out_shape=[shape((rhs, (width + 1) * PTS), F32), shape((rhs, wide), F32)],
        in_specs=[SM] + [VM] * 5,
        out_specs=[VM] * 2,
        scratch_shapes=[
            pltpu.VMEM((rhs, (width + 1) * PTS), BF16),
            pltpu.VMEM(((width + 1) * PTS, KF), BF16),
            pltpu.VMEM(((width + 1) * 8, 128), F32),
            pltpu.VMEM((8, 128), jnp.int32),
        ]
        + buffers()
        + [pltpu.SMEM((8, 128), jnp.int32), pltpu.SemaphoreType.DMA],
        compiler_params=params(12),
        cost_estimate=cost(70),
    )(counts, db, pc, box, tab, piece)
    back = passed_along(halo, 1)
    own = pl.pallas_call(
        lambda *refs: tail_kernel(cells, *refs),
        name="tail",
        out_shape=shape((rhs, cells * PTS), F32),
        in_specs=[SM] + [VM] * 4 + [SM, VM],
        out_specs=VM,
        scratch_shapes=[
            pltpu.SMEM((cells,), jnp.int32),
            pltpu.VMEM((rhs, wide), F32),
            pltpu.VMEM((rhs, wide), F32),
        ]
        + buffers(),
        compiler_params=params(12),
        cost_estimate=cost(180),
    )(counts, db, pc, fs, cen, tab, acc_e)
    return own, back


def sums_kernel(cnt, own, back, nug, dirs, res, ritz, image, sums):
    cells = own.shape[1] // PTS
    halo_cells = back.shape[1] // PTS - 1
    lane1 = lax.broadcasted_iota(jnp.int32, (1, PTS), 1)

    def of_cell(c, part, extra):
        live = lane1 < cnt[c]
        d = jnp.where(live, dirs[:, cols(c)], 0.0)
        r = jnp.where(live, res[:, cols(c)], 0.0)
        k = own[:, cols(c)]
        if extra:
            k = k + back[:, cols(c)]
        im = jnp.where(live, nug[:, cols(c)] * d + k, 0.0)
        image[:, cols(c)] = im
        dk, rr, ri, ii, prod = part
        both = jnp.concatenate([r, im], axis=0)
        bh = high(both)
        z = ritz[:, cols(c)]
        zh = high(z)
        left = jnp.concatenate([bh, both - bh], axis=0).astype(BF16)
        right = jnp.concatenate([zh, z - zh], axis=0).astype(BF16)
        return dk + d * im, rr + r * r, ri + r * im, ii + im * im, prod + mm_t(left, right)

    rhs = own.shape[0]
    zero = jnp.zeros((rhs, PTS), F32)
    part = (zero, zero, zero, zero, jnp.zeros((4 * rhs, 2 * ritz.shape[0]), F32))
    part = lax.fori_loop(0, halo_cells, lambda c, p: of_cell(c, p, True), part, unroll=4)
    part = lax.fori_loop(halo_cells, cells, lambda c, p: of_cell(c, p, False), part, unroll=4)
    dots = [jnp.sum(p, axis=1, keepdims=True) for p in part[:4]]
    prod = part[4]
    n = ritz.shape[0]
    h = 2 * rhs
    prod = prod[:h, :n] + prod[:h, n:] + prod[h:, :n]
    sums[...] = jnp.zeros_like(sums)
    sums[:, :n] = prod[:rhs]
    sums[:, n : 2 * n] = prod[rhs:]
    for k in range(4):
        sums[:, 2 * n + k : 2 * n + k + 1] = dots[k]


def local_sums(counts, own, back, nugget, direction, residual, ritz_image):
    return pl.pallas_call(
        sums_kernel,
        name="sums",
        out_shape=[
            jax.ShapeDtypeStruct(own.shape, F32),
            jax.ShapeDtypeStruct((own.shape[0], 128), F32),
        ],
        in_specs=[SM] + [VM] * 6,
        out_specs=[VM, VM],
        compiler_params=params(12),
    )(counts, own, back, nugget, direction, residual, ritz_image)


def finish_kernel(
    cnt, sums, gram, image, dirs, res, sol, basis, sol_h, res_h, dir_h, sol_out, res_out, dir_out, sem
):
    cells = image.shape[1] // PTS
    n = gram.shape[0]
    lane1 = lax.broadcasted_iota(jnp.int32, (1, PTS), 1)
    curvature, rr, ri, ii = (sums[:, 2 * n + k : 2 * n + k + 1] for k in range(4))
    step = rr / curvature
    growth = (rr + step * (step * ii - 2.0 * ri)) / rr
    projected = sums[:, :n] - step * sums[:, n : 2 * n]
    coef = lax.dot_general(
        projected,
        gram[...],
        (((1,), (1,)), ((), ())),
        precision=lax.Precision.HIGHEST,
        preferred_element_type=F32,
    )
    ch = high(coef)
    left = jnp.concatenate([ch, ch, coef - ch], axis=1).astype(BF16)

    def of_cell(c, _):
        live = lane1 < cnt[c]
        d = jnp.where(live, dirs[:, cols(c)], 0.0)
        r = jnp.where(live, res[:, cols(c)], 0.0)
        s = jnp.where(live, sol[:, cols(c)], 0.0)
        b = basis[:, cols(c)]
        bh = high(b)
        right = jnp.concatenate([bh, b - bh, bh], axis=0).astype(BF16)
        new = r - step * image[:, cols(c)]
        sol_out[:, cols(c)] = s + step * d
        res_out[:, cols(c)] = new
        dir_out[:, cols(c)] = jnp.where(live, growth * d + new - mm(left, right), 0.0)
        return 0

    pieces = 4
    many = cells // pieces
    copies = []
    for k in range(pieces):
        lax.fori_loop(k * many, (k + 1) * many, of_cell, 0, unroll=4)
        at = pl.ds(k * many * PTS, many * PTS)
        for n, (src, dst) in enumerate(((sol_out, sol_h), (res_out, res_h), (dir_out, dir_h))):
            copies.append(pltpu.make_async_copy(src.at[:, at], dst.at[:, at], sem.at[3 * k + n]))
            copies[-1].start()
    for copy in copies:
        copy.wait()


def finish(counts, sums, gram, image, direction, residual, solution, basis):
    return pl.pallas_call(
        finish_kernel,
        name="finish",
        out_shape=[jax.ShapeDtypeStruct(image.shape, F32)] * 3,
        in_specs=[SM] + [VM] * 7,
        out_specs=[HB] * 3,
        scratch_shapes=[pltpu.VMEM(image.shape, F32)] * 3 + [pltpu.SemaphoreType.DMA((12,))],
        compiler_params=params(12),
    )(counts, sums, gram, image, direction, residual, solution, basis)


def passed_along(array, by):
    length = lax.axis_size(AXES)
    pairs = [(i, i + by) for i in range(length) if 0 <= i + by < length]
    return lax.ppermute(array, AXES, pairs)


def summed(array):
    for axis in ("cell", "region"):
        copies = jnp.broadcast_to(array[None], (lax.axis_size(axis),) + array.shape)
        array = jnp.sum(lax.all_to_all(copies, axis, 0, 0), axis=0)
    return array


def local(
    points,
    cell_counts,
    pair_cells,
    pair_counts,
    nugget,
    solution,
    residual,
    direction,
    ritz_basis,
    ritz_image,
    inverse_gram,
):
    own, back = pair_products(cell_counts, points, direction)
    image, sums = local_sums(
        cell_counts, own, back, nugget.reshape(1, -1), direction, residual, ritz_image
    )
    return tuple(
        finish(
            cell_counts,
            summed(sums),
            inverse_gram,
            image,
            direction,
            residual,
            solution,
            ritz_basis,
        )
    )


def solution(mesh):
    split = P(None, AXES)
    line = P(AXES)
    in_specs = (split, line, split, line, line, split, split, split, split, split, P())
    return jax.shard_map(
        local, mesh=mesh, in_specs=in_specs, out_specs=(split,) * 3, check_vma=False
    )
```

```python
import jax
import jax.numpy as jnp
from jax import lax
from jax.experimental import pallas as pl
from jax.experimental.pallas import tpu as pltpu
from jax.sharding import PartitionSpec as P

PTS = 256
REACH = 12
KF = 48
FAR = 1e18
ROOM = 16.0
AXES = ("region", "cell")
F32 = jnp.float32
BF16 = jnp.bfloat16


def mm(x, y):
    return lax.dot_general(x, y, (((1,), (0,)), ((), ())), preferred_element_type=F32)


def mm_t(x, y):
    return lax.dot_general(x, y, (((1,), (1,)), ((), ())), preferred_element_type=F32)


def high(x):
    return x.astype(BF16).astype(F32)


def split3(x):
    h = high(x)
    m = high(x - h)
    return h, m, high(x - h - m)


def tile_of(scaled_square):
    s = jnp.maximum(scaled_square, 1e-30)
    t = s * lax.rsqrt(s)
    u = jnp.maximum(4.0 - t, 0.0)
    u2 = u * u
    return ((u2 * u2) * (t + 1.0)).astype(BF16)


def cols(block, size=PTS):
    return pl.ds(pl.multiple_of(block * size, size), size)


def with_norm(vec):
    row = lax.broadcasted_iota(jnp.int32, vec.shape, 0)
    return row, jnp.sum(vec * vec, axis=0, keepdims=True)


def weights_side(p):
    row, norm = with_norm(p)
    a = jnp.where(row == 3, norm, -2.0 * p)
    h, m, l = split3(a)
    one_h = jnp.where(row == 3, 1.0, h)
    one_m = jnp.where(row == 3, 1.0, m)
    return jnp.concatenate([h, m, one_h, one_m, l, one_h], axis=0).astype(BF16)


def rows_side(q):
    row, norm = with_norm(q)
    a = jnp.where(row == 3, norm, q)
    h, m, l = split3(a)
    one = jnp.where(row == 3, 1.0, h)
    mid_h = jnp.where(row == 3, h, m)
    return jnp.concatenate([one, one, mid_h, m, one, l], axis=0), norm


def pack(cells, cnt, off, dirs, pts, dc, pc):
    lane1 = lax.broadcasted_iota(jnp.int32, (1, PTS), 1)
    lane128 = lax.broadcasted_iota(jnp.int32, (1, 128), 1)

    def place(c, at):
        off[c] = at
        shift = at % 128
        base = pl.multiple_of((at // 128) * 128, 128)
        live = lane1 < cnt[c]
        dv = jnp.where(live, dirs[:, cols(c)], 0.0)
        pv = jnp.where(live, pts[:, cols(c)], 0.0)
        for ref, val in ((dc, dv), (pc, pv)):
            rows = val.shape[0]
            wide = jnp.concatenate([val, jnp.zeros((rows, 128), F32)], axis=1)
            wide = pltpu.roll(wide, shift, 1)
            old = ref[:rows, pl.ds(base, 128)]
            ref[:rows, pl.ds(base, 128)] = jnp.where(lane128 < shift, old, wide[:, :128])
            ref[:rows, pl.ds(base + 128, 256)] = wide[:, 128:]
        return at + cnt[c]

    return lax.fori_loop(0, cells, place, jnp.int32(0), unroll=8)


def prepare(blocks, pc, end, cen, fs):
    lane1 = lax.broadcasted_iota(jnp.int32, (1, PTS), 1)
    lane128 = lax.broadcasted_iota(jnp.int32, (1, 128), 1)

    def one(j, carry):
        low, top, far = carry
        here = pc[:, cols(j)]
        valid = j * PTS + lane1 < end
        lo = jnp.min(jnp.where(valid, here, FAR), axis=1, keepdims=True)
        hi = jnp.max(jnp.where(valid, here, -FAR), axis=1, keepdims=True)
        centre = jnp.where(lo <= hi, 0.5 * (lo + hi), 0.0)
        cen[pl.ds(pl.multiple_of(j * 8, 8), 8), :] = jnp.broadcast_to(centre, (8, 128))
        feats, norm = rows_side(4.0 * (here - centre))
        fs[cols(j), :] = feats.T.astype(BF16)
        low = jnp.where(lane128 == j, lo, low)
        top = jnp.where(lane128 == j, hi, top)
        return low, top, jnp.maximum(far, jnp.where(valid, norm, 0.0))

    start = (
        jnp.full((8, 128), FAR, F32),
        jnp.full((8, 128), -FAR, F32),
        jnp.zeros((1, PTS), F32),
    )
    low, top, far = lax.fori_loop(0, blocks, one, start, unroll=4 if blocks % 8 else 8)
    cen[pl.ds(blocks * 8, 8), :] = jnp.zeros((8, 128), F32)
    fs[pl.ds(blocks * PTS, PTS), :] = jnp.zeros((PTS, KF), BF16)
    wide = jnp.max(far, axis=1, keepdims=True) > 16.0 * ROOM
    return low, top, jnp.where(wide, 1, 0)


def square(v):
    return jnp.concatenate([v, jnp.zeros((120, 128), F32)], axis=0).T


def near(low_i, top_i, low_j, top_j):
    low_t, top_t = square(low_i), square(top_i)
    gap2 = jnp.zeros((128, 128), F32)
    for k in range(3):
        gap = jnp.maximum(
            low_j[k : k + 1] - top_t[:, k : k + 1], low_t[:, k : k + 1] - top_j[k : k + 1]
        )
        gap = jnp.maximum(gap, 0.0)
        gap2 = gap2 + gap * gap
    return gap2 <= 1.001


def as_rows(last):
    last = jnp.max(last.astype(F32), axis=1, keepdims=True)
    return jnp.broadcast_to(last, (128, 128)).T[:8].astype(jnp.int32)


def to_scalars(values, tab_v, tab_s, sem):
    tab_v[...] = values
    copy = pltpu.make_async_copy(tab_v, tab_s, sem)
    copy.start()
    copy.wait()


def sweep(first, end, begin, stop, spare, spread, side_i, side_j, acc_i, acc_j, bufs):
    pc_i, db_i = side_i
    pc_j, db_j, fs_j, cen_j = side_j
    depth = len(bufs)
    zero = jnp.int32(0)

    def enter(i):
        i = jnp.where(i >= end, spare[0], i)
        return i, jnp.where(i == spare[0], spare[1], begin(i))

    def following(i, j):
        n = j + 1
        over = (n >= stop(i)) | (i == spare[0])
        i2, j2 = enter(i + 1)
        return jnp.where(over, i2, i), jnp.where(over, j2, n)

    def squares(i, j, out):
        c = cen_j[pl.ds(pl.multiple_of(j * 8, 8), 8), :]
        f = weights_side(4.0 * (pc_i[:, cols(i)] - jnp.concatenate([c, c], axis=1)))
        out[...] = mm(fs_j[cols(j), :], f)

    same = db_i is db_j

    def products(i, j, tile):
        other = mm_t(db_i[:, cols(i)], tile)
        if same:
            other = other * jnp.where(j > i, 1.0, 0.0)
        return i, j, mm(db_j[:, cols(j)], tile), other

    def add(i, j, mine, other):
        acc_i[:, cols(i)] += mine
        acc_j[:, cols(j)] += other

    total = lax.fori_loop(first, end, lambda i, n: n + stop(i) - begin(i), zero)
    queue = [enter(jnp.int32(first))]
    for _ in range(depth - 1):
        queue.append(following(*queue[-1]))

    @pl.when(spread == 0)
    def _():
        for k in range(depth - 1):
            squares(*queue[k], bufs[k])

        def turn(units):
            def one(_, carry):
                q = list(carry)
                waiting = None
                for g in range(units):
                    squares(*q[-1], bufs[(g + depth - 1) % depth])
                    done = products(*q[0], tile_of(bufs[g % depth][...]))
                    if waiting is not None:
                        add(*waiting)
                    waiting = done
                    q = q[1:] + [following(*q[-1])]
                add(*waiting)
                return tuple(q)

            return one

        state = lax.fori_loop(0, total // LONG, turn(LONG), tuple(queue))
        left = total - (total // LONG) * LONG
        lax.fori_loop(0, (left + depth - 1) // depth, turn(depth), state)

    @pl.when(spread != 0)
    def _():
        def one(_, carry):
            i, j = carry
            pj = pc_j[:, cols(j)].T
            pi = pc_i[:, cols(i)]
            for h in range(0, PTS, 64):
                s = jnp.zeros((64, PTS), F32)
                for k in range(3):
                    d = 4.0 * (pj[h : h + 64, k : k + 1] - pi[k : k + 1, :])
                    s = s + d * d
                bufs[0][pl.ds(h, 64), :] = s
            add(*products(i, j, tile_of(bufs[0][...])))
            return following(i, j)

        lax.fori_loop(0, total, one, queue[0])


def strips_of(cells, cnt):
    return (lax.fori_loop(0, cells, lambda c, n: n + cnt[c], jnp.int32(0)) + (PTS - 1)) // PTS


def fetch(pairs, sems):
    copies = [pltpu.make_async_copy(src, dst, sems.at[k]) for k, (src, dst) in enumerate(pairs)]
    for copy in copies:
        copy.start()
    return copies


def head_kernel(cells, cnt_h, pts_h, dirs_h, db, pc, fs, cen, box, tab, cnt, pts, dirs, off, dc, sem):
    copies = fetch(((cnt_h, cnt), (pts_h, pts), (dirs_h, dirs)), sem)
    dc[...] = jnp.zeros_like(dc)
    pc[...] = jnp.zeros_like(pc)
    for copy in copies:
        copy.wait()
    own_end = pack(cells, cnt, off, dirs, pts, dc, pc)
    db[...] = dc[...].astype(BF16)
    low, top, spread = prepare(cells, pc, own_end, cen, fs)
    box[0:8, :] = low
    box[8:16, :] = top
    ri = lax.broadcasted_iota(jnp.int32, (128, 128), 0)
    rj = lax.broadcasted_iota(jnp.int32, (128, 128), 1)
    need = near(low, top, low, top) & (rj > ri)
    stop = as_rows(jnp.where(need, rj + 1, ri + 1))
    lane128 = lax.broadcasted_iota(jnp.int32, (1, 128), 1)
    tab[...] = jnp.where(lane128 == 127, spread, stop)


def edge_kernel(cells, halo_cells, cnt, db, pc, box, tab, piece, halo, acc_i, hdb, hfs, hcen, tab_v, *rest):
    *bufs, tab_s, sem = rest
    strips = strips_of(cells, cnt)
    acc_i[...] = jnp.zeros_like(acc_i)
    halo[...] = jnp.zeros_like(halo)
    rhs = hdb.shape[0]
    hdb[:, : halo_cells * PTS] = piece[:rhs, :].astype(BF16)
    hdb[:, halo_cells * PTS :] = jnp.zeros((rhs, PTS), BF16)
    hpc = piece.at[rhs : rhs + 8]
    low, top, spread = prepare(halo_cells, hpc, halo_cells * PTS, hcen, hfs)
    ri = lax.broadcasted_iota(jnp.int32, (128, 128), 0)
    rj = lax.broadcasted_iota(jnp.int32, (128, 128), 1)
    need = near(box[0:8, :], box[8:16, :], low, top) & (rj < halo_cells) & (ri < cells)
    stop = as_rows(jnp.where(need, rj + 1, 0))
    lane128 = lax.broadcasted_iota(jnp.int32, (1, 128), 1)
    first = jnp.min(jnp.where(need, ri, 127).astype(F32), axis=(0, 1), keepdims=True)
    stop = jnp.where(lane128 == 126, first.astype(jnp.int32), stop)
    wide = jnp.where((tab[...] != 0) & (lane128 == 127), 1, 0)
    to_scalars(jnp.where(lane128 == 127, spread + wide, stop), tab_v, tab_s, sem)
    sweep(
        jnp.minimum(tab_s[0, 126], strips), strips, lambda i: jnp.int32(0),
        lambda i: jnp.maximum(tab_s[0, i], 1), (cells, halo_cells), tab_s[0, 127],
        (pc, db), (hpc, hdb, hfs, hcen), acc_i, halo, bufs,
    )
    halo[:, : halo_cells * PTS] = halo[:, : halo_cells * PTS] * (1.0 / 256.0)


def tail_kernel(cells, cnt, db, pc, fs, cen, tab, acc_e, own, off, acc_i, acc_j, *rest):
    bufs = rest
    lane1 = lax.broadcasted_iota(jnp.int32, (1, PTS), 1)
    acc_i[...] = acc_e[...]
    acc_j[...] = jnp.zeros_like(acc_j)

    def place(c, at):
        off[c] = at
        return at + cnt[c]

    end = lax.fori_loop(0, cells, place, jnp.int32(0))
    strips = (end + (PTS - 1)) // PTS
    side = (pc, db, fs, cen)
    sweep(
        0, strips, lambda i: i, lambda i: tab[0, i], (cells, cells), tab[0, 127],
        side[:2], side, acc_i, acc_j, bufs,
    )

    def take(c, _):
        at = off[c]
        base = pl.multiple_of((at // 128) * 128, 128)
        both = acc_i[:, pl.ds(base, 384)] + acc_j[:, pl.ds(base, 384)]
        back = pltpu.roll(both, 384 - at % 128, 1)[:, :PTS] * (1.0 / 256.0)
        own[:, cols(c)] = jnp.where(lane1 < cnt[c], back, 0.0)
        return 0

    lax.fori_loop(0, cells, take, 0, unroll=4)


def piece_kernel(cells, cnt_h, pts_h, dirs_h, piece, cnt, pts, dirs, sem):
    rhs = dirs.shape[0]
    span = pl.ds(0, cells * PTS)
    copies = fetch(((cnt_h, cnt), (pts_h.at[:, span], pts), (dirs_h.at[:, span], dirs)), sem)
    lane1 = lax.broadcasted_iota(jnp.int32, (1, PTS), 1)
    piece[rhs:, :] = jnp.zeros_like(piece[rhs:, :])
    for copy in copies:
        copy.wait()
    for c in range(cells):
        at = slice(c * PTS, (c + 1) * PTS)
        live = lane1 < cnt[c]
        piece[:rhs, at] = jnp.where(live, dirs[:, at], 0.0)
        piece[rhs : rhs + 3, at] = jnp.where(live, pts[:, at], pts[:, c * PTS : c * PTS + 1])


VM = pl.BlockSpec(memory_space=pltpu.VMEM)
SM = pl.BlockSpec(memory_space=pltpu.SMEM)
HB = pl.BlockSpec(memory_space=pltpu.MemorySpace.HBM)
LONG = 16
DEPTH = 4


def params(mib):
    return pltpu.CompilerParams(vmem_limit_bytes=mib << 20)


def buffers():
    return [pltpu.VMEM((PTS, PTS), F32)] * DEPTH


def cost(units):
    return pl.CostEstimate(flops=units * 60_000_000, bytes_accessed=4_000_000, transcendentals=units * 65536)


def pair_products(counts, points, direction):
    cells = counts.shape[0]
    rhs = direction.shape[0]
    width = min(cells, REACH)
    blocks = cells + 1
    wide = blocks * PTS + 256
    shape = jax.ShapeDtypeStruct

    held = [pltpu.with_memory_space_constraint(x, pltpu.MemorySpace.HBM) for x in (counts, points, direction)]
    piece = pl.pallas_call(
        lambda *refs: piece_kernel(width, *refs),
        name="piece",
        out_shape=shape((rhs + 8, width * PTS), F32),
        in_specs=[HB] * 3,
        out_specs=VM,
        scratch_shapes=[
            pltpu.SMEM((cells,), jnp.int32),
            pltpu.VMEM((3, width * PTS), F32),
            pltpu.VMEM((rhs, width * PTS), F32),
            pltpu.SemaphoreType.DMA((3,)),
        ],
        compiler_params=params(8),
    )(*held)
    piece = passed_along(piece, -1)
    db, pc, fs, cen, box, tab = pl.pallas_call(
        lambda *refs: head_kernel(cells, *refs),
        name="head",
        out_shape=[
            shape((rhs, wide), BF16),
            shape((8, wide), F32),
            shape((blocks * PTS, KF), BF16),
            shape((blocks * 8, 128), F32),
            shape((16, 128), F32),
            shape((8, 128), jnp.int32),
        ],
        in_specs=[HB] * 3,
        out_specs=[VM] * 6,
        scratch_shapes=[
            pltpu.SMEM((cells,), jnp.int32),
            pltpu.VMEM(points.shape, F32),
            pltpu.VMEM(direction.shape, F32),
            pltpu.SMEM((cells,), jnp.int32),
            pltpu.VMEM((rhs, wide), F32),
            pltpu.SemaphoreType.DMA((3,)),
        ],
        compiler_params=params(12),
        cost_estimate=cost(100),
    )(*held)
    halo, acc_e = pl.pallas_call(
        lambda *refs: edge_kernel(cells, width, *refs),
        name="edge",
        out_shape=[shape((rhs, (width + 1) * PTS), F32), shape((rhs, wide), F32)],
        in_specs=[SM] + [VM] * 5,
        out_specs=[VM] * 2,
        scratch_shapes=[
            pltpu.VMEM((rhs, (width + 1) * PTS), BF16),
            pltpu.VMEM(((width + 1) * PTS, KF), BF16),
            pltpu.VMEM(((width + 1) * 8, 128), F32),
            pltpu.VMEM((8, 128), jnp.int32),
        ]
        + buffers()
        + [pltpu.SMEM((8, 128), jnp.int32), pltpu.SemaphoreType.DMA],
        compiler_params=params(12),
        cost_estimate=cost(70),
    )(counts, db, pc, box, tab, piece)
    back = passed_along(halo, 1)
    own = pl.pallas_call(
        lambda *refs: tail_kernel(cells, *refs),
        name="tail",
        out_shape=shape((rhs, cells * PTS), F32),
        in_specs=[SM] + [VM] * 4 + [SM, VM],
        out_specs=VM,
        scratch_shapes=[
            pltpu.SMEM((cells,), jnp.int32),
            pltpu.VMEM((rhs, wide), F32),
            pltpu.VMEM((rhs, wide), F32),
        ]
        + buffers(),
        compiler_params=params(12),
        cost_estimate=cost(180),
    )(counts, db, pc, fs, cen, tab, acc_e)
    return own, back


def sums_kernel(cnt, own, back, nug, dirs, res, ritz, image, sums):
    cells = own.shape[1] // PTS
    halo_cells = back.shape[1] // PTS - 1
    lane1 = lax.broadcasted_iota(jnp.int32, (1, PTS), 1)

    def of_cell(c, part, extra):
        live = lane1 < cnt[c]
        d = jnp.where(live, dirs[:, cols(c)], 0.0)
        r = jnp.where(live, res[:, cols(c)], 0.0)
        k = own[:, cols(c)]
        if extra:
            k = k + back[:, cols(c)]
        im = jnp.where(live, nug[:, cols(c)] * d + k, 0.0)
        image[:, cols(c)] = im
        dk, rr, ri, ii, prod = part
        both = jnp.concatenate([r, im], axis=0)
        bh = high(both)
        z = ritz[:, cols(c)]
        zh = high(z)
        left = jnp.concatenate([bh, both - bh], axis=0).astype(BF16)
        right = jnp.concatenate([zh, z - zh], axis=0).astype(BF16)
        return dk + d * im, rr + r * r, ri + r * im, ii + im * im, prod + mm_t(left, right)

    rhs = own.shape[0]
    zero = jnp.zeros((rhs, PTS), F32)
    part = (zero, zero, zero, zero, jnp.zeros((4 * rhs, 2 * ritz.shape[0]), F32))
    part = lax.fori_loop(0, halo_cells, lambda c, p: of_cell(c, p, True), part, unroll=6)
    part = lax.fori_loop(halo_cells, cells, lambda c, p: of_cell(c, p, False), part, unroll=5)
    dots = [jnp.sum(p, axis=1, keepdims=True) for p in part[:4]]
    prod = part[4]
    n = ritz.shape[0]
    h = 2 * rhs
    prod = prod[:h, :n] + prod[:h, n:] + prod[h:, :n]
    sums[...] = jnp.zeros_like(sums)
    sums[:, :n] = prod[:rhs]
    sums[:, n : 2 * n] = prod[rhs:]
    for k in range(4):
        sums[:, 2 * n + k : 2 * n + k + 1] = dots[k]


def local_sums(counts, own, back, nugget, direction, residual, ritz_image):
    return pl.pallas_call(
        sums_kernel,
        name="sums",
        out_shape=[
            jax.ShapeDtypeStruct(own.shape, F32),
            jax.ShapeDtypeStruct((own.shape[0], 128), F32),
        ],
        in_specs=[SM] + [VM] * 6,
        out_specs=[VM, VM],
        compiler_params=params(12),
    )(counts, own, back, nugget, direction, residual, ritz_image)


def finish_kernel(
    cnt, sums, gram, image, dirs, res, sol, basis, sol_h, res_h, dir_h, sol_out, res_out, dir_out, sem
):
    cells = image.shape[1] // PTS
    n = gram.shape[0]
    lane1 = lax.broadcasted_iota(jnp.int32, (1, PTS), 1)
    curvature, rr, ri, ii = (sums[:, 2 * n + k : 2 * n + k + 1] for k in range(4))
    step = rr / curvature
    growth = (rr + step * (step * ii - 2.0 * ri)) / rr
    projected = sums[:, :n] - step * sums[:, n : 2 * n]
    ph = high(projected)
    g = gram[...]
    gh = high(g)
    coef = mm_t(
        jnp.concatenate([ph, ph, projected - ph], axis=1).astype(BF16),
        jnp.concatenate([gh, g - gh, gh], axis=1).astype(BF16),
    )
    ch = high(coef)
    left = jnp.concatenate([ch, ch, coef - ch], axis=1).astype(BF16)

    def of_cell(c, _):
        live = lane1 < cnt[c]
        d = jnp.where(live, dirs[:, cols(c)], 0.0)
        r = jnp.where(live, res[:, cols(c)], 0.0)
        s = jnp.where(live, sol[:, cols(c)], 0.0)
        b = basis[:, cols(c)]
        bh = high(b)
        right = jnp.concatenate([bh, b - bh, bh], axis=0).astype(BF16)
        new = r - step * image[:, cols(c)]
        sol_out[:, cols(c)] = s + step * d
        res_out[:, cols(c)] = new
        dir_out[:, cols(c)] = jnp.where(live, growth * d + new - mm(left, right), 0.0)
        return 0

    pieces = 4
    many = cells // pieces
    copies = []
    for k in range(pieces):
        lax.fori_loop(k * many, (k + 1) * many, of_cell, 0, unroll=8)
        at = pl.ds(k * many * PTS, many * PTS)
        for n, (src, dst) in enumerate(((sol_out, sol_h), (res_out, res_h), (dir_out, dir_h))):
            copies.append(pltpu.make_async_copy(src.at[:, at], dst.at[:, at], sem.at[3 * k + n]))
            copies[-1].start()
    for copy in copies:
        copy.wait()


def finish(counts, sums, gram, image, direction, residual, solution, basis):
    return pl.pallas_call(
        finish_kernel,
        name="finish",
        out_shape=[jax.ShapeDtypeStruct(image.shape, F32)] * 3,
        in_specs=[SM] + [VM] * 7,
        out_specs=[HB] * 3,
        scratch_shapes=[pltpu.VMEM(image.shape, F32)] * 3 + [pltpu.SemaphoreType.DMA((12,))],
        compiler_params=params(12),
    )(counts, sums, gram, image, direction, residual, solution, basis)


def passed_along(array, by):
    length = lax.axis_size(AXES)
    pairs = [(i, i + by) for i in range(length) if 0 <= i + by < length]
    return lax.ppermute(array, AXES, pairs)


def groups_of(length, bits):
    others = [i for i in range(length) if not any(i >> b & 1 for b in bits)]
    spread = [sum((m >> k & 1) << b for k, b in enumerate(bits)) for m in range(1 << len(bits))]
    return [[i + s for s in spread] for i in others]


def summed(array):
    length = lax.axis_size(AXES)
    array = array + lax.ppermute(array, AXES, [(i, i ^ 1) for i in range(length)])
    for bits in ((1, 2, 3, 4), (5, 6, 7)):
        copies = jnp.broadcast_to(array[None], (1 << len(bits),) + array.shape)
        parts = lax.all_to_all(copies, AXES, 0, 0, axis_index_groups=groups_of(length, bits))
        array = jnp.sum(parts, axis=0)
    return array


def local(
    points,
    cell_counts,
    pair_cells,
    pair_counts,
    nugget,
    solution,
    residual,
    direction,
    ritz_basis,
    ritz_image,
    inverse_gram,
):
    own, back = pair_products(cell_counts, points, direction)
    image, sums = local_sums(
        cell_counts, own, back, nugget.reshape(1, -1), direction, residual, ritz_image
    )
    return tuple(
        finish(
            cell_counts,
            summed(sums),
            inverse_gram,
            image,
            direction,
            residual,
            solution,
            ritz_basis,
        )
    )


def solution(mesh):
    split = P(None, AXES)
    line = P(AXES)
    in_specs = (split, line, split, line, line, split, split, split, split, split, P())
    return jax.shard_map(
        local, mesh=mesh, in_specs=in_specs, out_specs=(split,) * 3, check_vma=False
    )
```

```python
import jax
import jax.numpy as jnp
from jax import lax
from jax.experimental import pallas as pl
from jax.experimental.pallas import tpu as pltpu
from jax.sharding import PartitionSpec as P

PTS = 256
REACH = 12
KF = 48
FAR = 1e18
ROOM = 16.0
AXES = ("region", "cell")
F32 = jnp.float32
BF16 = jnp.bfloat16


def mm(x, y):
    return lax.dot_general(x, y, (((1,), (0,)), ((), ())), preferred_element_type=F32)


def mm_t(x, y):
    return lax.dot_general(x, y, (((1,), (1,)), ((), ())), preferred_element_type=F32)


def high(x):
    return x.astype(BF16).astype(F32)


def split3(x):
    h = high(x)
    m = high(x - h)
    return h, m, high(x - h - m)


def tile_of(scaled_square):
    s = jnp.maximum(scaled_square, 1e-30)
    t = s * lax.rsqrt(s)
    u = jnp.maximum(4.0 - t, 0.0)
    u2 = u * u
    return ((u2 * u2) * (t + 1.0)).astype(BF16)


def cols(block, size=PTS):
    return pl.ds(pl.multiple_of(block * size, size), size)


def with_norm(vec):
    row = lax.broadcasted_iota(jnp.int32, vec.shape, 0)
    return row, jnp.sum(vec * vec, axis=0, keepdims=True)


def weights_side(p):
    row, norm = with_norm(p)
    a = jnp.where(row == 3, norm, -2.0 * p)
    h, m, l = split3(a)
    one_h = jnp.where(row == 3, 1.0, h)
    one_m = jnp.where(row == 3, 1.0, m)
    return jnp.concatenate([h, m, one_h, one_m, l, one_h], axis=0).astype(BF16)


def rows_side(q):
    row, norm = with_norm(q)
    a = jnp.where(row == 3, norm, q)
    h, m, l = split3(a)
    one = jnp.where(row == 3, 1.0, h)
    mid_h = jnp.where(row == 3, h, m)
    return jnp.concatenate([one, one, mid_h, m, one, l], axis=0), norm


def pack(cells, cnt, off, dirs, pts, dc, pc):
    lane1 = lax.broadcasted_iota(jnp.int32, (1, PTS), 1)
    lane128 = lax.broadcasted_iota(jnp.int32, (1, 128), 1)

    def place(c, at):
        off[c] = at
        shift = at % 128
        base = pl.multiple_of((at // 128) * 128, 128)
        live = lane1 < cnt[c]
        dv = jnp.where(live, dirs[:, cols(c)], 0.0)
        pv = jnp.where(live, pts[:, cols(c)], 0.0)
        for ref, val in ((dc, dv), (pc, pv)):
            rows = val.shape[0]
            wide = jnp.concatenate([val, jnp.zeros((rows, 128), F32)], axis=1)
            wide = pltpu.roll(wide, shift, 1)
            old = ref[:rows, pl.ds(base, 128)]
            ref[:rows, pl.ds(base, 128)] = jnp.where(lane128 < shift, old, wide[:, :128])
            ref[:rows, pl.ds(base + 128, 256)] = wide[:, 128:]
        return at + cnt[c]

    return lax.fori_loop(0, cells, place, jnp.int32(0), unroll=8)


def prepare(blocks, pc, end, cen, fs):
    lane1 = lax.broadcasted_iota(jnp.int32, (1, PTS), 1)
    lane128 = lax.broadcasted_iota(jnp.int32, (1, 128), 1)

    def one(j, carry):
        low, top, far = carry
        here = pc[:, cols(j)]
        valid = j * PTS + lane1 < end
        lo = jnp.min(jnp.where(valid, here, FAR), axis=1, keepdims=True)
        hi = jnp.max(jnp.where(valid, here, -FAR), axis=1, keepdims=True)
        centre = jnp.where(lo <= hi, 0.5 * (lo + hi), 0.0)
        cen[pl.ds(pl.multiple_of(j * 8, 8), 8), :] = jnp.broadcast_to(centre, (8, 128))
        feats, norm = rows_side(4.0 * (here - centre))
        fs[cols(j), :] = feats.T.astype(BF16)
        low = jnp.where(lane128 == j, lo, low)
        top = jnp.where(lane128 == j, hi, top)
        return low, top, jnp.maximum(far, jnp.where(valid, norm, 0.0))

    start = (
        jnp.full((8, 128), FAR, F32),
        jnp.full((8, 128), -FAR, F32),
        jnp.zeros((1, PTS), F32),
    )
    low, top, far = lax.fori_loop(0, blocks, one, start, unroll=12 if blocks % 12 == 0 else 8)
    cen[pl.ds(blocks * 8, 8), :] = jnp.zeros((8, 128), F32)
    fs[pl.ds(blocks * PTS, PTS), :] = jnp.zeros((PTS, KF), BF16)
    wide = jnp.max(far, axis=1, keepdims=True) > 16.0 * ROOM
    return low, top, jnp.where(wide, 1, 0)


def square(v):
    return jnp.concatenate([v, jnp.zeros((120, 128), F32)], axis=0).T


def near(low_i, top_i, low_j, top_j):
    low_t, top_t = square(low_i), square(top_i)
    gap2 = jnp.zeros((128, 128), F32)
    for k in range(3):
        gap = jnp.maximum(
            low_j[k : k + 1] - top_t[:, k : k + 1], low_t[:, k : k + 1] - top_j[k : k + 1]
        )
        gap = jnp.maximum(gap, 0.0)
        gap2 = gap2 + gap * gap
    return gap2 <= 1.001


def as_rows(last):
    last = jnp.max(last.astype(F32), axis=1, keepdims=True)
    return jnp.broadcast_to(last, (128, 128)).T[:8].astype(jnp.int32)


def lanes_sum(values):
    return jnp.sum(values.astype(F32), axis=1, keepdims=True).astype(jnp.int32)


def to_scalars(values, tab_v, tab_s, sem):
    tab_v[...] = values
    copy = pltpu.make_async_copy(tab_v, tab_s, sem)
    copy.start()
    copy.wait()


def sweep(first, end, begin, stop, total, spare, spread, side_i, side_j, acc_i, acc_j, bufs):
    pc_i, db_i = side_i
    pc_j, db_j, fs_j, cen_j = side_j
    depth = len(bufs)
    def enter(i):
        i = jnp.where(i >= end, spare[0], i)
        return i, jnp.where(i == spare[0], spare[1], begin(i))

    def following(i, j):
        n = j + 1
        over = (n >= stop(i)) | (i == spare[0])
        i2, j2 = enter(i + 1)
        return jnp.where(over, i2, i), jnp.where(over, j2, n)

    def squares(i, j, out):
        c = cen_j[pl.ds(pl.multiple_of(j * 8, 8), 8), :]
        f = weights_side(4.0 * (pc_i[:, cols(i)] - jnp.concatenate([c, c], axis=1)))
        out[...] = mm(fs_j[cols(j), :], f)

    same = db_i is db_j

    def products(i, j, tile):
        other = mm_t(db_i[:, cols(i)], tile)
        if same:
            other = other * jnp.where(j > i, 1.0, 0.0)
        return i, j, mm(db_j[:, cols(j)], tile), other

    def add(i, j, mine, other):
        acc_i[:, cols(i)] += mine
        acc_j[:, cols(j)] += other

    queue = [enter(first)]
    for _ in range(depth - 1):
        queue.append(following(*queue[-1]))

    @pl.when(spread == 0)
    def _():
        for k in range(depth - 1):
            squares(*queue[k], bufs[k])

        def turn(units):
            def one(_, carry):
                q = list(carry)
                waiting = None
                for g in range(units):
                    squares(*q[-1], bufs[(g + depth - 1) % depth])
                    done = products(*q[0], tile_of(bufs[g % depth][...]))
                    if waiting is not None:
                        add(*waiting)
                    waiting = done
                    q = q[1:] + [following(*q[-1])]
                add(*waiting)
                return tuple(q)

            return one

        state = lax.fori_loop(0, total // LONG, turn(LONG), tuple(queue))
        left = total - (total // LONG) * LONG
        lax.fori_loop(0, (left + depth - 1) // depth, turn(depth), state)

    @pl.when(spread != 0)
    def _():
        def one(_, carry):
            i, j = carry
            pj = pc_j[:, cols(j)].T
            pi = pc_i[:, cols(i)]
            for h in range(0, PTS, 64):
                s = jnp.zeros((64, PTS), F32)
                for k in range(3):
                    d = 4.0 * (pj[h : h + 64, k : k + 1] - pi[k : k + 1, :])
                    s = s + d * d
                bufs[0][pl.ds(h, 64), :] = s
            add(*products(i, j, tile_of(bufs[0][...])))
            return following(i, j)

        lax.fori_loop(0, total, one, queue[0])


def fetch(pairs, sems):
    copies = [pltpu.make_async_copy(src, dst, sems.at[k]) for k, (src, dst) in enumerate(pairs)]
    for copy in copies:
        copy.start()
    return copies


def head_kernel(cells, cnt_h, pts_h, dirs_h, db, pc, fs, cen, box, tab, off, cnt, pts, dirs, dc, sem):
    copies = fetch(((cnt_h, cnt), (pts_h, pts), (dirs_h, dirs)), sem)
    dc[...] = jnp.zeros_like(dc)
    pc[...] = jnp.zeros_like(pc)
    for copy in copies:
        copy.wait()
    own_end = pack(cells, cnt, off, dirs, pts, dc, pc)
    db[...] = dc[...].astype(BF16)
    low, top, spread = prepare(cells, pc, own_end, cen, fs)
    box[0:8, :] = low
    box[8:16, :] = top
    ri = lax.broadcasted_iota(jnp.int32, (128, 128), 0)
    rj = lax.broadcasted_iota(jnp.int32, (128, 128), 1)
    need = near(low, top, low, top) & (rj > ri)
    stop = as_rows(jnp.where(need, rj + 1, ri + 1))
    lane128 = lax.broadcasted_iota(jnp.int32, (1, 128), 1)
    strips = (own_end + (PTS - 1)) // PTS
    total = lanes_sum(jnp.where(lane128 < strips, stop - lane128, 0))
    stop = jnp.where(lane128 == 125, strips, jnp.where(lane128 == 126, total, stop))
    tab[...] = jnp.where(lane128 == 127, spread, stop)


def edge_kernel(cells, halo_cells, db, pc, box, tab, piece, halo, acc_i, hdb, hfs, hcen, tab_v, *rest):
    *bufs, tab_s, sem = rest
    strips = tab[0, 125]
    acc_i[...] = jnp.zeros_like(acc_i)
    halo[...] = jnp.zeros_like(halo)
    rhs = hdb.shape[0]
    hdb[:, : halo_cells * PTS] = piece[:rhs, :].astype(BF16)
    hdb[:, halo_cells * PTS :] = jnp.zeros((rhs, PTS), BF16)
    hpc = piece.at[rhs : rhs + 8]
    low, top, spread = prepare(halo_cells, hpc, halo_cells * PTS, hcen, hfs)
    ri = lax.broadcasted_iota(jnp.int32, (128, 128), 0)
    rj = lax.broadcasted_iota(jnp.int32, (128, 128), 1)
    need = near(box[0:8, :], box[8:16, :], low, top) & (rj < halo_cells) & (ri < cells)
    stop = as_rows(jnp.where(need, rj + 1, 0))
    lane128 = lax.broadcasted_iota(jnp.int32, (1, 128), 1)
    first = jnp.min(jnp.where(need, ri, 127).astype(F32), axis=(0, 1), keepdims=True)
    first = jnp.minimum(first.astype(jnp.int32), strips)
    stop = jnp.maximum(stop, 1)
    total = lanes_sum(jnp.where((lane128 >= first) & (lane128 < strips), stop, 0))
    stop = jnp.where(lane128 == 125, total, jnp.where(lane128 == 126, first, stop))
    to_scalars(jnp.where(lane128 == 127, spread + tab[0, 127], stop), tab_v, tab_s, sem)
    sweep(
        tab_s[0, 126], strips, lambda i: jnp.int32(0), lambda i: tab_s[0, i], tab_s[0, 125],
        (cells, halo_cells), tab_s[0, 127],
        (pc, db), (hpc, hdb, hfs, hcen), acc_i, halo, bufs,
    )
    halo[:, : halo_cells * PTS] = halo[:, : halo_cells * PTS] * (1.0 / 256.0)


def tail_kernel(cells, cnt, off, db, pc, fs, cen, tab, acc_e, own, acc_i, acc_j, *bufs):
    lane1 = lax.broadcasted_iota(jnp.int32, (1, PTS), 1)
    acc_i[...] = acc_e[...]
    acc_j[...] = jnp.zeros_like(acc_j)
    side = (pc, db, fs, cen)
    sweep(
        jnp.int32(0), tab[0, 125], lambda i: i, lambda i: tab[0, i], tab[0, 126],
        (cells, cells), tab[0, 127],
        side[:2], side, acc_i, acc_j, bufs,
    )

    def take(c, _):
        at = off[c]
        base = pl.multiple_of((at // 128) * 128, 128)
        both = acc_i[:, pl.ds(base, 384)] + acc_j[:, pl.ds(base, 384)]
        back = pltpu.roll(both, 384 - at % 128, 1)[:, :PTS] * (1.0 / 256.0)
        own[:, cols(c)] = jnp.where(lane1 < cnt[c], back, 0.0)
        return 0

    lax.fori_loop(0, cells, take, 0, unroll=4)


def piece_kernel(cells, cnt_h, pts_h, dirs_h, piece, cnt, pts, dirs, sem):
    rhs = dirs.shape[0]
    span = pl.ds(0, cells * PTS)
    copies = fetch(((cnt_h, cnt), (pts_h.at[:, span], pts), (dirs_h.at[:, span], dirs)), sem)
    lane1 = lax.broadcasted_iota(jnp.int32, (1, PTS), 1)
    piece[rhs:, :] = jnp.zeros_like(piece[rhs:, :])
    for copy in copies:
        copy.wait()
    for c in range(cells):
        at = slice(c * PTS, (c + 1) * PTS)
        live = lane1 < cnt[c]
        piece[:rhs, at] = jnp.where(live, dirs[:, at], 0.0)
        piece[rhs : rhs + 3, at] = jnp.where(live, pts[:, at], pts[:, c * PTS : c * PTS + 1])


VM = pl.BlockSpec(memory_space=pltpu.VMEM)
SM = pl.BlockSpec(memory_space=pltpu.SMEM)
HB = pl.BlockSpec(memory_space=pltpu.MemorySpace.HBM)
LONG = 24
DEPTH = 4


def params(mib):
    return pltpu.CompilerParams(vmem_limit_bytes=mib << 20)


def buffers():
    return [pltpu.VMEM((PTS, PTS), F32)] * DEPTH


def cost(units):
    return pl.CostEstimate(flops=units * 60_000_000, bytes_accessed=4_000_000, transcendentals=units * 65536)


def pair_products(counts, points, direction):
    cells = counts.shape[0]
    rhs = direction.shape[0]
    width = min(cells, REACH)
    blocks = cells + 1
    wide = blocks * PTS + 256
    shape = jax.ShapeDtypeStruct

    held = [pltpu.with_memory_space_constraint(x, pltpu.MemorySpace.HBM) for x in (counts, points, direction)]
    piece = pl.pallas_call(
        lambda *refs: piece_kernel(width, *refs),
        name="piece",
        out_shape=shape((rhs + 8, width * PTS), F32),
        in_specs=[HB] * 3,
        out_specs=VM,
        scratch_shapes=[
            pltpu.SMEM((cells,), jnp.int32),
            pltpu.VMEM((3, width * PTS), F32),
            pltpu.VMEM((rhs, width * PTS), F32),
            pltpu.SemaphoreType.DMA((3,)),
        ],
        compiler_params=params(8),
    )(*held)
    piece = passed_along(piece, -1)
    db, pc, fs, cen, box, tab, off = pl.pallas_call(
        lambda *refs: head_kernel(cells, *refs),
        name="head",
        out_shape=[
            shape((rhs, wide), BF16),
            shape((8, wide), F32),
            shape((blocks * PTS, KF), BF16),
            shape((blocks * 8, 128), F32),
            shape((16, 128), F32),
            shape((8, 128), jnp.int32),
            shape((cells,), jnp.int32),
        ],
        in_specs=[HB] * 3,
        out_specs=[VM] * 6 + [SM],
        scratch_shapes=[
            pltpu.SMEM((cells,), jnp.int32),
            pltpu.VMEM(points.shape, F32),
            pltpu.VMEM(direction.shape, F32),
            pltpu.VMEM((rhs, wide), F32),
            pltpu.SemaphoreType.DMA((3,)),
        ],
        compiler_params=params(12),
        cost_estimate=cost(100),
    )(*held)
    halo, acc_e = pl.pallas_call(
        lambda *refs: edge_kernel(cells, width, *refs),
        name="edge",
        out_shape=[shape((rhs, (width + 1) * PTS), F32), shape((rhs, wide), F32)],
        in_specs=[VM] * 3 + [SM, VM],
        out_specs=[VM] * 2,
        scratch_shapes=[
            pltpu.VMEM((rhs, (width + 1) * PTS), BF16),
            pltpu.VMEM(((width + 1) * PTS, KF), BF16),
            pltpu.VMEM(((width + 1) * 8, 128), F32),
            pltpu.VMEM((8, 128), jnp.int32),
        ]
        + buffers()
        + [pltpu.SMEM((8, 128), jnp.int32), pltpu.SemaphoreType.DMA],
        compiler_params=params(12),
        cost_estimate=cost(70),
    )(db, pc, box, tab, piece)
    back = passed_along(halo, 1)
    own = pl.pallas_call(
        lambda *refs: tail_kernel(cells, *refs),
        name="tail",
        out_shape=shape((rhs, cells * PTS), F32),
        in_specs=[SM, SM] + [VM] * 4 + [SM, VM],
        out_specs=VM,
        scratch_shapes=[pltpu.VMEM((rhs, wide), F32)] * 2 + buffers(),
        compiler_params=params(12),
        cost_estimate=cost(180),
    )(counts, off, db, pc, fs, cen, tab, acc_e)
    return own, back


def sums_kernel(cnt, own, back, nug, dirs, res, ritz, image, sums):
    cells = own.shape[1] // PTS
    halo_cells = back.shape[1] // PTS - 1
    lane1 = lax.broadcasted_iota(jnp.int32, (1, PTS), 1)

    def of_cell(c, part, extra):
        live = lane1 < cnt[c]
        d = jnp.where(live, dirs[:, cols(c)], 0.0)
        r = jnp.where(live, res[:, cols(c)], 0.0)
        k = own[:, cols(c)]
        if extra:
            k = k + back[:, cols(c)]
        im = jnp.where(live, nug[:, cols(c)] * d + k, 0.0)
        image[:, cols(c)] = im
        dk, rr, ri, ii, prod = part
        both = jnp.concatenate([r, im], axis=0)
        bh = high(both)
        z = ritz[:, cols(c)]
        zh = high(z)
        left = jnp.concatenate([bh, both - bh], axis=0).astype(BF16)
        right = jnp.concatenate([zh, z - zh], axis=0).astype(BF16)
        return dk + d * im, rr + r * r, ri + r * im, ii + im * im, prod + mm_t(left, right)

    rhs = own.shape[0]
    zero = jnp.zeros((rhs, PTS), F32)
    part = (zero, zero, zero, zero, jnp.zeros((4 * rhs, 2 * ritz.shape[0]), F32))
    part = lax.fori_loop(0, halo_cells, lambda c, p: of_cell(c, p, True), part, unroll=6)
    part = lax.fori_loop(halo_cells, cells, lambda c, p: of_cell(c, p, False), part, unroll=5)
    dots = [jnp.sum(p, axis=1, keepdims=True) for p in part[:4]]
    prod = part[4]
    n = ritz.shape[0]
    h = 2 * rhs
    prod = prod[:h, :n] + prod[:h, n:] + prod[h:, :n]
    sums[...] = jnp.zeros_like(sums)
    sums[:, :n] = prod[:rhs]
    sums[:, n : 2 * n] = prod[rhs:]
    for k in range(4):
        sums[:, 2 * n + k : 2 * n + k + 1] = dots[k]


def local_sums(counts, own, back, nugget, direction, residual, ritz_image):
    return pl.pallas_call(
        sums_kernel,
        name="sums",
        out_shape=[
            jax.ShapeDtypeStruct(own.shape, F32),
            jax.ShapeDtypeStruct((own.shape[0], 128), F32),
        ],
        in_specs=[SM] + [VM] * 6,
        out_specs=[VM, VM],
        compiler_params=params(12),
    )(counts, own, back, nugget, direction, residual, ritz_image)


def finish_kernel(
    cnt, sums, gram, image, dirs, res, sol, basis, sol_h, res_h, dir_h, sol_out, res_out, dir_out, sem
):
    cells = image.shape[1] // PTS
    n = gram.shape[0]
    lane1 = lax.broadcasted_iota(jnp.int32, (1, PTS), 1)
    curvature, rr, ri, ii = (sums[:, 2 * n + k : 2 * n + k + 1] for k in range(4))
    step = rr / curvature
    growth = (rr + step * (step * ii - 2.0 * ri)) / rr
    projected = sums[:, :n] - step * sums[:, n : 2 * n]
    ph = high(projected)
    g = gram[...]
    gh = high(g)
    coef = mm_t(
        jnp.concatenate([ph, ph, projected - ph], axis=1).astype(BF16),
        jnp.concatenate([gh, g - gh, gh], axis=1).astype(BF16),
    )
    ch = high(coef)
    left = jnp.concatenate([ch, ch, coef - ch], axis=1).astype(BF16)

    def of_cell(c, _):
        live = lane1 < cnt[c]
        d = jnp.where(live, dirs[:, cols(c)], 0.0)
        r = jnp.where(live, res[:, cols(c)], 0.0)
        s = jnp.where(live, sol[:, cols(c)], 0.0)
        b = basis[:, cols(c)]
        bh = high(b)
        right = jnp.concatenate([bh, b - bh, bh], axis=0).astype(BF16)
        new = r - step * image[:, cols(c)]
        sol_out[:, cols(c)] = s + step * d
        res_out[:, cols(c)] = new
        dir_out[:, cols(c)] = jnp.where(live, growth * d + new - mm(left, right), 0.0)
        return 0

    pieces = 4
    many = cells // pieces
    copies = []
    for k in range(pieces):
        lax.fori_loop(k * many, (k + 1) * many, of_cell, 0, unroll=8)
        at = pl.ds(k * many * PTS, many * PTS)
        for n, (src, dst) in enumerate(((sol_out, sol_h), (res_out, res_h), (dir_out, dir_h))):
            copies.append(pltpu.make_async_copy(src.at[:, at], dst.at[:, at], sem.at[3 * k + n]))
            copies[-1].start()
    for copy in copies:
        copy.wait()


def finish(counts, sums, gram, image, direction, residual, solution, basis):
    return pl.pallas_call(
        finish_kernel,
        name="finish",
        out_shape=[jax.ShapeDtypeStruct(image.shape, F32)] * 3,
        in_specs=[SM] + [VM] * 7,
        out_specs=[HB] * 3,
        scratch_shapes=[pltpu.VMEM(image.shape, F32)] * 3 + [pltpu.SemaphoreType.DMA((12,))],
        compiler_params=params(12),
    )(counts, sums, gram, image, direction, residual, solution, basis)


def passed_along(array, by):
    length = lax.axis_size(AXES)
    pairs = [(i, i + by) for i in range(length) if 0 <= i + by < length]
    return lax.ppermute(array, AXES, pairs)


def groups_of(length, bits):
    others = [i for i in range(length) if not any(i >> b & 1 for b in bits)]
    spread = [sum((m >> k & 1) << b for k, b in enumerate(bits)) for m in range(1 << len(bits))]
    return [[i + s for s in spread] for i in others]


def summed(array):
    length = lax.axis_size(AXES)
    array = array + lax.ppermute(array, AXES, [(i, i ^ 1) for i in range(length)])
    for bits in ((1, 2, 3, 4), (5, 6, 7)):
        copies = jnp.broadcast_to(array[None], (1 << len(bits),) + array.shape)
        parts = lax.all_to_all(copies, AXES, 0, 0, axis_index_groups=groups_of(length, bits))
        array = jnp.sum(parts, axis=0)
    return array


def local(
    points,
    cell_counts,
    pair_cells,
    pair_counts,
    nugget,
    solution,
    residual,
    direction,
    ritz_basis,
    ritz_image,
    inverse_gram,
):
    own, back = pair_products(cell_counts, points, direction)
    image, sums = local_sums(
        cell_counts, own, back, nugget.reshape(1, -1), direction, residual, ritz_image
    )
    return tuple(
        finish(
            cell_counts,
            summed(sums),
            inverse_gram,
            image,
            direction,
            residual,
            solution,
            ritz_basis,
        )
    )


def solution(mesh):
    split = P(None, AXES)
    line = P(AXES)
    in_specs = (split, line, split, line, line, split, split, split, split, split, P())
    return jax.shard_map(
        local, mesh=mesh, in_specs=in_specs, out_specs=(split,) * 3, check_vma=False
    )
```

```python
import jax
import jax.numpy as jnp
from jax import lax
from jax.experimental import pallas as pl
from jax.experimental.pallas import tpu as pltpu
from jax.sharding import PartitionSpec as P

PTS = 256
REACH = 12
KF = 48
FAR = 1e18
ROOM = 16.0
AXES = ("region", "cell")
F32 = jnp.float32
BF16 = jnp.bfloat16


def mm(x, y):
    return lax.dot_general(x, y, (((1,), (0,)), ((), ())), preferred_element_type=F32)


def mm_t(x, y):
    return lax.dot_general(x, y, (((1,), (1,)), ((), ())), preferred_element_type=F32)


def high(x):
    return x.astype(BF16).astype(F32)


def split3(x):
    h = high(x)
    m = high(x - h)
    return h, m, x - h - m


def tile_of(scaled_square):
    s = jnp.maximum(scaled_square, 1e-30)
    t = s * lax.rsqrt(s)
    u = jnp.maximum(4.0 - t, 0.0)
    u2 = u * u
    return ((u2 * u2) * (t + 1.0)).astype(BF16)


def cols(block, size=PTS):
    return pl.ds(pl.multiple_of(block * size, size), size)


def with_norm(vec):
    row = lax.broadcasted_iota(jnp.int32, vec.shape, 0)
    return row, jnp.sum(vec * vec, axis=0, keepdims=True)


def weights_side(p):
    row, norm = with_norm(p)
    a = jnp.where(row == 3, norm, p)
    h, m, l = split3(a)
    one_h = jnp.where(row == 3, 1.0, h)
    one_m = jnp.where(row == 3, 1.0, m)
    return jnp.concatenate([h, m, one_h, one_m, l, one_h], axis=0).astype(BF16)


def rows_side(q):
    row, norm = with_norm(q)
    a = jnp.where(row == 3, norm, -2.0 * q)
    h, m, l = split3(a)
    one = jnp.where(row == 3, 1.0, h)
    mid_h = jnp.where(row == 3, h, m)
    return jnp.concatenate([one, one, mid_h, m, one, l], axis=0), norm


def pack(cells, cnt, off, dirs, pts, dc, pc):
    lane1 = lax.broadcasted_iota(jnp.int32, (1, PTS), 1)
    lane128 = lax.broadcasted_iota(jnp.int32, (1, 128), 1)

    def place(c, at):
        off[c] = at
        shift = at % 128
        base = pl.multiple_of((at // 128) * 128, 128)
        live = lane1 < cnt[c]
        dv = jnp.where(live, dirs[:, cols(c)], 0.0)
        pv = jnp.where(live, 4.0 * pts[:, cols(c)], 0.0)
        for ref, val in ((dc, dv), (pc, pv)):
            rows = val.shape[0]
            wide = jnp.concatenate([val, jnp.zeros((rows, 128), F32)], axis=1)
            wide = pltpu.roll(wide, shift, 1)
            old = ref[:rows, pl.ds(base, 128)]
            ref[:rows, pl.ds(base, 128)] = jnp.where(lane128 < shift, old, wide[:, :128])
            ref[:rows, pl.ds(base + 128, 256)] = wide[:, 128:]
        return at + cnt[c]

    return lax.fori_loop(0, cells, place, jnp.int32(0), unroll=8)


def prepare(blocks, pc, end, cen, fs):
    lane1 = lax.broadcasted_iota(jnp.int32, (1, PTS), 1)
    lane128 = lax.broadcasted_iota(jnp.int32, (1, 128), 1)

    def one(j, carry):
        low, top, far = carry
        here = pc[:, cols(j)]
        valid = j * PTS + lane1 < end
        lo = jnp.min(jnp.where(valid, here, FAR), axis=1, keepdims=True)
        hi = jnp.max(jnp.where(valid, here, -FAR), axis=1, keepdims=True)
        centre = jnp.where(lo <= hi, 0.5 * (lo + hi), 0.0)
        cen[pl.ds(pl.multiple_of(j * 8, 8), 8), :] = jnp.broadcast_to(centre, (8, 128))
        feats, norm = rows_side(here - centre)
        fs[cols(j), :] = feats.T.astype(BF16)
        low = jnp.where(lane128 == j, lo, low)
        top = jnp.where(lane128 == j, hi, top)
        return low, top, jnp.maximum(far, jnp.where(valid, norm, 0.0))

    start = (
        jnp.full((8, 128), FAR, F32),
        jnp.full((8, 128), -FAR, F32),
        jnp.zeros((1, PTS), F32),
    )
    low, top, far = lax.fori_loop(0, blocks, one, start, unroll=12 if blocks % 12 == 0 else 8)
    cen[pl.ds(blocks * 8, 8), :] = jnp.zeros((8, 128), F32)
    fs[pl.ds(blocks * PTS, PTS), :] = jnp.zeros((PTS, KF), BF16)
    wide = jnp.max(far, axis=1, keepdims=True) > 16.0 * ROOM
    return low, top, jnp.where(wide, 1, 0)


def square(v):
    return jnp.concatenate([v, jnp.zeros((120, 128), F32)], axis=0).T


def near(low_i, top_i, low_j, top_j):
    low_t, top_t = square(low_i), square(top_i)
    gap2 = jnp.zeros((128, 128), F32)
    for k in range(3):
        gap = jnp.maximum(
            low_j[k : k + 1] - top_t[:, k : k + 1], low_t[:, k : k + 1] - top_j[k : k + 1]
        )
        gap = jnp.maximum(gap, 0.0)
        gap2 = gap2 + gap * gap
    return gap2 <= 16.016


def as_rows(last):
    last = jnp.max(last.astype(F32), axis=1, keepdims=True)
    return jnp.broadcast_to(last, (128, 128)).T[:8].astype(jnp.int32)


def lanes_sum(values):
    return jnp.sum(values.astype(F32), axis=1, keepdims=True).astype(jnp.int32)


def to_scalars(values, tab_v, tab_s, sem):
    tab_v[...] = values
    copy = pltpu.make_async_copy(tab_v, tab_s, sem)
    copy.start()
    copy.wait()


def sweep(first, end, begin, stop, total, spare, spread, side_i, side_j, acc_i, acc_j, bufs):
    pc_i, db_i = side_i
    pc_j, db_j, fs_j, cen_j = side_j
    depth = len(bufs)
    def enter(i):
        i = jnp.where(i >= end, spare[0], i)
        return i, jnp.where(i == spare[0], spare[1], begin(i))

    def following(i, j):
        n = j + 1
        over = (n >= stop(i)) | (i == spare[0])
        i2, j2 = enter(i + 1)
        return jnp.where(over, i2, i), jnp.where(over, j2, n)

    def squares(i, j, out):
        c = cen_j[pl.ds(pl.multiple_of(j * 8, 8), 8), :]
        f = weights_side(pc_i[:, cols(i)] - jnp.concatenate([c, c], axis=1))
        out[...] = mm(fs_j[cols(j), :], f)

    same = db_i is db_j

    def products(i, j, tile):
        other = mm_t(db_i[:, cols(i)], tile)
        mine = mm(db_j[:, cols(j)], tile)
        return i, jnp.where(j > i, j, spare[1]) if same else j, mine, other

    def add(i, j, mine, other):
        acc_i[:, cols(i)] += mine
        acc_j[:, cols(j)] += other

    queue = [enter(first)]
    for _ in range(depth - 1):
        queue.append(following(*queue[-1]))

    @pl.when(spread == 0)
    def _():
        for k in range(depth - 1):
            squares(*queue[k], bufs[k])

        def turn(units):
            def one(_, carry):
                q = list(carry)
                waiting = None
                for g in range(units):
                    squares(*q[-1], bufs[(g + depth - 1) % depth])
                    done = products(*q[0], tile_of(bufs[g % depth][...]))
                    if waiting is not None:
                        add(*waiting)
                    waiting = done
                    q = q[1:] + [following(*q[-1])]
                add(*waiting)
                return tuple(q)

            return one

        state = lax.fori_loop(0, total // LONG, turn(LONG), tuple(queue))
        left = total - (total // LONG) * LONG
        lax.fori_loop(0, (left + depth - 1) // depth, turn(depth), state)

    @pl.when(spread != 0)
    def _():
        def one(_, carry):
            i, j = carry
            pj = pc_j[:, cols(j)].T
            pi = pc_i[:, cols(i)]
            for h in range(0, PTS, 64):
                s = jnp.zeros((64, PTS), F32)
                for k in range(3):
                    d = pj[h : h + 64, k : k + 1] - pi[k : k + 1, :]
                    s = s + d * d
                bufs[0][pl.ds(h, 64), :] = s
            add(*products(i, j, tile_of(bufs[0][...])))
            return following(i, j)

        lax.fori_loop(0, total, one, queue[0])


def fetch(pairs, sems):
    copies = [pltpu.make_async_copy(src, dst, sems.at[k]) for k, (src, dst) in enumerate(pairs)]
    for copy in copies:
        copy.start()
    return copies


def head_kernel(cells, cnt_h, pts_h, dirs_h, db, pc, fs, cen, box, tab, off, cnt, pts, dirs, dc, sem):
    copies = fetch(((cnt_h, cnt), (pts_h, pts), (dirs_h, dirs)), sem)
    dc[...] = jnp.zeros_like(dc)
    pc[...] = jnp.zeros_like(pc)
    for copy in copies:
        copy.wait()
    own_end = pack(cells, cnt, off, dirs, pts, dc, pc)
    db[...] = dc[...].astype(BF16)
    low, top, spread = prepare(cells, pc, own_end, cen, fs)
    box[0:8, :] = low
    box[8:16, :] = top
    ri = lax.broadcasted_iota(jnp.int32, (128, 128), 0)
    rj = lax.broadcasted_iota(jnp.int32, (128, 128), 1)
    need = near(low, top, low, top) & (rj > ri)
    stop = as_rows(jnp.where(need, rj + 1, ri + 1))
    lane128 = lax.broadcasted_iota(jnp.int32, (1, 128), 1)
    strips = (own_end + (PTS - 1)) // PTS
    total = lanes_sum(jnp.where(lane128 < strips, stop - lane128, 0))
    stop = jnp.where(lane128 == 125, strips, jnp.where(lane128 == 126, total, stop))
    tab[...] = jnp.where(lane128 == 127, spread, stop)


def edge_kernel(cells, halo_cells, db, pc, box, tab, piece, halo, acc_i, hdb, hfs, hcen, tab_v, *rest):
    *bufs, tab_s, sem = rest
    strips = tab[0, 125]
    acc_i[...] = jnp.zeros_like(acc_i)
    halo[...] = jnp.zeros_like(halo)
    rhs = hdb.shape[0]
    hdb[:, : halo_cells * PTS] = piece[:rhs, :].astype(BF16)
    hdb[:, halo_cells * PTS :] = jnp.zeros((rhs, PTS), BF16)
    hpc = piece.at[rhs : rhs + 8]
    low, top, spread = prepare(halo_cells, hpc, halo_cells * PTS, hcen, hfs)
    ri = lax.broadcasted_iota(jnp.int32, (128, 128), 0)
    rj = lax.broadcasted_iota(jnp.int32, (128, 128), 1)
    need = near(box[0:8, :], box[8:16, :], low, top) & (rj < halo_cells) & (ri < cells)
    stop = as_rows(jnp.where(need, rj + 1, 0))
    lane128 = lax.broadcasted_iota(jnp.int32, (1, 128), 1)
    first = jnp.min(jnp.where(need, ri, 127).astype(F32), axis=(0, 1), keepdims=True)
    first = jnp.minimum(first.astype(jnp.int32), strips)
    stop = jnp.maximum(stop, 1)
    total = lanes_sum(jnp.where((lane128 >= first) & (lane128 < strips), stop, 0))
    stop = jnp.where(lane128 == 125, total, jnp.where(lane128 == 126, first, stop))
    to_scalars(jnp.where(lane128 == 127, spread + tab[0, 127], stop), tab_v, tab_s, sem)
    sweep(
        tab_s[0, 126], strips, lambda i: jnp.int32(0), lambda i: tab_s[0, i], tab_s[0, 125],
        (cells, halo_cells), tab_s[0, 127],
        (pc, db), (hpc, hdb, hfs, hcen), acc_i, halo, bufs,
    )
    halo[:, : halo_cells * PTS] = halo[:, : halo_cells * PTS] * (1.0 / 256.0)


def tail_kernel(cells, db, pc, fs, cen, tab, acc_e, acc_i, acc_j, *bufs):
    acc_i[...] = acc_e[...]
    acc_j[...] = jnp.zeros_like(acc_j)
    side = (pc, db, fs, cen)
    sweep(
        jnp.int32(0), tab[0, 125], lambda i: i, lambda i: tab[0, i], tab[0, 126],
        (cells, cells), tab[0, 127],
        side[:2], side, acc_i, acc_j, bufs,
    )


def piece_kernel(cells, cnt_h, pts_h, dirs_h, piece, cnt, pts, dirs, sem):
    rhs = dirs.shape[0]
    span = pl.ds(0, cells * PTS)
    copies = fetch(((cnt_h, cnt), (pts_h.at[:, span], pts), (dirs_h.at[:, span], dirs)), sem)
    lane1 = lax.broadcasted_iota(jnp.int32, (1, PTS), 1)
    piece[rhs:, :] = jnp.zeros_like(piece[rhs:, :])
    for copy in copies:
        copy.wait()
    for c in range(cells):
        at = slice(c * PTS, (c + 1) * PTS)
        live = lane1 < cnt[c]
        piece[:rhs, at] = jnp.where(live, dirs[:, at], 0.0)
        here = jnp.where(live, pts[:, at], pts[:, c * PTS : c * PTS + 1])
        piece[rhs : rhs + 3, at] = 4.0 * here


VM = pl.BlockSpec(memory_space=pltpu.VMEM)
SM = pl.BlockSpec(memory_space=pltpu.SMEM)
HB = pl.BlockSpec(memory_space=pltpu.MemorySpace.HBM)
LONG = 24
DEPTH = 4


def params(mib):
    return pltpu.CompilerParams(vmem_limit_bytes=mib << 20)


def buffers():
    return [pltpu.VMEM((PTS, PTS), F32)] * DEPTH


def cost(units):
    return pl.CostEstimate(flops=units * 60_000_000, bytes_accessed=4_000_000, transcendentals=units * 65536)


def pair_products(counts, points, direction):
    cells = counts.shape[0]
    rhs = direction.shape[0]
    width = min(cells, REACH)
    blocks = cells + 1
    wide = blocks * PTS + 256
    shape = jax.ShapeDtypeStruct

    held = [pltpu.with_memory_space_constraint(x, pltpu.MemorySpace.HBM) for x in (counts, points, direction)]
    piece = pl.pallas_call(
        lambda *refs: piece_kernel(width, *refs),
        name="piece",
        out_shape=shape((rhs + 8, width * PTS), F32),
        in_specs=[HB] * 3,
        out_specs=VM,
        scratch_shapes=[
            pltpu.SMEM((cells,), jnp.int32),
            pltpu.VMEM((3, width * PTS), F32),
            pltpu.VMEM((rhs, width * PTS), F32),
            pltpu.SemaphoreType.DMA((3,)),
        ],
        compiler_params=params(8),
    )(*held)
    piece = passed_along(piece, -1)
    db, pc, fs, cen, box, tab, off = pl.pallas_call(
        lambda *refs: head_kernel(cells, *refs),
        name="head",
        out_shape=[
            shape((rhs, wide), BF16),
            shape((8, wide), F32),
            shape((blocks * PTS, KF), BF16),
            shape((blocks * 8, 128), F32),
            shape((16, 128), F32),
            shape((8, 128), jnp.int32),
            shape((cells,), jnp.int32),
        ],
        in_specs=[HB] * 3,
        out_specs=[VM] * 6 + [SM],
        scratch_shapes=[
            pltpu.SMEM((cells,), jnp.int32),
            pltpu.VMEM(points.shape, F32),
            pltpu.VMEM(direction.shape, F32),
            pltpu.VMEM((rhs, wide), F32),
            pltpu.SemaphoreType.DMA((3,)),
        ],
        compiler_params=params(12),
        cost_estimate=cost(100),
    )(*held)
    halo, acc_e = pl.pallas_call(
        lambda *refs: edge_kernel(cells, width, *refs),
        name="edge",
        out_shape=[shape((rhs, (width + 1) * PTS), F32), shape((rhs, wide), F32)],
        in_specs=[VM] * 3 + [SM, VM],
        out_specs=[VM] * 2,
        scratch_shapes=[
            pltpu.VMEM((rhs, (width + 1) * PTS), BF16),
            pltpu.VMEM(((width + 1) * PTS, KF), BF16),
            pltpu.VMEM(((width + 1) * 8, 128), F32),
            pltpu.VMEM((8, 128), jnp.int32),
        ]
        + buffers()
        + [pltpu.SMEM((8, 128), jnp.int32), pltpu.SemaphoreType.DMA],
        compiler_params=params(12),
        cost_estimate=cost(70),
    )(db, pc, box, tab, piece)
    back = passed_along(halo, 1)
    acc_i, acc_j = pl.pallas_call(
        lambda *refs: tail_kernel(cells, *refs),
        name="tail",
        out_shape=[shape((rhs, wide), F32)] * 2,
        in_specs=[VM] * 4 + [SM, VM],
        out_specs=[VM] * 2,
        scratch_shapes=buffers(),
        compiler_params=params(12),
        cost_estimate=cost(180),
    )(db, pc, fs, cen, tab, acc_e)
    return off, acc_i, acc_j, back


def sums_kernel(cnt, off, acc_i, acc_j, back, nug, dirs, res, ritz, image, sums):
    cells = image.shape[1] // PTS
    halo_cells = back.shape[1] // PTS - 1
    lane1 = lax.broadcasted_iota(jnp.int32, (1, PTS), 1)

    def of_cell(c, part, extra):
        live = lane1 < cnt[c]
        d = jnp.where(live, dirs[:, cols(c)], 0.0)
        r = jnp.where(live, res[:, cols(c)], 0.0)
        at = off[c]
        base = pl.multiple_of((at // 128) * 128, 128)
        k = acc_i[:, pl.ds(base, 384)] + acc_j[:, pl.ds(base, 384)]
        k = pltpu.roll(k, 384 - at % 128, 1)[:, :PTS] * (1.0 / 256.0)
        if extra:
            k = k + back[:, cols(c)]
        im = jnp.where(live, nug[:, cols(c)] * d + k, 0.0)
        image[:, cols(c)] = im
        dk, rr, ri, ii, prod = part
        both = jnp.concatenate([r, im], axis=0)
        bh = high(both)
        z = ritz[:, cols(c)]
        zh = high(z)
        left = jnp.concatenate([bh, both - bh], axis=0).astype(BF16)
        right = jnp.concatenate([zh, z - zh], axis=0).astype(BF16)
        return dk + d * im, rr + r * r, ri + r * im, ii + im * im, prod + mm_t(left, right)

    rhs = image.shape[0]
    zero = jnp.zeros((rhs, PTS), F32)
    part = (zero, zero, zero, zero, jnp.zeros((4 * rhs, 2 * ritz.shape[0]), F32))
    part = lax.fori_loop(0, halo_cells, lambda c, p: of_cell(c, p, True), part, unroll=6)
    part = lax.fori_loop(halo_cells, cells, lambda c, p: of_cell(c, p, False), part, unroll=5)
    dots = [jnp.sum(p, axis=1, keepdims=True) for p in part[:4]]
    prod = part[4]
    n = ritz.shape[0]
    h = 2 * rhs
    prod = prod[:h, :n] + prod[:h, n:] + prod[h:, :n]
    half = rhs // 2
    both = jnp.concatenate([prod[:rhs], prod[rhs:]], axis=1)
    both = jnp.concatenate([both[:half], both[half:]], axis=1)
    for k in range(half):
        sums[k] = both[k : k + 1]
    lane = lax.broadcasted_iota(jnp.int32, (rhs, 128), 1)
    table = jnp.zeros((rhs, 128), F32)
    for k in range(4):
        table = jnp.where(lane == k, dots[k], table)
    table = jnp.concatenate([table, jnp.zeros((128 - rhs, 128), F32)], axis=0).T
    line = jnp.zeros((1, 128), F32)
    lane = lane[:1]
    for k in range(4):
        row = table[k : k + 1]
        row = row if k == 0 else pltpu.roll(row, k * rhs, 1)
        line = jnp.where((lane >= k * rhs) & (lane < (k + 1) * rhs), row, line)
    sums[half] = line


def local_sums(counts, off, acc_i, acc_j, back, nugget, direction, residual, ritz_image):
    return pl.pallas_call(
        sums_kernel,
        name="sums",
        out_shape=[
            jax.ShapeDtypeStruct(direction.shape, F32),
            jax.ShapeDtypeStruct((9, 1, 128), F32),
        ],
        in_specs=[SM, SM] + [VM] * 7,
        out_specs=[VM, VM],
        compiler_params=params(12),
    )(counts, off, acc_i, acc_j, back, nugget, direction, residual, ritz_image)


def finish_kernel(
    cnt, sums, gram, image, dirs, res, sol, basis, sol_h, res_h, dir_h, sol_out, res_out, dir_out, sem
):
    cells = image.shape[1] // PTS
    n = gram.shape[0]
    lane1 = lax.broadcasted_iota(jnp.int32, (1, PTS), 1)
    rhs = image.shape[0]
    half = rhs // 2
    both = jnp.concatenate([sums[k] for k in range(half)], axis=0)
    both = jnp.concatenate([both[:, : 2 * n], both[:, 2 * n :]], axis=0)
    line = sums[half]
    table = [line if k == 0 else pltpu.roll(line, 128 - k * rhs, 1) for k in range(4)]
    table = jnp.concatenate(table + [jnp.zeros((124, 128), F32)], axis=0).T
    curvature, rr, ri, ii = (table[:rhs, k : k + 1] for k in range(4))
    step = rr / curvature
    growth = (rr + step * (step * ii - 2.0 * ri)) / rr
    projected = both[:, :n] - step * both[:, n:]
    ph = high(projected)
    g = gram[...]
    gh = high(g)
    coef = mm_t(
        jnp.concatenate([ph, ph, projected - ph], axis=1).astype(BF16),
        jnp.concatenate([gh, g - gh, gh], axis=1).astype(BF16),
    )
    ch = high(coef)
    left = jnp.concatenate([ch, ch, coef - ch], axis=1).astype(BF16)

    def of_cell(c, _):
        live = lane1 < cnt[c]
        d = jnp.where(live, dirs[:, cols(c)], 0.0)
        r = jnp.where(live, res[:, cols(c)], 0.0)
        s = jnp.where(live, sol[:, cols(c)], 0.0)
        b = basis[:, cols(c)]
        bh = high(b)
        right = jnp.concatenate([bh, b - bh, bh], axis=0).astype(BF16)
        new = r - step * image[:, cols(c)]
        sol_out[:, cols(c)] = s + step * d
        res_out[:, cols(c)] = new
        dir_out[:, cols(c)] = jnp.where(live, growth * d + new - mm(left, right), 0.0)
        return 0

    pieces = 4
    many = cells // pieces
    copies = []
    for k in range(pieces):
        lax.fori_loop(k * many, (k + 1) * many, of_cell, 0, unroll=8)
        at = pl.ds(k * many * PTS, many * PTS)
        for n, (src, dst) in enumerate(((sol_out, sol_h), (res_out, res_h), (dir_out, dir_h))):
            copies.append(pltpu.make_async_copy(src.at[:, at], dst.at[:, at], sem.at[3 * k + n]))
            copies[-1].start()
    for copy in copies:
        copy.wait()


def finish(counts, sums, gram, image, direction, residual, solution, basis):
    return pl.pallas_call(
        finish_kernel,
        name="finish",
        out_shape=[jax.ShapeDtypeStruct(image.shape, F32)] * 3,
        in_specs=[SM] + [VM] * 7,
        out_specs=[HB] * 3,
        scratch_shapes=[pltpu.VMEM(image.shape, F32)] * 3 + [pltpu.SemaphoreType.DMA((12,))],
        compiler_params=params(12),
    )(counts, sums, gram, image, direction, residual, solution, basis)


def passed_along(array, by):
    length = lax.axis_size(AXES)
    pairs = [(i, i + by) for i in range(length) if 0 <= i + by < length]
    return lax.ppermute(array, AXES, pairs)


def groups_of(length, bits):
    others = [i for i in range(length) if not any(i >> b & 1 for b in bits)]
    spread = [sum((m >> k & 1) << b for k, b in enumerate(bits)) for m in range(1 << len(bits))]
    return [[i + s for s in spread] for i in others]


def summed(array):
    length = lax.axis_size(AXES)
    array = array + lax.ppermute(array, AXES, [(i, i ^ 1) for i in range(length)])
    for bits in ((1, 2, 3, 4), (5, 6, 7)):
        copies = jnp.broadcast_to(array[None], (1 << len(bits),) + array.shape)
        parts = lax.all_to_all(copies, AXES, 0, 0, axis_index_groups=groups_of(length, bits))
        array = jnp.sum(parts, axis=0)
    return array


def local(
    points,
    cell_counts,
    pair_cells,
    pair_counts,
    nugget,
    solution,
    residual,
    direction,
    ritz_basis,
    ritz_image,
    inverse_gram,
):
    off, acc_i, acc_j, back = pair_products(cell_counts, points, direction)
    image, sums = local_sums(
        cell_counts, off, acc_i, acc_j, back, nugget.reshape(1, -1), direction, residual, ritz_image
    )
    return tuple(
        finish(
            cell_counts,
            summed(sums),
            inverse_gram,
            image,
            direction,
            residual,
            solution,
            ritz_basis,
        )
    )


def solution(mesh):
    split = P(None, AXES)
    line = P(AXES)
    in_specs = (split, line, split, line, line, split, split, split, split, split, P())
    return jax.shard_map(
        local, mesh=mesh, in_specs=in_specs, out_specs=(split,) * 3, check_vma=False
    )
```

```python
import jax
import jax.numpy as jnp
from jax import lax
from jax.experimental import pallas as pl
from jax.experimental.pallas import tpu as pltpu
from jax.sharding import PartitionSpec as P

PTS = 256
REACH = 12
KF = 48
FAR = 1e18
ROOM = 16.0
AXES = ("region", "cell")
F32 = jnp.float32
BF16 = jnp.bfloat16


def mm(x, y):
    return lax.dot_general(x, y, (((1,), (0,)), ((), ())), preferred_element_type=F32)


def mm_t(x, y):
    return lax.dot_general(x, y, (((1,), (1,)), ((), ())), preferred_element_type=F32)


def high(x):
    return x.astype(BF16).astype(F32)


def split3(x):
    h = high(x)
    m = high(x - h)
    return h, m, x - h - m


def tile_of(scaled_square):
    s = jnp.maximum(scaled_square, 1e-30)
    t = s * lax.rsqrt(s)
    u = jnp.maximum(4.0 - t, 0.0)
    u2 = u * u
    return ((u2 * u2) * (t + 1.0)).astype(BF16)


def cols(block, size=PTS):
    return pl.ds(pl.multiple_of(block * size, size), size)


def with_norm(vec):
    row = lax.broadcasted_iota(jnp.int32, vec.shape, 0)
    return row, jnp.sum(vec * vec, axis=0, keepdims=True)


def weights_side(p):
    row, norm = with_norm(p)
    a = jnp.where(row == 3, norm, p)
    h, m, l = split3(a)
    one_h = jnp.where(row == 3, 1.0, h)
    one_m = jnp.where(row == 3, 1.0, m)
    return jnp.concatenate([h, m, one_h, one_m, l, one_h], axis=0).astype(BF16)


def rows_side(q):
    row, norm = with_norm(q)
    a = jnp.where(row == 3, norm, -2.0 * q)
    h, m, l = split3(a)
    one = jnp.where(row == 3, 1.0, h)
    mid_h = jnp.where(row == 3, h, m)
    return jnp.concatenate([one, one, mid_h, m, one, l], axis=0), norm


def pack(cells, cnt, off, dirs, pts, dc, pc):
    lane1 = lax.broadcasted_iota(jnp.int32, (1, PTS), 1)
    lane128 = lax.broadcasted_iota(jnp.int32, (1, 128), 1)

    def place(c, at):
        off[c] = at
        shift = at % 128
        base = pl.multiple_of((at // 128) * 128, 128)
        live = lane1 < cnt[c]
        dv = jnp.where(live, dirs[:, cols(c)], 0.0)
        pv = jnp.where(live, 4.0 * pts[:, cols(c)], 0.0)
        for ref, val in ((dc, dv), (pc, pv)):
            rows = val.shape[0]
            wide = jnp.concatenate([val, jnp.zeros((rows, 128), F32)], axis=1)
            wide = pltpu.roll(wide, shift, 1)
            old = ref[:rows, pl.ds(base, 128)]
            ref[:rows, pl.ds(base, 128)] = jnp.where(lane128 < shift, old, wide[:, :128])
            ref[:rows, pl.ds(base + 128, 256)] = wide[:, 128:]
        return at + cnt[c]

    return lax.fori_loop(0, cells, place, jnp.int32(0), unroll=8)


def prepare(blocks, pc, end, cen, fs):
    lane1 = lax.broadcasted_iota(jnp.int32, (1, PTS), 1)
    lane128 = lax.broadcasted_iota(jnp.int32, (1, 128), 1)

    def one(j, carry):
        low, top, far = carry
        here = pc[:, cols(j)]
        valid = j * PTS + lane1 < end
        lo = jnp.min(jnp.where(valid, here, FAR), axis=1, keepdims=True)
        hi = jnp.max(jnp.where(valid, here, -FAR), axis=1, keepdims=True)
        centre = jnp.where(lo <= hi, 0.5 * (lo + hi), 0.0)
        cen[pl.ds(pl.multiple_of(j * 8, 8), 8), :] = jnp.broadcast_to(centre, (8, 128))
        feats, norm = rows_side(here - centre)
        fs[cols(j), :] = feats.T.astype(BF16)
        low = jnp.where(lane128 == j, lo, low)
        top = jnp.where(lane128 == j, hi, top)
        return low, top, jnp.maximum(far, jnp.where(valid, norm, 0.0))

    start = (
        jnp.full((8, 128), FAR, F32),
        jnp.full((8, 128), -FAR, F32),
        jnp.zeros((1, PTS), F32),
    )
    low, top, far = lax.fori_loop(0, blocks, one, start, unroll=12 if blocks % 12 == 0 else 8)
    cen[pl.ds(blocks * 8, 8), :] = jnp.zeros((8, 128), F32)
    fs[pl.ds(blocks * PTS, PTS), :] = jnp.zeros((PTS, KF), BF16)
    wide = jnp.max(far, axis=1, keepdims=True) > 16.0 * ROOM
    return low, top, jnp.where(wide, 1, 0)


def square(v):
    return jnp.concatenate([v, jnp.zeros((120, 128), F32)], axis=0).T


def near(low_i, top_i, low_j, top_j):
    low_t, top_t = square(low_i), square(top_i)
    gap2 = jnp.zeros((128, 128), F32)
    for k in range(3):
        gap = jnp.maximum(
            low_j[k : k + 1] - top_t[:, k : k + 1], low_t[:, k : k + 1] - top_j[k : k + 1]
        )
        gap = jnp.maximum(gap, 0.0)
        gap2 = gap2 + gap * gap
    return gap2 <= 16.016


def as_rows(last):
    last = jnp.max(last.astype(F32), axis=1, keepdims=True)
    return jnp.broadcast_to(last, (128, 128)).T[:8].astype(jnp.int32)


def lanes_sum(values):
    return jnp.sum(values.astype(F32), axis=1, keepdims=True).astype(jnp.int32)


def to_scalars(values, tab_v, tab_s, sem):
    tab_v[...] = values
    copy = pltpu.make_async_copy(tab_v, tab_s, sem)
    copy.start()
    copy.wait()


def sweep(first, end, begin, stop, total, spare, spread, side_i, side_j, acc_i, acc_j, bufs):
    pc_i, db_i = side_i
    pc_j, db_j, fs_j, cen_j = side_j
    depth = len(bufs)
    def enter(i):
        i = jnp.where(i >= end, spare[0], i)
        return i, jnp.where(i == spare[0], spare[1], begin(i))

    def following(i, j):
        n = j + 1
        over = (n >= stop(i)) | (i == spare[0])
        i2, j2 = enter(i + 1)
        return jnp.where(over, i2, i), jnp.where(over, j2, n)

    def squares(i, j, out):
        c = cen_j[pl.ds(pl.multiple_of(j * 8, 8), 8), :]
        f = weights_side(pc_i[:, cols(i)] - jnp.concatenate([c, c], axis=1))
        out[...] = mm(fs_j[cols(j), :], f)

    same = db_i is db_j

    def products(i, j, tile):
        other = mm_t(db_i[:, cols(i)], tile)
        mine = mm(db_j[:, cols(j)], tile)
        return i, jnp.where(j > i, j, spare[1]) if same else j, mine, other

    def add(i, j, mine, other):
        acc_i[:, cols(i)] += mine
        acc_j[:, cols(j)] += other

    queue = [enter(first)]
    for _ in range(depth - 1):
        queue.append(following(*queue[-1]))

    @pl.when(spread == 0)
    def _():
        for k in range(depth - 1):
            squares(*queue[k], bufs[k])

        def turn(units):
            def one(_, carry):
                q = list(carry)
                waiting = None
                for g in range(units):
                    squares(*q[-1], bufs[(g + depth - 1) % depth])
                    done = products(*q[0], tile_of(bufs[g % depth][...]))
                    if waiting is not None:
                        add(*waiting)
                    waiting = done
                    q = q[1:] + [following(*q[-1])]
                add(*waiting)
                return tuple(q)

            return one

        state = lax.fori_loop(0, total // LONG, turn(LONG), tuple(queue))
        left = total - (total // LONG) * LONG
        lax.fori_loop(0, (left + depth - 1) // depth, turn(depth), state)

    @pl.when(spread != 0)
    def _():
        def one(_, carry):
            i, j = carry
            pj = pc_j[:, cols(j)].T
            pi = pc_i[:, cols(i)]
            for h in range(0, PTS, 64):
                s = jnp.zeros((64, PTS), F32)
                for k in range(3):
                    d = pj[h : h + 64, k : k + 1] - pi[k : k + 1, :]
                    s = s + d * d
                bufs[0][pl.ds(h, 64), :] = s
            add(*products(i, j, tile_of(bufs[0][...])))
            return following(i, j)

        lax.fori_loop(0, total, one, queue[0])


def fetch(pairs, sems):
    copies = [pltpu.make_async_copy(src, dst, sems.at[k]) for k, (src, dst) in enumerate(pairs)]
    for copy in copies:
        copy.start()
    return copies


def head_kernel(cells, cnt_h, pts_h, dirs_h, db, pc, fs, cen, box, tab, off, cnt, pts, dirs, dc, sem):
    copies = fetch(((cnt_h, cnt), (pts_h, pts), (dirs_h, dirs)), sem)
    dc[...] = jnp.zeros_like(dc)
    pc[...] = jnp.zeros_like(pc)
    for copy in copies:
        copy.wait()
    own_end = pack(cells, cnt, off, dirs, pts, dc, pc)
    db[...] = dc[...].astype(BF16)
    low, top, spread = prepare(cells, pc, own_end, cen, fs)
    box[0:8, :] = low
    box[8:16, :] = top
    ri = lax.broadcasted_iota(jnp.int32, (128, 128), 0)
    rj = lax.broadcasted_iota(jnp.int32, (128, 128), 1)
    need = near(low, top, low, top) & (rj > ri)
    stop = as_rows(jnp.where(need, rj + 1, ri + 1))
    lane128 = lax.broadcasted_iota(jnp.int32, (1, 128), 1)
    strips = (own_end + (PTS - 1)) // PTS
    total = lanes_sum(jnp.where(lane128 < strips, stop - lane128, 0))
    stop = jnp.where(lane128 == 125, strips, jnp.where(lane128 == 126, total, stop))
    tab[...] = jnp.where(lane128 == 127, spread, stop)


def edge_kernel(cells, halo_cells, db, pc, box, tab, piece, halo, acc_i, hdb, hfs, hcen, tab_v, *rest):
    *bufs, tab_s, sem = rest
    strips = tab[0, 125]
    acc_i[...] = jnp.zeros_like(acc_i)
    halo[...] = jnp.zeros_like(halo)
    rhs = hdb.shape[0]
    hdb[:, : halo_cells * PTS] = piece[:rhs, :].astype(BF16)
    hdb[:, halo_cells * PTS :] = jnp.zeros((rhs, PTS), BF16)
    hpc = piece.at[rhs : rhs + 8]
    low, top, spread = prepare(halo_cells, hpc, halo_cells * PTS, hcen, hfs)
    ri = lax.broadcasted_iota(jnp.int32, (128, 128), 0)
    rj = lax.broadcasted_iota(jnp.int32, (128, 128), 1)
    need = near(box[0:8, :], box[8:16, :], low, top) & (rj < halo_cells) & (ri < cells)
    stop = as_rows(jnp.where(need, rj + 1, 0))
    lane128 = lax.broadcasted_iota(jnp.int32, (1, 128), 1)
    first = jnp.min(jnp.where(need, ri, 127).astype(F32), axis=(0, 1), keepdims=True)
    first = jnp.minimum(first.astype(jnp.int32), strips)
    stop = jnp.maximum(stop, 1)
    total = lanes_sum(jnp.where((lane128 >= first) & (lane128 < strips), stop, 0))
    stop = jnp.where(lane128 == 125, total, jnp.where(lane128 == 126, first, stop))
    to_scalars(jnp.where(lane128 == 127, spread + tab[0, 127], stop), tab_v, tab_s, sem)
    sweep(
        tab_s[0, 126], strips, lambda i: jnp.int32(0), lambda i: tab_s[0, i], tab_s[0, 125],
        (cells, halo_cells), tab_s[0, 127],
        (pc, db), (hpc, hdb, hfs, hcen), acc_i, halo, bufs,
    )
    halo[:, : halo_cells * PTS] = halo[:, : halo_cells * PTS] * (1.0 / 256.0)


def tail_kernel(cells, db, pc, fs, cen, tab, acc_e, acc_i, acc_j, *bufs):
    acc_i[...] = acc_e[...]
    acc_j[...] = jnp.zeros_like(acc_j)
    side = (pc, db, fs, cen)
    sweep(
        jnp.int32(0), tab[0, 125], lambda i: i, lambda i: tab[0, i], tab[0, 126],
        (cells, cells), tab[0, 127],
        side[:2], side, acc_i, acc_j, bufs,
    )


def piece_kernel(cells, cnt_h, pts_h, dirs_h, piece, cnt, pts, dirs, sem):
    rhs = dirs.shape[0]
    span = pl.ds(0, cells * PTS)
    copies = fetch(((cnt_h, cnt), (pts_h.at[:, span], pts), (dirs_h.at[:, span], dirs)), sem)
    lane1 = lax.broadcasted_iota(jnp.int32, (1, PTS), 1)
    piece[rhs:, :] = jnp.zeros_like(piece[rhs:, :])
    for copy in copies:
        copy.wait()
    for c in range(cells):
        at = slice(c * PTS, (c + 1) * PTS)
        live = lane1 < cnt[c]
        piece[:rhs, at] = jnp.where(live, dirs[:, at], 0.0)
        here = jnp.where(live, pts[:, at], pts[:, c * PTS : c * PTS + 1])
        piece[rhs : rhs + 3, at] = 4.0 * here


VM = pl.BlockSpec(memory_space=pltpu.VMEM)
SM = pl.BlockSpec(memory_space=pltpu.SMEM)
HB = pl.BlockSpec(memory_space=pltpu.MemorySpace.HBM)
LONG = 24
DEPTH = 4


def params(mib):
    return pltpu.CompilerParams(vmem_limit_bytes=mib << 20)


def buffers():
    return [pltpu.VMEM((PTS, PTS), F32)] * DEPTH


def cost(units):
    return pl.CostEstimate(flops=units * 60_000_000, bytes_accessed=4_000_000, transcendentals=units * 65536)


def pair_products(counts, points, direction):
    cells = counts.shape[0]
    rhs = direction.shape[0]
    width = min(cells, REACH)
    blocks = cells + 1
    wide = blocks * PTS + 256
    shape = jax.ShapeDtypeStruct

    held = [pltpu.with_memory_space_constraint(x, pltpu.MemorySpace.HBM) for x in (counts, points, direction)]
    piece = pl.pallas_call(
        lambda *refs: piece_kernel(width, *refs),
        name="piece",
        out_shape=shape((rhs + 8, width * PTS), F32),
        in_specs=[HB] * 3,
        out_specs=VM,
        scratch_shapes=[
            pltpu.SMEM((cells,), jnp.int32),
            pltpu.VMEM((3, width * PTS), F32),
            pltpu.VMEM((rhs, width * PTS), F32),
            pltpu.SemaphoreType.DMA((3,)),
        ],
        compiler_params=params(8),
    )(*held)
    piece = passed_along(piece, -1)
    db, pc, fs, cen, box, tab, off = pl.pallas_call(
        lambda *refs: head_kernel(cells, *refs),
        name="head",
        out_shape=[
            shape((rhs, wide), BF16),
            shape((8, wide), F32),
            shape((blocks * PTS, KF), BF16),
            shape((blocks * 8, 128), F32),
            shape((16, 128), F32),
            shape((8, 128), jnp.int32),
            shape((cells,), jnp.int32),
        ],
        in_specs=[HB] * 3,
        out_specs=[VM] * 6 + [SM],
        scratch_shapes=[
            pltpu.SMEM((cells,), jnp.int32),
            pltpu.VMEM(points.shape, F32),
            pltpu.VMEM(direction.shape, F32),
            pltpu.VMEM((rhs, wide), F32),
            pltpu.SemaphoreType.DMA((3,)),
        ],
        compiler_params=params(12),
        cost_estimate=cost(100),
    )(*held)
    halo, acc_e = pl.pallas_call(
        lambda *refs: edge_kernel(cells, width, *refs),
        name="edge",
        out_shape=[shape((rhs, (width + 1) * PTS), F32), shape((rhs, wide), F32)],
        in_specs=[VM] * 3 + [SM, VM],
        out_specs=[VM] * 2,
        scratch_shapes=[
            pltpu.VMEM((rhs, (width + 1) * PTS), BF16),
            pltpu.VMEM(((width + 1) * PTS, KF), BF16),
            pltpu.VMEM(((width + 1) * 8, 128), F32),
            pltpu.VMEM((8, 128), jnp.int32),
        ]
        + buffers()
        + [pltpu.SMEM((8, 128), jnp.int32), pltpu.SemaphoreType.DMA],
        compiler_params=params(12),
        cost_estimate=cost(70),
    )(db, pc, box, tab, piece)
    back = passed_along(halo, 1)
    acc_i, acc_j = pl.pallas_call(
        lambda *refs: tail_kernel(cells, *refs),
        name="tail",
        out_shape=[shape((rhs, wide), F32)] * 2,
        in_specs=[VM] * 4 + [SM, VM],
        out_specs=[VM] * 2,
        scratch_shapes=buffers(),
        compiler_params=params(12),
        cost_estimate=cost(180),
    )(db, pc, fs, cen, tab, acc_e)
    return off, acc_i, acc_j, back


def sums_kernel(cnt, off, acc_i, acc_j, back, nug, dirs, res, ritz, image, sums):
    cells = image.shape[1] // PTS
    halo_cells = back.shape[1] // PTS - 1
    lane1 = lax.broadcasted_iota(jnp.int32, (1, PTS), 1)

    def of_cell(c, part, extra):
        live = lane1 < cnt[c]
        d = jnp.where(live, dirs[:, cols(c)], 0.0)
        r = jnp.where(live, res[:, cols(c)], 0.0)
        at = off[c]
        base = pl.multiple_of((at // 128) * 128, 128)
        k = acc_i[:, pl.ds(base, 384)] + acc_j[:, pl.ds(base, 384)]
        k = pltpu.roll(k, 384 - at % 128, 1)[:, :PTS] * (1.0 / 256.0)
        if extra:
            k = k + back[:, cols(c)]
        im = jnp.where(live, nug[:, cols(c)] * d + k, 0.0)
        image[:, cols(c)] = im
        dk, rr, ri, ii, prod = part
        both = jnp.concatenate([r, im], axis=0)
        bh = high(both)
        z = ritz[:, cols(c)]
        zh = high(z)
        left = jnp.concatenate([bh, both - bh], axis=0).astype(BF16)
        right = jnp.concatenate([zh, z - zh], axis=0).astype(BF16)
        return dk + d * im, rr + r * r, ri + r * im, ii + im * im, prod + mm_t(left, right)

    rhs = image.shape[0]
    zero = jnp.zeros((rhs, PTS), F32)
    part = (zero, zero, zero, zero, jnp.zeros((4 * rhs, 2 * ritz.shape[0]), F32))
    part = lax.fori_loop(0, halo_cells, lambda c, p: of_cell(c, p, True), part, unroll=12)
    part = lax.fori_loop(halo_cells, cells, lambda c, p: of_cell(c, p, False), part, unroll=20)
    dots = [jnp.sum(p, axis=1, keepdims=True) for p in part[:4]]
    prod = part[4]
    n = ritz.shape[0]
    h = 2 * rhs
    prod = prod[:h, :n] + prod[:h, n:] + prod[h:, :n]
    half = rhs // 2
    both = jnp.concatenate([prod[:rhs], prod[rhs:]], axis=1)
    both = jnp.concatenate([both[:half], both[half:]], axis=1)
    for k in range(half):
        sums[k] = both[k : k + 1]
    lane = lax.broadcasted_iota(jnp.int32, (rhs, 128), 1)
    table = jnp.zeros((rhs, 128), F32)
    for k in range(4):
        table = jnp.where(lane == k, dots[k], table)
    table = jnp.concatenate([table, jnp.zeros((128 - rhs, 128), F32)], axis=0).T
    line = jnp.zeros((1, 128), F32)
    lane = lane[:1]
    for k in range(4):
        row = table[k : k + 1]
        row = row if k == 0 else pltpu.roll(row, k * rhs, 1)
        line = jnp.where((lane >= k * rhs) & (lane < (k + 1) * rhs), row, line)
    sums[half] = line


def local_sums(counts, off, acc_i, acc_j, back, nugget, direction, residual, ritz_image):
    return pl.pallas_call(
        sums_kernel,
        name="sums",
        out_shape=[
            jax.ShapeDtypeStruct(direction.shape, F32),
            jax.ShapeDtypeStruct((9, 1, 128), F32),
        ],
        in_specs=[SM, SM] + [VM] * 7,
        out_specs=[VM, VM],
        compiler_params=params(12),
    )(counts, off, acc_i, acc_j, back, nugget, direction, residual, ritz_image)


def finish_kernel(
    cnt, sums, gram, image, dirs, res, sol, basis, sol_h, res_h, dir_h, sol_out, res_out, dir_out, sem
):
    cells = image.shape[1] // PTS
    n = gram.shape[0]
    lane1 = lax.broadcasted_iota(jnp.int32, (1, PTS), 1)
    rhs = image.shape[0]
    half = rhs // 2
    both = jnp.concatenate([sums[k] for k in range(half)], axis=0)
    both = jnp.concatenate([both[:, : 2 * n], both[:, 2 * n :]], axis=0)
    line = sums[half]
    table = [line if k == 0 else pltpu.roll(line, 128 - k * rhs, 1) for k in range(4)]
    table = jnp.concatenate(table + [jnp.zeros((124, 128), F32)], axis=0).T
    curvature, rr, ri, ii = (table[:rhs, k : k + 1] for k in range(4))
    step = rr / curvature
    growth = (rr + step * (step * ii - 2.0 * ri)) / rr
    projected = both[:, :n] - step * both[:, n:]
    ph = high(projected)
    g = gram[...]
    gh = high(g)
    coef = mm_t(
        jnp.concatenate([ph, ph, projected - ph], axis=1).astype(BF16),
        jnp.concatenate([gh, g - gh, gh], axis=1).astype(BF16),
    )
    ch = high(coef)
    left = jnp.concatenate([ch, ch, coef - ch], axis=1).astype(BF16)

    def of_cell(c, _):
        live = lane1 < cnt[c]
        d = jnp.where(live, dirs[:, cols(c)], 0.0)
        r = jnp.where(live, res[:, cols(c)], 0.0)
        s = jnp.where(live, sol[:, cols(c)], 0.0)
        b = basis[:, cols(c)]
        bh = high(b)
        right = jnp.concatenate([bh, b - bh, bh], axis=0).astype(BF16)
        new = r - step * image[:, cols(c)]
        sol_out[:, cols(c)] = s + step * d
        res_out[:, cols(c)] = new
        dir_out[:, cols(c)] = jnp.where(live, growth * d + new - mm(left, right), 0.0)
        return 0

    pieces = 4
    many = cells // pieces
    copies = []
    for k in range(pieces):
        lax.fori_loop(k * many, (k + 1) * many, of_cell, 0, unroll=8)
        at = pl.ds(k * many * PTS, many * PTS)
        for n, (src, dst) in enumerate(((sol_out, sol_h), (res_out, res_h), (dir_out, dir_h))):
            copies.append(pltpu.make_async_copy(src.at[:, at], dst.at[:, at], sem.at[3 * k + n]))
            copies[-1].start()
    for copy in copies:
        copy.wait()


def finish(counts, sums, gram, image, direction, residual, solution, basis):
    return pl.pallas_call(
        finish_kernel,
        name="finish",
        out_shape=[jax.ShapeDtypeStruct(image.shape, F32)] * 3,
        in_specs=[SM] + [VM] * 7,
        out_specs=[HB] * 3,
        scratch_shapes=[pltpu.VMEM(image.shape, F32)] * 3 + [pltpu.SemaphoreType.DMA((12,))],
        compiler_params=params(12),
    )(counts, sums, gram, image, direction, residual, solution, basis)


def passed_along(array, by):
    length = lax.axis_size(AXES)
    pairs = [(i, i + by) for i in range(length) if 0 <= i + by < length]
    return lax.ppermute(array, AXES, pairs)


def groups_of(length, bits):
    others = [i for i in range(length) if not any(i >> b & 1 for b in bits)]
    spread = [sum((m >> k & 1) << b for k, b in enumerate(bits)) for m in range(1 << len(bits))]
    return [[i + s for s in spread] for i in others]


def summed(array):
    length = lax.axis_size(AXES)
    array = array + lax.ppermute(array, AXES, [(i, i ^ 1) for i in range(length)])
    for bits in ((1, 2, 3, 4), (5, 6, 7)):
        copies = jnp.broadcast_to(array[None], (1 << len(bits),) + array.shape)
        parts = lax.all_to_all(copies, AXES, 0, 0, axis_index_groups=groups_of(length, bits))
        array = jnp.sum(parts, axis=0)
    return array


def local(
    points,
    cell_counts,
    pair_cells,
    pair_counts,
    nugget,
    solution,
    residual,
    direction,
    ritz_basis,
    ritz_image,
    inverse_gram,
):
    off, acc_i, acc_j, back = pair_products(cell_counts, points, direction)
    image, sums = local_sums(
        cell_counts, off, acc_i, acc_j, back, nugget.reshape(1, -1), direction, residual, ritz_image
    )
    return tuple(
        finish(
            cell_counts,
            summed(sums),
            inverse_gram,
            image,
            direction,
            residual,
            solution,
            ritz_basis,
        )
    )


def solution(mesh):
    split = P(None, AXES)
    line = P(AXES)
    in_specs = (split, line, split, line, line, split, split, split, split, split, P())
    return jax.shard_map(
        local, mesh=mesh, in_specs=in_specs, out_specs=(split,) * 3, check_vma=False
    )
```

```python
import jax
import jax.numpy as jnp
from jax import lax
from jax.experimental import pallas as pl
from jax.experimental.pallas import tpu as pltpu
from jax.sharding import PartitionSpec as P

PTS = 256
REACH = 12
KF = 48
FAR = 1e18
ROOM = 16.0
AXES = ("region", "cell")
F32 = jnp.float32
BF16 = jnp.bfloat16


def mm(x, y):
    return lax.dot_general(x, y, (((1,), (0,)), ((), ())), preferred_element_type=F32)


def mm_t(x, y):
    return lax.dot_general(x, y, (((1,), (1,)), ((), ())), preferred_element_type=F32)


def high(x):
    return x.astype(BF16).astype(F32)


def split3(x):
    h = high(x)
    m = high(x - h)
    return h, m, x - h - m


def tile_of(scaled_square):
    s = jnp.maximum(scaled_square, 1e-30)
    t = s * lax.rsqrt(s)
    u = jnp.maximum(4.0 - t, 0.0)
    u2 = u * u
    return ((u2 * u2) * (t + 1.0)).astype(BF16)


def cols(block, size=PTS):
    return pl.ds(pl.multiple_of(block * size, size), size)


def with_norm(vec):
    row = lax.broadcasted_iota(jnp.int32, vec.shape, 0)
    return row, jnp.sum(vec * vec, axis=0, keepdims=True)


def weights_side(p):
    row, norm = with_norm(p)
    a = jnp.where(row == 3, norm, p)
    h, m, l = split3(a)
    one_h = jnp.where(row == 3, 1.0, h)
    one_m = jnp.where(row == 3, 1.0, m)
    return jnp.concatenate([h, m, one_h, one_m, l, one_h], axis=0).astype(BF16)


def rows_side(q):
    row, norm = with_norm(q)
    a = jnp.where(row == 3, norm, -2.0 * q)
    h, m, l = split3(a)
    one = jnp.where(row == 3, 1.0, h)
    mid_h = jnp.where(row == 3, h, m)
    return jnp.concatenate([one, one, mid_h, m, one, l], axis=0), norm


def pack(cells, cnt, off, dirs, pts, dc, pc):
    lane1 = lax.broadcasted_iota(jnp.int32, (1, PTS), 1)
    lane128 = lax.broadcasted_iota(jnp.int32, (1, 128), 1)

    def place(c, at):
        off[c] = at
        shift = at % 128
        base = pl.multiple_of((at // 128) * 128, 128)
        live = lane1 < cnt[c]
        dv = jnp.where(live, dirs[:, cols(c)], 0.0)
        pv = jnp.where(live, 4.0 * pts[:, cols(c)], 0.0)
        for ref, val in ((dc, dv), (pc, pv)):
            rows = val.shape[0]
            wide = jnp.concatenate([val, jnp.zeros((rows, 128), F32)], axis=1)
            wide = pltpu.roll(wide, shift, 1)
            old = ref[:rows, pl.ds(base, 128)]
            ref[:rows, pl.ds(base, 128)] = jnp.where(lane128 < shift, old, wide[:, :128])
            ref[:rows, pl.ds(base + 128, 256)] = wide[:, 128:]
        return at + cnt[c]

    return lax.fori_loop(0, cells, place, jnp.int32(0), unroll=8)


def prepare(blocks, pc, end, cen, fs):
    lane1 = lax.broadcasted_iota(jnp.int32, (1, PTS), 1)
    lane128 = lax.broadcasted_iota(jnp.int32, (1, 128), 1)

    def one(j, carry):
        low, top, far = carry
        here = pc[:, cols(j)]
        valid = j * PTS + lane1 < end
        lo = jnp.min(jnp.where(valid, here, FAR), axis=1, keepdims=True)
        hi = jnp.max(jnp.where(valid, here, -FAR), axis=1, keepdims=True)
        centre = jnp.where(lo <= hi, 0.5 * (lo + hi), 0.0)
        cen[pl.ds(pl.multiple_of(j * 8, 8), 8), :] = jnp.broadcast_to(centre, (8, 128))
        feats, norm = rows_side(here - centre)
        fs[cols(j), :] = feats.T.astype(BF16)
        low = jnp.where(lane128 == j, lo, low)
        top = jnp.where(lane128 == j, hi, top)
        return low, top, jnp.maximum(far, jnp.where(valid, norm, 0.0))

    start = (
        jnp.full((8, 128), FAR, F32),
        jnp.full((8, 128), -FAR, F32),
        jnp.zeros((1, PTS), F32),
    )
    low, top, far = lax.fori_loop(0, blocks, one, start, unroll=12 if blocks % 12 == 0 else 8)
    cen[pl.ds(blocks * 8, 8), :] = jnp.zeros((8, 128), F32)
    fs[pl.ds(blocks * PTS, PTS), :] = jnp.zeros((PTS, KF), BF16)
    wide = jnp.max(far, axis=1, keepdims=True) > 16.0 * ROOM
    return low, top, jnp.where(wide, 1, 0)


def square(v):
    return jnp.concatenate([v, jnp.zeros((120, 128), F32)], axis=0).T


def near(low_i, top_i, low_j, top_j):
    low_t, top_t = square(low_i), square(top_i)
    gap2 = jnp.zeros((128, 128), F32)
    for k in range(3):
        gap = jnp.maximum(
            low_j[k : k + 1] - top_t[:, k : k + 1], low_t[:, k : k + 1] - top_j[k : k + 1]
        )
        gap = jnp.maximum(gap, 0.0)
        gap2 = gap2 + gap * gap
    return gap2 <= 16.016


def as_rows(last):
    last = jnp.max(last.astype(F32), axis=1, keepdims=True)
    return jnp.broadcast_to(last, (128, 128)).T[:8].astype(jnp.int32)


def lanes_sum(values):
    return jnp.sum(values.astype(F32), axis=1, keepdims=True).astype(jnp.int32)


def to_scalars(values, tab_v, tab_s, sem):
    tab_v[...] = values
    copy = pltpu.make_async_copy(tab_v, tab_s, sem)
    copy.start()
    copy.wait()


def sweep(first, end, begin, stop, total, spare, spread, side_i, side_j, acc_i, acc_j, bufs):
    pc_i, db_i = side_i
    pc_j, db_j, fs_j, cen_j = side_j
    depth = len(bufs)
    def enter(i):
        i = jnp.where(i >= end, spare[0], i)
        return i, jnp.where(i == spare[0], spare[1], begin(i))

    def following(i, j):
        n = j + 1
        over = (n >= stop(i)) | (i == spare[0])
        i2, j2 = enter(i + 1)
        return jnp.where(over, i2, i), jnp.where(over, j2, n)

    def squares(i, j, out):
        c = cen_j[pl.ds(pl.multiple_of(j * 8, 8), 8), :]
        f = weights_side(pc_i[:, cols(i)] - jnp.concatenate([c, c], axis=1))
        out[...] = mm(fs_j[cols(j), :], f)

    same = db_i is db_j

    def products(i, j, tile):
        other = mm_t(db_i[:, cols(i)], tile)
        mine = mm(db_j[:, cols(j)], tile)
        return i, jnp.where(j > i, j, spare[1]) if same else j, mine, other

    def add(i, j, mine, other):
        acc_i[:, cols(i)] += mine
        acc_j[:, cols(j)] += other

    queue = [enter(first)]
    for _ in range(depth - 1):
        queue.append(following(*queue[-1]))

    @pl.when(spread == 0)
    def _():
        for k in range(depth - 1):
            squares(*queue[k], bufs[k])

        def turn(units):
            def one(_, carry):
                q = list(carry)
                waiting = None
                for g in range(units):
                    squares(*q[-1], bufs[(g + depth - 1) % depth])
                    done = products(*q[0], tile_of(bufs[g % depth][...]))
                    if waiting is not None:
                        add(*waiting)
                    waiting = done
                    q = q[1:] + [following(*q[-1])]
                add(*waiting)
                return tuple(q)

            return one

        state = lax.fori_loop(0, total // LONG, turn(LONG), tuple(queue))
        left = total - (total // LONG) * LONG
        lax.fori_loop(0, (left + depth - 1) // depth, turn(depth), state)

    @pl.when(spread != 0)
    def _():
        def one(_, carry):
            i, j = carry
            pj = pc_j[:, cols(j)].T
            pi = pc_i[:, cols(i)]
            for h in range(0, PTS, 64):
                s = jnp.zeros((64, PTS), F32)
                for k in range(3):
                    d = pj[h : h + 64, k : k + 1] - pi[k : k + 1, :]
                    s = s + d * d
                bufs[0][pl.ds(h, 64), :] = s
            add(*products(i, j, tile_of(bufs[0][...])))
            return following(i, j)

        lax.fori_loop(0, total, one, queue[0])


def fetch(pairs, sems):
    copies = [pltpu.make_async_copy(src, dst, sems.at[k]) for k, (src, dst) in enumerate(pairs)]
    for copy in copies:
        copy.start()
    return copies


def head_kernel(cells, cnt_h, pts_h, dirs_h, db, pc, fs, cen, box, tab, off, cnt, pts, dirs, dc, sem):
    copies = fetch(((cnt_h, cnt), (pts_h, pts), (dirs_h, dirs)), sem)
    dc[...] = jnp.zeros_like(dc)
    pc[...] = jnp.zeros_like(pc)
    for copy in copies:
        copy.wait()
    own_end = pack(cells, cnt, off, dirs, pts, dc, pc)
    db[...] = dc[...].astype(BF16)
    low, top, spread = prepare(cells, pc, own_end, cen, fs)
    box[0:8, :] = low
    box[8:16, :] = top
    ri = lax.broadcasted_iota(jnp.int32, (128, 128), 0)
    rj = lax.broadcasted_iota(jnp.int32, (128, 128), 1)
    need = near(low, top, low, top) & (rj > ri)
    stop = as_rows(jnp.where(need, rj + 1, ri + 1))
    lane128 = lax.broadcasted_iota(jnp.int32, (1, 128), 1)
    strips = (own_end + (PTS - 1)) // PTS
    total = lanes_sum(jnp.where(lane128 < strips, stop - lane128, 0))
    stop = jnp.where(lane128 == 125, strips, jnp.where(lane128 == 126, total, stop))
    tab[...] = jnp.where(lane128 == 127, spread, stop)


def edge_kernel(cells, halo_cells, db, pc, box, tab, piece, halo, acc_i, hdb, hfs, hcen, tab_v, *rest):
    *bufs, tab_s, sem = rest
    strips = tab[0, 125]
    acc_i[...] = jnp.zeros_like(acc_i)
    halo[...] = jnp.zeros_like(halo)
    rhs = hdb.shape[0]
    hdb[:, : halo_cells * PTS] = piece[:rhs, :].astype(BF16)
    hdb[:, halo_cells * PTS :] = jnp.zeros((rhs, PTS), BF16)
    hpc = piece.at[rhs : rhs + 8]
    low, top, spread = prepare(halo_cells, hpc, halo_cells * PTS, hcen, hfs)
    ri = lax.broadcasted_iota(jnp.int32, (128, 128), 0)
    rj = lax.broadcasted_iota(jnp.int32, (128, 128), 1)
    need = near(box[0:8, :], box[8:16, :], low, top) & (rj < halo_cells) & (ri < cells)
    stop = as_rows(jnp.where(need, rj + 1, 0))
    lane128 = lax.broadcasted_iota(jnp.int32, (1, 128), 1)
    first = jnp.min(jnp.where(need, ri, 127).astype(F32), axis=(0, 1), keepdims=True)
    first = jnp.minimum(first.astype(jnp.int32), strips)
    stop = jnp.maximum(stop, 1)
    total = lanes_sum(jnp.where((lane128 >= first) & (lane128 < strips), stop, 0))
    stop = jnp.where(lane128 == 125, total, jnp.where(lane128 == 126, first, stop))
    to_scalars(jnp.where(lane128 == 127, spread + tab[0, 127], stop), tab_v, tab_s, sem)
    sweep(
        tab_s[0, 126], strips, lambda i: jnp.int32(0), lambda i: tab_s[0, i], tab_s[0, 125],
        (cells, halo_cells), tab_s[0, 127],
        (pc, db), (hpc, hdb, hfs, hcen), acc_i, halo, bufs,
    )
    halo[:, : halo_cells * PTS] = halo[:, : halo_cells * PTS] * (1.0 / 256.0)


def tail_kernel(cells, db, pc, fs, cen, tab, acc_e, acc_i, acc_j, *bufs):
    acc_i[...] = acc_e[...]
    acc_j[...] = jnp.zeros_like(acc_j)
    side = (pc, db, fs, cen)
    sweep(
        jnp.int32(0), tab[0, 125], lambda i: i, lambda i: tab[0, i], tab[0, 126],
        (cells, cells), tab[0, 127],
        side[:2], side, acc_i, acc_j, bufs,
    )


def piece_kernel(cells, cnt_h, pts_h, dirs_h, piece, cnt, pts, dirs, sem):
    rhs = dirs.shape[0]
    span = pl.ds(0, cells * PTS)
    copies = fetch(((cnt_h, cnt), (pts_h.at[:, span], pts), (dirs_h.at[:, span], dirs)), sem)
    lane1 = lax.broadcasted_iota(jnp.int32, (1, PTS), 1)
    piece[rhs:, :] = jnp.zeros_like(piece[rhs:, :])
    for copy in copies:
        copy.wait()
    for c in range(cells):
        at = slice(c * PTS, (c + 1) * PTS)
        live = lane1 < cnt[c]
        piece[:rhs, at] = jnp.where(live, dirs[:, at], 0.0)
        here = jnp.where(live, pts[:, at], pts[:, c * PTS : c * PTS + 1])
        piece[rhs : rhs + 3, at] = 4.0 * here


VM = pl.BlockSpec(memory_space=pltpu.VMEM)
SM = pl.BlockSpec(memory_space=pltpu.SMEM)
HB = pl.BlockSpec(memory_space=pltpu.MemorySpace.HBM)
LONG = 24
DEPTH = 4


def params(mib):
    return pltpu.CompilerParams(vmem_limit_bytes=mib << 20)


def buffers():
    return [pltpu.VMEM((PTS, PTS), F32)] * DEPTH


def cost(units):
    return pl.CostEstimate(flops=units * 60_000_000, bytes_accessed=4_000_000, transcendentals=units * 65536)


def pair_products(counts, points, direction):
    cells = counts.shape[0]
    rhs = direction.shape[0]
    width = min(cells, REACH)
    blocks = cells + 1
    wide = blocks * PTS + 256
    shape = jax.ShapeDtypeStruct

    held = [pltpu.with_memory_space_constraint(x, pltpu.MemorySpace.HBM) for x in (counts, points, direction)]
    piece = pl.pallas_call(
        lambda *refs: piece_kernel(width, *refs),
        name="piece",
        out_shape=shape((rhs + 8, width * PTS), F32),
        in_specs=[HB] * 3,
        out_specs=VM,
        scratch_shapes=[
            pltpu.SMEM((cells,), jnp.int32),
            pltpu.VMEM((3, width * PTS), F32),
            pltpu.VMEM((rhs, width * PTS), F32),
            pltpu.SemaphoreType.DMA((3,)),
        ],
        compiler_params=params(8),
    )(*held)
    piece = passed_along(piece, -1)
    db, pc, fs, cen, box, tab, off = pl.pallas_call(
        lambda *refs: head_kernel(cells, *refs),
        name="head",
        out_shape=[
            shape((rhs, wide), BF16),
            shape((8, wide), F32),
            shape((blocks * PTS, KF), BF16),
            shape((blocks * 8, 128), F32),
            shape((16, 128), F32),
            shape((8, 128), jnp.int32),
            shape((cells,), jnp.int32),
        ],
        in_specs=[HB] * 3,
        out_specs=[VM] * 6 + [SM],
        scratch_shapes=[
            pltpu.SMEM((cells,), jnp.int32),
            pltpu.VMEM(points.shape, F32),
            pltpu.VMEM(direction.shape, F32),
            pltpu.VMEM((rhs, wide), F32),
            pltpu.SemaphoreType.DMA((3,)),
        ],
        compiler_params=params(12),
        cost_estimate=cost(100),
    )(*held)
    halo, acc_e = pl.pallas_call(
        lambda *refs: edge_kernel(cells, width, *refs),
        name="edge",
        out_shape=[shape((rhs, (width + 1) * PTS), F32), shape((rhs, wide), F32)],
        in_specs=[VM] * 3 + [SM, VM],
        out_specs=[VM] * 2,
        scratch_shapes=[
            pltpu.VMEM((rhs, (width + 1) * PTS), BF16),
            pltpu.VMEM(((width + 1) * PTS, KF), BF16),
            pltpu.VMEM(((width + 1) * 8, 128), F32),
            pltpu.VMEM((8, 128), jnp.int32),
        ]
        + buffers()
        + [pltpu.SMEM((8, 128), jnp.int32), pltpu.SemaphoreType.DMA],
        compiler_params=params(12),
        cost_estimate=cost(70),
    )(db, pc, box, tab, piece)
    back = passed_along(halo, 1)
    acc_i, acc_j = pl.pallas_call(
        lambda *refs: tail_kernel(cells, *refs),
        name="tail",
        out_shape=[shape((rhs, wide), F32)] * 2,
        in_specs=[VM] * 4 + [SM, VM],
        out_specs=[VM] * 2,
        scratch_shapes=buffers(),
        compiler_params=params(12),
        cost_estimate=cost(180),
    )(db, pc, fs, cen, tab, acc_e)
    return off, acc_i, acc_j, back


def sums_kernel(cnt, off, acc_i, acc_j, back, nug, dirs, res, ritz, image, sums):
    cells = image.shape[1] // PTS
    halo_cells = back.shape[1] // PTS - 1
    lane1 = lax.broadcasted_iota(jnp.int32, (1, PTS), 1)

    def of_cell(c, part, extra):
        live = lane1 < cnt[c]
        d = jnp.where(live, dirs[:, cols(c)], 0.0)
        r = jnp.where(live, res[:, cols(c)], 0.0)
        at = off[c]
        base = pl.multiple_of((at // 128) * 128, 128)
        k = acc_i[:, pl.ds(base, 384)] + acc_j[:, pl.ds(base, 384)]
        k = pltpu.roll(k, 384 - at % 128, 1)[:, :PTS] * (1.0 / 256.0)
        if extra:
            k = k + back[:, cols(c)]
        im = jnp.where(live, nug[:, cols(c)] * d + k, 0.0)
        image[:, cols(c)] = im
        dk, rr, ri, ii, prod = part
        both = jnp.concatenate([r, im], axis=0)
        bh = high(both)
        z = ritz[:, cols(c)]
        zh = high(z)
        left = jnp.concatenate([bh, both - bh], axis=0).astype(BF16)
        right = jnp.concatenate([zh, z - zh], axis=0).astype(BF16)
        return dk + d * im, rr + r * r, ri + r * im, ii + im * im, prod + mm_t(left, right)

    rhs = image.shape[0]
    zero = jnp.zeros((rhs, PTS), F32)
    part = (zero, zero, zero, zero, jnp.zeros((4 * rhs, 2 * ritz.shape[0]), F32))
    part = lax.fori_loop(0, halo_cells, lambda c, p: of_cell(c, p, True), part, unroll=12)
    part = lax.fori_loop(halo_cells, cells, lambda c, p: of_cell(c, p, False), part, unroll=20)
    dots = [jnp.sum(p, axis=1, keepdims=True) for p in part[:4]]
    prod = part[4]
    n = ritz.shape[0]
    h = 2 * rhs
    prod = prod[:h, :n] + prod[:h, n:] + prod[h:, :n]
    half = rhs // 2
    both = jnp.concatenate([prod[:rhs], prod[rhs:]], axis=1)
    both = jnp.concatenate([both[:half], both[half:]], axis=1)
    for k in range(half):
        sums[k] = both[k : k + 1]
    lane = lax.broadcasted_iota(jnp.int32, (rhs, 128), 1)
    table = jnp.zeros((rhs, 128), F32)
    for k in range(4):
        table = jnp.where(lane == k, dots[k], table)
    table = jnp.concatenate([table, jnp.zeros((128 - rhs, 128), F32)], axis=0).T
    line = jnp.zeros((1, 128), F32)
    lane = lane[:1]
    for k in range(4):
        row = table[k : k + 1]
        row = row if k == 0 else pltpu.roll(row, k * rhs, 1)
        line = jnp.where((lane >= k * rhs) & (lane < (k + 1) * rhs), row, line)
    sums[half] = line


def local_sums(counts, off, acc_i, acc_j, back, nugget, direction, residual, ritz_image):
    return pl.pallas_call(
        sums_kernel,
        name="sums",
        out_shape=[
            jax.ShapeDtypeStruct(direction.shape, F32),
            jax.ShapeDtypeStruct((9, 1, 128), F32),
        ],
        in_specs=[SM, SM] + [VM] * 7,
        out_specs=[VM, VM],
        compiler_params=params(12),
    )(counts, off, acc_i, acc_j, back, nugget, direction, residual, ritz_image)


def finish_kernel(
    cnt, sums, gram, image, dirs, res, sol, basis, sol_h, res_h, dir_h, sol_out, res_out, dir_out, sem
):
    cells = image.shape[1] // PTS
    n = gram.shape[0]
    lane1 = lax.broadcasted_iota(jnp.int32, (1, PTS), 1)
    rhs = image.shape[0]
    half = rhs // 2
    both = jnp.concatenate([sums[k] for k in range(half)], axis=0)
    both = jnp.concatenate([both[:, : 2 * n], both[:, 2 * n :]], axis=0)
    line = sums[half]
    table = [line if k == 0 else pltpu.roll(line, 128 - k * rhs, 1) for k in range(4)]
    table = jnp.concatenate(table + [jnp.zeros((124, 128), F32)], axis=0).T
    curvature, rr, ri, ii = (table[:rhs, k : k + 1] for k in range(4))
    step = rr / curvature
    growth = (rr + step * (step * ii - 2.0 * ri)) / rr
    projected = both[:, :n] - step * both[:, n:]
    ph = high(projected)
    g = gram[...]
    gh = high(g)
    coef = mm_t(
        jnp.concatenate([ph, ph, projected - ph], axis=1).astype(BF16),
        jnp.concatenate([gh, g - gh, gh], axis=1).astype(BF16),
    )
    ch = high(coef)
    left = jnp.concatenate([ch, ch, coef - ch], axis=1).astype(BF16)

    def of_cell(c, _):
        live = lane1 < cnt[c]
        d = jnp.where(live, dirs[:, cols(c)], 0.0)
        r = jnp.where(live, res[:, cols(c)], 0.0)
        s = jnp.where(live, sol[:, cols(c)], 0.0)
        b = basis[:, cols(c)]
        bh = high(b)
        right = jnp.concatenate([bh, b - bh, bh], axis=0).astype(BF16)
        new = r - step * image[:, cols(c)]
        sol_out[:, cols(c)] = s + step * d
        res_out[:, cols(c)] = new
        dir_out[:, cols(c)] = jnp.where(live, growth * d + new - mm(left, right), 0.0)
        return 0

    pieces = 4
    many = cells // pieces
    copies = []
    for k in range(pieces):
        lax.fori_loop(k * many, (k + 1) * many, of_cell, 0, unroll=8)
        at = pl.ds(k * many * PTS, many * PTS)
        for n, (src, dst) in enumerate(((sol_out, sol_h), (res_out, res_h), (dir_out, dir_h))):
            copies.append(pltpu.make_async_copy(src.at[:, at], dst.at[:, at], sem.at[3 * k + n]))
            copies[-1].start()
    for copy in copies:
        copy.wait()


def finish(counts, sums, gram, image, direction, residual, solution, basis):
    return pl.pallas_call(
        finish_kernel,
        name="finish",
        out_shape=[jax.ShapeDtypeStruct(image.shape, F32)] * 3,
        in_specs=[SM] + [VM] * 7,
        out_specs=[HB] * 3,
        scratch_shapes=[pltpu.VMEM(image.shape, F32)] * 3 + [pltpu.SemaphoreType.DMA((12,))],
        compiler_params=params(12),
    )(counts, sums, gram, image, direction, residual, solution, basis)


def passed_along(array, by):
    length = lax.axis_size(AXES)
    pairs = [(i, i + by) for i in range(length) if 0 <= i + by < length]
    return lax.ppermute(array, AXES, pairs)


def groups_of(length, bits):
    others = [i for i in range(length) if not any(i >> b & 1 for b in bits)]
    spread = [sum((m >> k & 1) << b for k, b in enumerate(bits)) for m in range(1 << len(bits))]
    return [[i + s for s in spread] for i in others]


def summed(array):
    length = lax.axis_size(AXES)
    array = array + lax.ppermute(array, AXES, [(i, i ^ 1) for i in range(length)])
    for bits in ((5, 6, 7), (1, 2, 3, 4)):
        copies = jnp.broadcast_to(array[None], (1 << len(bits),) + array.shape)
        parts = lax.all_to_all(copies, AXES, 0, 0, axis_index_groups=groups_of(length, bits))
        array = jnp.sum(parts, axis=0)
    return array


def local(
    points,
    cell_counts,
    pair_cells,
    pair_counts,
    nugget,
    solution,
    residual,
    direction,
    ritz_basis,
    ritz_image,
    inverse_gram,
):
    off, acc_i, acc_j, back = pair_products(cell_counts, points, direction)
    image, sums = local_sums(
        cell_counts, off, acc_i, acc_j, back, nugget.reshape(1, -1), direction, residual, ritz_image
    )
    return tuple(
        finish(
            cell_counts,
            summed(sums),
            inverse_gram,
            image,
            direction,
            residual,
            solution,
            ritz_basis,
        )
    )


def solution(mesh):
    split = P(None, AXES)
    line = P(AXES)
    in_specs = (split, line, split, line, line, split, split, split, split, split, P())
    return jax.shard_map(
        local, mesh=mesh, in_specs=in_specs, out_specs=(split,) * 3, check_vma=False
    )
```
